32 devices in a mesh: dp: 2 (over x), row: 4 (over y, core), col: 4 (over z).
Axes of the slice: x: 2, y: 2, z: 4, core: 2. Of those that a mesh axis runs over, the one named last changes fastest.
Arguments:
- block_in: bfloat16 [2048, 2048], P(('dp', 'col'), 'row'), may hold values from -6 to 6
- norm1_gain: float32 [2048], P('row'), may hold values from 0.5 to 1.5
- norm1_bias: float32 [2048], P('row'), may hold values from -3 to 3
- w_qkv: bfloat16 [2048, 3, 2048], P('row', None, 'col'), may hold values from -0.125 to 0.125
- qkv_bias: float32 [3, 2048], P(None, 'col'), may hold values from -3 to 3
- w_proj: bfloat16 [2048, 2048], P('col', 'row'), may hold values from -1.5 to 1.5
- norm2_gain: float32 [2048], P('row'), may hold values from 0.25 to 1.75
- norm2_bias: float32 [2048], P('row'), may hold values from -3 to 3
- w_gateup: bfloat16 [2048, 2, 5632], P('row', None, 'col'), may hold values from -0.125 to 0.125
- w_down: bfloat16 [5632, 2048], P('col', 'row'), may hold values from -0.078125 to 0.078125
- out_grad: bfloat16 [2048, 2048], P(('dp', 'col'), 'row'), may hold values from -6 to 6
Outputs:
- block_out: float32 [2048, 2048], P(('dp', 'col'), 'row')
- grad_in: float32 [2048, 2048], P(('dp', 'col'), 'row')
- grad_qkv: float32 [2048, 3, 2048], P('row', None, 'col')
- grad_bias: float32 [3, 2048], P(None, 'col')
- grad_proj: float32 [2048, 2048], P('col', 'row')
- gain1_grad: float32 [2048], P('row')
- bias1_grad: float32 [2048], P('row')
- gain2_grad: float32 [2048], P('row')
- bias2_grad: float32 [2048], P('row')
- grad_gateup: float32 [2048, 2, 5632], P('row', None, 'col')
- grad_down: float32 [5632, 2048], P('col', 'row')
The draws below stay inside these ranges and needn't reach their ends.
All inputs are finite; a program needn't handle non-finite values.
Results may differ from the reference program's by a relative error of at most 0.012.
Values may be sent and summed in bfloat16 or wider, within the bound.
No kernel may reach another device: no remote copies, remote signals or barrier semaphores. Data moves between devices by JAX's collectives and lax.ppermute only.
A program may use at most 128 MiB of HBM per device.

```python
import math
import jax
import jax.numpy as jnp
from jax import lax

D = 2048
HEADS = 32
HD = 64
ROT = 16
FF = 5632
SEQ = 256
TOK_GRP = 1024
TOKENS = 2048
N_DP = 2
N_ROW = 4


def block_levels(stream_key, dims, shards, least, largest):
    def one(axis_at, blocks):
        draws = jax.random.uniform(jax.random.fold_in(jax.random.fold_in(stream_key, 6), axis_at), (blocks,), jnp.float32, least / len(shards), largest / len(shards))
        return jnp.repeat(jnp.exp(draws), dims[axis_at] // blocks).reshape((-1,) + (1,) * (len(dims) - axis_at - 1))

    loudness = one(*shards[0])
    for cut in shards[1:]:
        loudness = loudness * one(*cut)
    return loudness


def gaussian(stream_key, extent, deviation, most, shards=(), kind=jnp.bfloat16):
    array = jax.random.normal(stream_key, extent, jnp.float32) * deviation
    if len(shards) > 0:
        array = block_levels(stream_key, extent, shards, -0.22, 0.18) * array
    return jnp.clip(array, min=-most, max=most).astype(kind)


def setup_inputs(seed: int = 0) -> dict:
    streams_of = jax.random.split(jax.random.key(seed), 12)
    return {
        "block_in": gaussian(streams_of[0], (TOKENS, D), 1.0, 6.0, ((0, 8), (1, 4))),
        "norm1_gain": jnp.clip(1.0 + 0.1 * jax.random.normal(streams_of[1], (D,), jnp.float32), 0.5, 1.5),
        "norm1_bias": gaussian(streams_of[2], (D,), 0.5, 3.0, ((0, 4),), jnp.float32),
        "w_qkv": gaussian(streams_of[3], (D, 3, D), D ** -0.5, 0.125, ((0, 4), (2, 4))),
        "qkv_bias": gaussian(streams_of[4], (3, D), 0.5, 3.0, ((1, 4),), jnp.float32),
        "w_proj": gaussian(streams_of[5], (D, D), (2 * D // SEQ) ** -0.5, 1.5, ((0, 4), (1, 4))),
        "norm2_gain": jnp.clip(1.0 + 0.15 * jax.random.normal(streams_of[6], (D,), jnp.float32), 0.25, 1.75),
        "norm2_bias": gaussian(streams_of[7], (D,), 0.5, 3.0, ((0, 4),), jnp.float32),
        "w_gateup": gaussian(streams_of[8], (D, 2, FF), D ** -0.5, 0.125, ((0, 4), (2, 4))),
        "w_down": gaussian(streams_of[9], (FF, D), FF ** -0.5, 0.078125, ((0, 4), (1, 4))),
        "out_grad": gaussian(streams_of[10], (TOKENS, D), 1.0, 6.0, ((0, 8), (1, 4))),
    }


EPS = 1e-05
THETA = 10000.0

def to_half(values):
    return lax.optimization_barrier(values.astype(jnp.bfloat16))

def blocked(left, right):
    return jnp.dot(left, right, preferred_element_type=jnp.float32)

def norm_forward(values, gain, shift):
    mean = lax.optimization_barrier(jnp.mean(values, -1, keepdims=True))
    second = lax.optimization_barrier(jnp.mean(values * values, -1, keepdims=True))
    inverse = lax.rsqrt(second - mean * mean + EPS)
    centred = (values - mean) * inverse
    return (centred, inverse, to_half(centred * gain + shift))

def norm_backward(grad_normed, centred, inverse, gain):
    scaled = grad_normed * gain
    return inverse * (scaled - lax.optimization_barrier(jnp.mean(scaled, -1, keepdims=True)) - centred * lax.optimization_barrier(jnp.mean(scaled * centred, -1, keepdims=True)))

def tables(length):
    half = ROT // 2
    freqs = THETA ** (-2.0 * jnp.arange(half, dtype=jnp.float32) / ROT)
    angles = jnp.arange(length, dtype=jnp.float32)[:, None] * freqs[None, :]
    return (jnp.cos(angles)[:, None, :], jnp.sin(angles)[:, None, :])

def rotate(vec, cos_t, sin_t):
    half = ROT // 2
    first = vec[..., :half]
    second = vec[..., half:ROT]
    return jnp.concatenate([first * cos_t - second * sin_t, second * cos_t + first * sin_t, vec[..., ROT:]], -1)

def bias_mask(width):
    lanes = jnp.arange(width) % HD < ROT
    ones = jnp.ones((width,), jnp.float32)
    return jnp.stack([ones, jnp.where(lanes, 1.0, 0.0).astype(jnp.float32), ones])

def masked_scores(query_blk, keys_f, start, length):
    block = query_blk.shape[0]
    scores = jnp.einsum('qhd,khd->hqk', query_blk.astype(jnp.float32), keys_f) * (1.0 / math.sqrt(HD))
    allowed = (start + jnp.arange(block))[:, None] >= jnp.arange(length)[None, :]
    return jnp.where(allowed[None], scores, -1e+30)

def attend(query, keys, values):
    length = query.shape[0]
    block = min(512, length)
    keys_f = keys.astype(jnp.float32)
    values_f = values.astype(jnp.float32)
    outs = []
    sums = []
    for start in range(0, length, block):
        scores = masked_scores(query[start:start + block], keys_f, start, length)
        top = lax.optimization_barrier(jnp.max(scores, -1, keepdims=True))
        lse = top + jnp.log(lax.optimization_barrier(jnp.sum(jnp.exp(scores - top), -1, keepdims=True)))
        probs = to_half(jnp.exp(scores - lse)).astype(jnp.float32)
        outs.append(to_half(jnp.einsum('hqk,khd->qhd', probs, values_f)))
        sums.append(lse[..., 0])
    return (jnp.concatenate(outs, 0), jnp.concatenate(sums, 1))

def attend_back(query, keys, values, output, lse, grad_out):
    length = query.shape[0]
    block = min(512, length)
    scale = 1.0 / math.sqrt(HD)
    keys_f = keys.astype(jnp.float32)
    values_f = values.astype(jnp.float32)
    grad_f = grad_out.astype(jnp.float32)
    delta = lax.optimization_barrier(jnp.sum(grad_f * output.astype(jnp.float32), -1))
    grad_keys = jnp.zeros(keys.shape, jnp.float32)
    grad_values = jnp.zeros(values.shape, jnp.float32)
    grad_query = []
    for start in range(0, length, block):
        query_f = query[start:start + block].astype(jnp.float32)
        grad_blk = grad_f[start:start + block]
        scores = masked_scores(query[start:start + block], keys_f, start, length)
        weights = jnp.exp(scores - lse[:, start:start + block, None])
        dprobs = jnp.einsum('qhd,khd->hqk', grad_blk, values_f)
        dscores = to_half(weights * (dprobs - delta[start:start + block].T[:, :, None])).astype(jnp.float32)
        grad_query.append(jnp.einsum('hqk,khd->qhd', dscores, keys_f) * scale)
        grad_keys = grad_keys + jnp.einsum('hqk,qhd->khd', dscores, query_f) * scale
        probs = to_half(weights).astype(jnp.float32)
        grad_values = grad_values + jnp.einsum('hqk,qhd->khd', probs, grad_blk)
    return (jnp.concatenate(grad_query, 0), grad_keys, grad_values)

def reference(block_in, norm1_gain, norm1_bias, w_qkv, qkv_bias, w_proj, norm2_gain, norm2_bias, w_gateup, w_down, out_grad):
    qkv_flat = w_qkv.reshape(D, 3 * D)
    inner_flat = w_gateup.reshape(D, 2 * FF)
    cos_t, sin_t = tables(SEQ)

    def group_pass(carry, inputs):
        tokens_in, tokens_grad = inputs
        inputs_f = tokens_in.astype(jnp.float32)
        centred1, inverse1, normed1 = norm_forward(inputs_f, norm1_gain, norm1_bias)
        qkv = blocked(normed1, qkv_flat) + qkv_bias.reshape(3 * D)
        parts = qkv.reshape(N_ROW, SEQ, 3, HEADS, HD)
        query = to_half(rotate(parts[:, :, 0], cos_t, sin_t))
        keys = to_half(rotate(parts[:, :, 1], cos_t, sin_t))
        values = to_half(parts[:, :, 2])
        attn, lse = lax.map(lambda item: attend(item[0], item[1], item[2]), (query, keys, values))
        attn_flat = attn.reshape(TOK_GRP, D)
        resid = inputs_f + jnp.dot(attn_flat, w_proj, preferred_element_type=jnp.float32)
        centred2, inverse2, normed2 = norm_forward(resid, norm2_gain, norm2_bias)
        inner = blocked(normed2, inner_flat)
        gate = inner[:, :FF]
        up = inner[:, FF:]
        hidden = to_half(jax.nn.silu(gate) * up)
        block_out = resid + jnp.dot(hidden, w_down, preferred_element_type=jnp.float32)
        d_hidden = blocked(tokens_grad, w_down.T)
        sig = jax.nn.sigmoid(gate)
        d_inner = to_half(jnp.concatenate([d_hidden * up * sig * (1.0 + gate * (1.0 - sig)), d_hidden * gate * sig], 1))
        part_gateup = jnp.dot(normed2.T, d_inner, preferred_element_type=jnp.float32)
        part_down = jnp.dot(hidden.T, tokens_grad, preferred_element_type=jnp.float32)
        d_normed2 = jnp.dot(d_inner, inner_flat.T, preferred_element_type=jnp.float32)
        part_gain2 = lax.optimization_barrier(jnp.sum(d_normed2 * centred2, 0))
        part_bias2 = lax.optimization_barrier(jnp.sum(d_normed2, 0))
        d_resid = tokens_grad.astype(jnp.float32) + norm_backward(d_normed2, centred2, inverse2, norm2_gain)
        d_rounded = to_half(d_resid)
        d_attn = to_half(blocked(d_rounded, w_proj.T))
        part_proj = jnp.dot(attn_flat.T, d_rounded, preferred_element_type=jnp.float32)
        grads = lax.map(lambda item: attend_back(item[0], item[1], item[2], item[3], item[4], item[5]), (query, keys, values, attn, lse, d_attn.reshape(N_ROW, SEQ, HEADS, HD)))
        d_query = rotate(grads[0], cos_t, -sin_t)
        d_keys = rotate(grads[1], cos_t, -sin_t)
        d_qkv = to_half(jnp.stack([d_query, d_keys, grads[2]], 2).reshape(TOK_GRP, 3 * D))
        part_qkv = jnp.dot(normed1.T, d_qkv, preferred_element_type=jnp.float32)
        part_bias = lax.optimization_barrier(jnp.sum(d_qkv.astype(jnp.float32), 0))
        d_normed1 = jnp.dot(d_qkv, qkv_flat.T, preferred_element_type=jnp.float32)
        part_gain1 = lax.optimization_barrier(jnp.sum(d_normed1 * centred1, 0))
        part_bias1 = lax.optimization_barrier(jnp.sum(d_normed1, 0))
        grad_in = d_resid + norm_backward(d_normed1, centred1, inverse1, norm1_gain)
        terms = (part_qkv, part_bias, part_proj, part_gain1, part_bias1, part_gain2, part_bias2, part_gateup, part_down)
        return (tuple((a + b for a, b in zip(carry, terms))), (block_out, grad_in))
    start_carry = (jnp.zeros((D, 3 * D), jnp.float32), jnp.zeros((3 * D,), jnp.float32), jnp.zeros((D, D), jnp.float32), jnp.zeros((D,), jnp.float32), jnp.zeros((D,), jnp.float32), jnp.zeros((D,), jnp.float32), jnp.zeros((D,), jnp.float32), jnp.zeros((D, 2 * FF), jnp.float32), jnp.zeros((FF, D), jnp.float32))
    carry, results = lax.scan(group_pass, start_carry, (block_in.reshape(N_DP, TOK_GRP, D), out_grad.reshape(N_DP, TOK_GRP, D)))
    block_out = results[0].reshape(TOKENS, D)
    grad_in = results[1].reshape(TOKENS, D)
    grad_bias = carry[1].reshape(3, D) * bias_mask(D)
    return (block_out, grad_in, carry[0].reshape(D, 3, D), grad_bias, carry[2], carry[3], carry[4], carry[5], carry[6], carry[7].reshape(D, 2, FF), carry[8])
```

```python
import math

import jax
import jax.numpy as jnp
from jax import lax
from jax.sharding import PartitionSpec as P

D = 2048
HD = 64
ROT = 16
SEQ = 256


EPS = 1e-05
THETA = 10000.0


def shortened(value):

    def short(part):
        return part.astype(jnp.bfloat16) if part.dtype == jnp.float32 else part

    return jax.tree.map(short, value)


def row_stats(first, second):
    return lax.psum((first, second), "row")


def spread_rows(local):
    return lax.all_gather(local, "col", axis=0, tiled=True)


def gather_tokens(local):
    return lax.all_gather(shortened(local), "row", axis=0, tiled=True).astype(local.dtype)


def row_reduce(left, right):
    rows = left.shape[0] // lax.axis_size("row")
    piece = lax.dynamic_slice_in_dim(left, jnp.int32(0), rows * lax.axis_size("row"), 0)
    return lax.psum_scatter(
        jnp.dot(piece, right, preferred_element_type=jnp.float32).astype(jnp.bfloat16),
        "row",
        scatter_dimension=0,
        tiled=True,
    ).astype(jnp.float32)


def col_reduce(left, right):
    rows = left.shape[0] // lax.axis_size("col")
    piece = lax.dynamic_slice_in_dim(left, jnp.int32(0), rows * lax.axis_size("col"), 0)
    return lax.psum_scatter(
        jnp.dot(piece, right, preferred_element_type=jnp.float32).astype(jnp.bfloat16),
        "col",
        scatter_dimension=0,
        tiled=True,
    ).astype(jnp.float32)


def over_groups(partial):
    if lax.axis_size("dp") != 2:
        return lax.psum(partial, "dp")
    mine = partial.astype(jnp.bfloat16)
    other = lax.ppermute(mine, "dp", [(0, 1), (1, 0)])
    return mine.astype(jnp.float32) + other.astype(jnp.float32)


def norm_forward(values, gain, shift):
    total, squares = row_stats(jnp.sum(values, 1), jnp.sum(values * values, 1))
    mean = (total / D)[:, None]
    inverse = lax.rsqrt(squares[:, None] / D - mean * mean + EPS)
    centred = (values - mean) * inverse
    return (centred, inverse, (centred * gain + shift).astype(jnp.bfloat16))


def norm_backward(grad_normed, centred, inverse, gain):
    scaled = grad_normed * gain
    total, cross = row_stats(jnp.sum(scaled, 1), jnp.sum(scaled * centred, 1))
    return inverse * (scaled - total[:, None] / D - centred * cross[:, None] / D)


def tables(length):
    half = ROT // 2
    freqs = THETA ** (-2.0 * jnp.arange(half, dtype=jnp.float32) / ROT)
    angles = jnp.arange(length, dtype=jnp.float32)[:, None] * freqs[None, :]
    return (jnp.cos(angles)[:, None, :], jnp.sin(angles)[:, None, :])


def rotate(vec, cos_t, sin_t):
    half = ROT // 2
    first = vec[..., :half]
    second = vec[..., half:ROT]
    return jnp.concatenate(
        [first * cos_t - second * sin_t, second * cos_t + first * sin_t, vec[..., ROT:]], -1
    )


def bias_mask(width):
    lanes = jnp.arange(width) % HD < ROT
    ones = jnp.ones((width,), jnp.float32)
    return jnp.stack([ones, jnp.where(lanes, 1.0, 0.0).astype(jnp.float32), ones])


def masked_scores(query_blk, keys, length):
    block = query_blk.shape[0]
    scores = jnp.einsum("qhd,khd->hqk", query_blk, keys, preferred_element_type=jnp.float32) * (
        1.0 / math.sqrt(HD)
    )
    allowed = jnp.arange(block)[:, None] >= jnp.arange(length)[None, :]
    return jnp.where(allowed[None], scores, -1e30)


def attend(query, keys, values):
    length = query.shape[0]
    scores = masked_scores(query, keys, length)
    top = jnp.max(scores, -1, keepdims=True)
    lse = top + jnp.log(jnp.sum(jnp.exp(scores - top), -1, keepdims=True))
    probs = jnp.exp(scores - lse).astype(jnp.bfloat16)
    outs = [
        jnp.einsum("hqk,khd->qhd", probs, values, preferred_element_type=jnp.float32).astype(
            jnp.bfloat16
        )
    ]
    sums = [lse[..., 0]]
    return (jnp.concatenate(outs, 0), jnp.concatenate(sums, 1))


def attend_back(query, keys, values, output, lse, grad_out):
    length = query.shape[0]
    block = min(512, length)
    scale = 1.0 / math.sqrt(HD)
    delta = jnp.sum(grad_out.astype(jnp.float32) * output.astype(jnp.float32), -1)
    grad_keys = jnp.zeros(keys.shape, jnp.float32)
    grad_values = jnp.zeros(values.shape, jnp.float32)
    grad_blk = grad_out[0:block]
    scores = masked_scores(query, keys, length)
    weights = jnp.exp(scores - lse[:, 0:block, None])
    dprobs = jnp.einsum("qhd,khd->hqk", grad_blk, values, preferred_element_type=jnp.float32)
    dscores = (weights * (dprobs - delta[0:block].T[:, :, None])).astype(jnp.bfloat16)
    grad_query = [
        jnp.einsum("hqk,khd->qhd", dscores, keys, preferred_element_type=jnp.float32) * scale
    ]
    grad_keys = (
        grad_keys
        + jnp.einsum("hqk,qhd->khd", dscores, query, preferred_element_type=jnp.float32) * scale
    )
    grad_values = grad_values + jnp.einsum(
        "hqk,qhd->khd", weights.astype(jnp.bfloat16), grad_blk, preferred_element_type=jnp.float32
    )
    return (jnp.concatenate(grad_query, 0), grad_keys, grad_values)


def body(
    block_in,
    norm1_gain,
    norm1_bias,
    w_qkv,
    qkv_bias,
    w_proj,
    norm2_gain,
    norm2_bias,
    w_gateup,
    w_down,
    out_grad,
):
    feat_rows = w_qkv.shape[0]
    head_cols = w_qkv.shape[2]
    heads_here = head_cols // HD
    hidden_cols = w_gateup.shape[2]
    qkv_flat = w_qkv.reshape(feat_rows, 3 * head_cols)
    inner_flat = w_gateup.reshape(feat_rows, 2 * hidden_cols)
    cos_t, sin_t = tables(SEQ)
    inputs_f = block_in.astype(jnp.float32)
    centred1, inverse1, normed1 = norm_forward(inputs_f, norm1_gain, norm1_bias)
    group1 = spread_rows(normed1)
    qkv = row_reduce(group1, qkv_flat) + qkv_bias.reshape(3 * head_cols)
    local_rows = qkv.shape[0]
    seqs_here = local_rows // SEQ
    parts = qkv.reshape(seqs_here, SEQ, 3, heads_here, HD)
    query = rotate(parts[:, :, 0], cos_t, sin_t).astype(jnp.bfloat16)
    keys = rotate(parts[:, :, 1], cos_t, sin_t).astype(jnp.bfloat16)
    values = parts[:, :, 2].astype(jnp.bfloat16)
    attn, lse = lax.map(lambda item: attend(item[0], item[1], item[2]), (query, keys, values))
    attn_group = gather_tokens(attn.reshape(local_rows, head_cols))
    resid = inputs_f + col_reduce(attn_group, w_proj)
    centred2, inverse2, normed2 = norm_forward(resid, norm2_gain, norm2_bias)
    group2 = spread_rows(normed2)
    inner = row_reduce(group2, inner_flat)
    hidden_group = gather_tokens(
        (jax.nn.silu(inner[:, :hidden_cols]) * inner[:, hidden_cols:]).astype(jnp.bfloat16)
    )
    gate = inner[:, :hidden_cols]
    up = inner[:, hidden_cols:]
    block_out = resid + col_reduce(hidden_group, w_down)
    grad_group = spread_rows(out_grad)
    d_hidden = row_reduce(grad_group, w_down.T)
    grad_down = jnp.dot(hidden_group.T, grad_group, preferred_element_type=jnp.float32)
    sig = jax.nn.sigmoid(gate)
    d_inner = jnp.concatenate(
        [d_hidden * up * sig * (1.0 + gate * (1.0 - sig)), d_hidden * gate * sig], 1
    ).astype(jnp.bfloat16)
    inner_group = gather_tokens(d_inner)
    grad_gateup = jnp.dot(group2.T, inner_group, preferred_element_type=jnp.float32).reshape(
        feat_rows, 2, hidden_cols
    )
    d_normed2 = col_reduce(inner_group, inner_flat.T)
    gain2_part = jnp.sum(d_normed2 * centred2, 0)
    bias2_part = jnp.sum(d_normed2, 0)
    d_resid = out_grad.astype(jnp.float32) + norm_backward(
        d_normed2, centred2, inverse2, norm2_gain
    )
    resid_group = spread_rows(d_resid.astype(jnp.bfloat16))
    d_attn = row_reduce(resid_group, w_proj.T).astype(jnp.bfloat16)
    grad_proj = jnp.dot(attn_group.T, resid_group, preferred_element_type=jnp.float32)
    grads = lax.map(
        lambda item: attend_back(item[0], item[1], item[2], item[3], item[4], item[5]),
        (query, keys, values, attn, lse, d_attn.reshape(seqs_here, SEQ, heads_here, HD)),
    )
    d_query = rotate(grads[0], cos_t, -sin_t)
    d_keys = rotate(grads[1], cos_t, -sin_t)
    d_qkv = (
        jnp.stack([d_query, d_keys, grads[2]], 2)
        .reshape(local_rows, 3 * head_cols)
        .astype(jnp.bfloat16)
    )
    qkv_group = gather_tokens(d_qkv)
    grad_qkv = jnp.dot(group1.T, qkv_group, preferred_element_type=jnp.float32).reshape(
        feat_rows, 3, head_cols
    )
    grad_bias = jnp.sum(qkv_group, 0, dtype=jnp.float32).reshape(3, head_cols) * bias_mask(
        head_cols
    )
    d_normed1 = col_reduce(qkv_group, qkv_flat.T)
    gain1_part = jnp.sum(d_normed1 * centred1, 0)
    bias1_part = jnp.sum(d_normed1, 0)
    grad_in = d_resid + norm_backward(d_normed1, centred1, inverse1, norm1_gain)
    grad_bias = lax.psum(grad_bias, "dp")
    grad_qkv, grad_proj, grad_gateup, grad_down = [
        over_groups(g) for g in (grad_qkv, grad_proj, grad_gateup, grad_down)
    ]
    gain1_grad, bias1_grad, gain2_grad, bias2_grad = lax.psum(
        (gain1_part, bias1_part, gain2_part, bias2_part), ("dp", "col")
    )
    return (
        block_out,
        grad_in,
        grad_qkv,
        grad_bias,
        grad_proj,
        gain1_grad,
        bias1_grad,
        gain2_grad,
        bias2_grad,
        grad_gateup,
        grad_down,
    )


def solution(mesh):
    return jax.shard_map(
        body,
        mesh=mesh,
        in_specs=(
            P(("dp", "col"), "row"),
            P("row"),
            P("row"),
            P("row", None, "col"),
            P(None, "col"),
            P("col", "row"),
            P("row"),
            P("row"),
            P("row", None, "col"),
            P("col", "row"),
            P(("dp", "col"), "row"),
        ),
        out_specs=(
            P(("dp", "col"), "row"),
            P(("dp", "col"), "row"),
            P("row", None, "col"),
            P(None, "col"),
            P("col", "row"),
            P("row"),
            P("row"),
            P("row"),
            P("row"),
            P("row", None, "col"),
            P("col", "row"),
        ),
        check_vma=False,
    )
```

```python
import math

import jax
import jax.numpy as jnp
from jax import lax
from jax.sharding import PartitionSpec as P

D = 2048
HD = 64
ROT = 16
SEQ = 256

EPS = 1e-05
THETA = 10000.0

HALF = jnp.bfloat16
FULL = jnp.float32


def swap(value, axis, bit):
    size = lax.axis_size(axis)
    return lax.ppermute(value, axis, [(i, i ^ bit) for i in range(size)])


def relative(blocks):
    row = lax.axis_index("row")
    odd, high = row % 2 == 1, row >= 2
    pairs = [(jnp.where(odd, blocks[k ^ 1], blocks[k])) for k in range(4)]
    return [jnp.where(high, pairs[k ^ 2], pairs[k]) for k in range(4)]


def row_exchange(blocks):
    return [blocks[0]] + [swap(blocks[k], "row", k) for k in range(1, 4)]


def col_exchange(blocks):
    return lax.all_to_all(blocks, "col", 0, 0, tiled=True)


def col_gather(local):
    cols = lax.axis_size("col")
    return col_exchange(jnp.broadcast_to(local[None], (cols,) + local.shape).reshape((cols * local.shape[0],) + local.shape[1:]))


def col_scatter(partial):
    cols = lax.axis_size("col")
    parts = col_exchange(partial.astype(HALF))
    parts = parts.reshape((cols, partial.shape[0] // cols) + partial.shape[1:])
    return jnp.sum(parts.astype(FULL), 0)


def row_gather(local):
    across = swap(local, "row", 2)
    beside = swap(local, "row", 1)
    both = swap(across, "row", 1)
    return [local, beside, across, both]


def weight_gather(weight, axis):
    if lax.axis_size("dp") % 2:
        return row_gather(weight)
    odd = lax.axis_index("dp") % 2
    half = weight.shape[axis] // 2
    mine = lax.dynamic_slice_in_dim(weight, odd * half, half, axis)
    first = swap(mine, "row", 2)
    second = swap(first, "dp", 1)
    across = jnp.concatenate(
        [jnp.where(odd == 0, first, second), jnp.where(odd == 0, second, first)], axis
    )
    return [weight, swap(weight, "row", 1), across, swap(across, "row", 1)]


def split_low(vectors):
    count = vectors.shape[0]
    high = lax.reduce_precision(vectors, 8, 7)
    low = (vectors - high).astype(HALF)
    high = high.astype(HALF)
    pad = jnp.zeros((16 - 2 * count, vectors.shape[1]), HALF)
    return jnp.concatenate([high, low, pad], 0)


def join_low(packed, count):
    return packed[:count].astype(FULL) + packed[count : 2 * count].astype(FULL)


def dot(left, right, left_dim=1, right_dim=0):
    return lax.dot_general(
        left, right, (((left_dim,), (right_dim,)), ((), ())), preferred_element_type=FULL
    )


def dot_in(wide, blocks, right_dim):
    width = wide.shape[1] // len(blocks)
    total = None
    for k, block in enumerate(blocks):
        part = dot(wide[:, k * width : (k + 1) * width], block, 1, right_dim)
        total = part if total is None else total + part
    return total


def dot_out(narrow, blocks, right_dim):
    return jnp.concatenate([dot(narrow, b, 1, right_dim).astype(HALF) for b in blocks], 1)


def token_dot(lefts, rights):
    return dot(jnp.concatenate(lefts, 0), jnp.concatenate(rights, 0), 0, 0)


def over_groups(partial):
    if lax.axis_size("dp") != 2:
        return lax.psum(partial, "dp")
    mine = partial.astype(HALF)
    other = swap(mine, "dp", 1)
    return mine.astype(FULL) + other.astype(FULL)


def centre(values):
    mean = jnp.mean(values, 1, keepdims=True)
    second = jnp.mean(values * values, 1, keepdims=True)
    inverse = lax.rsqrt(second - mean * mean + EPS)
    return ((values - mean) * inverse, inverse)


def norm_backward(grad_normed, centred, inverse, gain):
    scaled = grad_normed * gain
    total = jnp.mean(scaled, 1, keepdims=True)
    cross = jnp.mean(scaled * centred, 1, keepdims=True)
    return inverse * (scaled - total - centred * cross)


def tables(length):
    half = ROT // 2
    freqs = THETA ** (-2.0 * jnp.arange(half, dtype=FULL) / ROT)
    angles = jnp.arange(length, dtype=FULL)[:, None] * freqs[None, :]
    return (jnp.cos(angles)[:, None, :], jnp.sin(angles)[:, None, :])


def rotate(vec, cos_t, sin_t):
    half = ROT // 2
    first = vec[..., :half]
    second = vec[..., half:ROT]
    return jnp.concatenate(
        [first * cos_t - second * sin_t, second * cos_t + first * sin_t, vec[..., ROT:]], -1
    )


def bias_mask(width):
    lanes = jnp.arange(width) % HD < ROT
    ones = jnp.ones((width,), FULL)
    return jnp.stack([ones, jnp.where(lanes, 1.0, 0.0).astype(FULL), ones])


def masked_scores(query, keys):
    length = query.shape[0]
    scores = jnp.einsum("qhd,khd->hqk", query, keys, preferred_element_type=FULL) * (
        1.0 / math.sqrt(HD)
    )
    allowed = jnp.arange(length)[:, None] >= jnp.arange(length)[None, :]
    return jnp.where(allowed[None], scores, -1e30)


def attend(query, keys, values):
    scores = masked_scores(query, keys)
    top = jnp.max(scores, -1, keepdims=True)
    lse = top + jnp.log(jnp.sum(jnp.exp(scores - top), -1, keepdims=True))
    probs = jnp.exp(scores - lse).astype(HALF)
    out = jnp.einsum("hqk,khd->qhd", probs, values, preferred_element_type=FULL).astype(HALF)
    return (out, lse)


def attend_back(query, keys, values, output, lse, grad_out):
    scale = 1.0 / math.sqrt(HD)
    delta = jnp.sum(grad_out.astype(FULL) * output.astype(FULL), -1)
    weights = jnp.exp(masked_scores(query, keys) - lse)
    dprobs = jnp.einsum("qhd,khd->hqk", grad_out, values, preferred_element_type=FULL)
    dscores = (weights * (dprobs - delta.T[:, :, None])).astype(HALF)
    grad_query = jnp.einsum("hqk,khd->qhd", dscores, keys, preferred_element_type=FULL) * scale
    grad_keys = jnp.einsum("hqk,qhd->khd", dscores, query, preferred_element_type=FULL) * scale
    grad_values = jnp.einsum(
        "hqk,qhd->khd", weights.astype(HALF), grad_out, preferred_element_type=FULL
    )
    return (grad_query, grad_keys, grad_values)


def body(
    block_in,
    norm1_gain,
    norm1_bias,
    w_qkv,
    qkv_bias,
    w_proj,
    norm2_gain,
    norm2_bias,
    w_gateup,
    w_down,
    out_grad,
):
    rows = lax.axis_size("row")
    cols = lax.axis_size("col")
    col = lax.axis_index("col")
    row = lax.axis_index("row")
    feats = w_qkv.shape[0]
    head_cols = w_qkv.shape[2]
    heads_here = head_cols // HD
    hidden_cols = w_gateup.shape[2]
    tokens = block_in.shape[0]
    chunk = tokens // cols
    width = rows * feats

    def own_chunk(value):
        return lax.dynamic_slice_in_dim(value, col * chunk, chunk, 0)

    def widen(blocks):
        return jnp.concatenate(blocks, 1)

    def narrow(wide):
        return [wide[:, k * feats : (k + 1) * feats] for k in range(rows)]

    def sequence(group, k):
        return lax.dynamic_index_in_dim(group, row ^ k, 0, False)

    qkv_w = row_gather(w_qkv.reshape(feats, 3 * head_cols))
    proj_w = row_gather(w_proj)
    inner_w = weight_gather(w_gateup.reshape(feats, 2 * hidden_cols), 1)
    down_w = weight_gather(w_down, 0)

    scales = split_low(jnp.stack([norm1_gain, norm1_bias, norm2_gain, norm2_bias]))
    in_group = col_gather(block_in).reshape(rows, tokens, feats)
    sent = [jnp.concatenate([sequence(in_group, k), scales], 0) for k in range(rows)]
    got = row_exchange(sent)
    in_seq = widen([g[:tokens] for g in got])
    scales = widen([join_low(g[tokens:], 4) for g in got])
    gain1, shift1, gain2, shift2 = [scales[i : i + 1] for i in range(4)]
    grad_group = col_gather(out_grad).reshape(rows, tokens, feats)
    grad_group = [sequence(grad_group, k) for k in range(rows)]
    grad_seq = widen(row_exchange(grad_group))

    cos_t, sin_t = tables(SEQ)
    normed1 = (centre(in_seq.astype(FULL))[0] * gain1 + shift1).astype(HALF)
    qkv = dot_in(normed1, qkv_w, 0) + qkv_bias.reshape(3 * head_cols)
    parts = qkv.reshape(tokens, 3, heads_here, HD)
    query = rotate(parts[:, 0], cos_t, sin_t).astype(HALF)
    keys = rotate(parts[:, 1], cos_t, sin_t).astype(HALF)
    values = parts[:, 2].astype(HALF)
    attn, lse = attend(query, keys, values)
    attn_flat = attn.reshape(tokens, head_cols)
    resid = own_chunk(in_seq).astype(FULL) + col_scatter(dot_out(attn_flat, proj_w, 0))
    centred2, inverse2 = centre(resid)
    normed2 = col_gather((centred2 * gain2 + shift2).astype(HALF))
    inner = dot_in(normed2, inner_w, 0)
    gate = inner[:, :hidden_cols]
    up = inner[:, hidden_cols:]
    d_hidden = dot_in(grad_seq, down_w, 1)
    sig = jax.nn.sigmoid(gate)
    hidden = (gate * sig * up).astype(HALF)
    d_inner = jnp.concatenate(
        [d_hidden * up * sig * (1.0 + gate * (1.0 - sig)), d_hidden * gate * sig], 1
    ).astype(HALF)
    d_normed2 = col_scatter(dot_out(d_inner, inner_w, 1))
    d_resid = own_chunk(grad_seq).astype(FULL) + norm_backward(
        d_normed2, centred2, inverse2, gain2
    )
    rounded = col_gather(d_resid.astype(HALF))
    d_attn = dot_in(rounded, proj_w, 1).astype(HALF)
    d_query, d_keys, d_values = attend_back(
        query, keys, values, attn, lse, d_attn.reshape(tokens, heads_here, HD)
    )
    d_qkv = (
        jnp.stack([rotate(d_query, cos_t, -sin_t), rotate(d_keys, cos_t, -sin_t), d_values], 1)
        .reshape(tokens, 3 * head_cols)
        .astype(HALF)
    )
    d_normed1 = col_scatter(dot_out(d_qkv, qkv_w, 1))
    centred1, inverse1 = centre(own_chunk(in_seq).astype(FULL))
    grad_in = d_resid + norm_backward(d_normed1, centred1, inverse1, gain1)
    vectors = jnp.stack(
        [
            jnp.sum(d_normed1 * centred1, 0),
            jnp.sum(d_normed1, 0),
            jnp.sum(d_normed2 * centred2, 0),
            jnp.sum(d_normed2, 0),
        ]
    )
    got = row_exchange(
        narrow(jnp.concatenate([grad_in.astype(HALF), split_low(vectors)], 0))
    )
    vectors = split_low(sum(join_low(g[chunk:], 4) for g in got))
    got = relative([g[:chunk] for g in got])
    got = col_exchange(jnp.concatenate([jnp.concatenate([g, vectors], 0) for g in got], 0))
    got = got.reshape(cols, chunk + 16, feats)
    grad_in = got[:, :chunk].reshape(tokens, feats).astype(FULL)
    vectors = sum(join_low(got[k, chunk:], 4) for k in range(cols))
    if lax.axis_size("dp") == 2:
        vectors = vectors + swap(vectors, "dp", 1)
    else:
        vectors = lax.psum(vectors, "dp")

    def by_row(wide):
        return row_exchange(narrow(wide))

    attn_group = row_gather(attn_flat)
    hidden_group = row_gather(hidden)
    own_out = [
        dot(a, w_proj) + dot(h, w_down) for a, h in zip(attn_group, hidden_group)
    ]
    own_out = jnp.concatenate(relative([o.astype(HALF) for o in own_out]), 0)
    block_out = block_in.astype(FULL) + col_scatter(own_out)
    grad_down = over_groups(token_dot(hidden_group, grad_group))
    inner_group = row_gather(d_inner)
    grad_gateup = over_groups(token_dot(by_row(normed2), inner_group))
    grad_proj = over_groups(token_dot(attn_group, by_row(rounded)))
    qkv_group = row_gather(d_qkv)
    grad_qkv = token_dot(by_row(normed1), qkv_group)
    grad_bias = sum(jnp.sum(q.astype(FULL), 0, keepdims=True) for q in qkv_group)
    both = over_groups(jnp.concatenate([grad_qkv, jnp.broadcast_to(grad_bias, (16, 3 * head_cols))], 0))
    grad_qkv = both[:feats]
    grad_bias = both[feats].reshape(3, head_cols) * bias_mask(head_cols)

    gain1_grad, bias1_grad, gain2_grad, bias2_grad = vectors
    return (
        block_out,
        grad_in,
        grad_qkv.reshape(feats, 3, head_cols),
        grad_bias,
        grad_proj,
        gain1_grad,
        bias1_grad,
        gain2_grad,
        bias2_grad,
        grad_gateup.reshape(feats, 2, hidden_cols),
        grad_down,
    )


def solution(mesh):
    return jax.shard_map(
        body,
        mesh=mesh,
        in_specs=(
            P(("dp", "col"), "row"),
            P("row"),
            P("row"),
            P("row", None, "col"),
            P(None, "col"),
            P("col", "row"),
            P("row"),
            P("row"),
            P("row", None, "col"),
            P("col", "row"),
            P(("dp", "col"), "row"),
        ),
        out_specs=(
            P(("dp", "col"), "row"),
            P(("dp", "col"), "row"),
            P("row", None, "col"),
            P(None, "col"),
            P("col", "row"),
            P("row"),
            P("row"),
            P("row"),
            P("row"),
            P("row", None, "col"),
            P("col", "row"),
        ),
        check_vma=False,
    )
```

```python
import functools
import math

import jax
import jax.numpy as jnp
from jax import lax
from jax.experimental import pallas as pl
from jax.experimental.pallas import tpu as pltpu
from jax.sharding import PartitionSpec as P


HD = 64
ROT = 16
SEQ = 256

EPS = 1e-05
THETA = 10000.0
SCALE = 1.0 / math.sqrt(HD)

HALF = jnp.bfloat16
FULL = jnp.float32
LANES = 128
PAIR = LANES // HD
MIB = 1 << 20


DP, ROW, COL = "dp", "row", "col"


def swap(value, axis, bit):
    size = lax.axis_size(axis)
    return lax.ppermute(value, axis, [(i, i ^ bit) for i in range(size)])


def row_exchange(blocks):
    return [blocks[0]] + [swap(blocks[k], ROW, k) for k in range(1, 4)]


def col_exchange(blocks):
    return lax.all_to_all(blocks, COL, 0, 0, tiled=True)


def row_gather(local):
    across = swap(local, ROW, 2)
    beside = swap(local, ROW, 1)
    both = swap(across, ROW, 1)
    return [local, beside, across, both]


def across(mine):
    first = swap(mine, ROW, 2)
    second = swap(first, DP, 1)
    third = swap(first, ROW, 1)
    return [first, second, third, swap(second, ROW, 1)]


def half_of(weight):
    half = weight.shape[0] // 2
    odd = lax.axis_index(DP) % 2
    return lax.dynamic_slice_in_dim(weight, odd * half, half, 0)


def total(pairs, shape, axis=1, tile=64):
    rows = shape[1 - axis]
    block = (tile, *shape[1:]) if axis == 1 else (shape[0], tile, shape[2])
    parts = [part for pair in pairs for part in pair]
    return pl.pallas_call(
        functools.partial(total_kernel, axis),
        grid=(rows // tile,),
        out_shape=jax.ShapeDtypeStruct(shape, FULL),
        in_specs=[pl.BlockSpec((tile, p.shape[1]), lambda n: (n, 0)) for p in parts],
        out_specs=pl.BlockSpec(block, (lambda n: (n, 0, 0)) if axis == 1 else (lambda n: (0, n, 0))),
        compiler_params=pltpu.CompilerParams(vmem_limit_bytes=8 * MIB),
        cost_estimate=pl.CostEstimate(
            flops=math.prod(shape), bytes_accessed=8 * math.prod(shape), transcendentals=0
        ),
    )(*parts)


def over_groups(mine):
    return lax.psum(mine.astype(FULL), DP)


def places(refs, axis, odd):
    size = refs[0].shape[axis]
    if len(refs) == 4:
        return [(ref, k * size, size) for k, ref in enumerate(refs)]
    half = size // 2
    own, beside, first, second, first_b, second_b = refs
    near = pl.multiple_of(odd * half, LANES)
    far = pl.multiple_of((1 - odd) * half, LANES)
    return [
        (own, 0, size),
        (beside, size, size),
        (first, 2 * size + near, half),
        (second, 2 * size + far, half),
        (first_b, 3 * size + near, half),
        (second_b, 3 * size + far, half),
    ]


def staged(refs, axis, odd, buffer, sems):
    copies, views, at = [], [], 0
    for i, (ref, start, size) in enumerate(places(refs, axis, odd)):
        here = pl.ds(at, size)
        view = buffer.at[here] if axis == 0 else buffer.at[:, here]
        copies.append(pltpu.make_async_copy(ref, view, sems.at[i]))
        views.append((view, start, size))
        at += size
    return copies, views


def lanes(at, size):
    return pl.ds(at if isinstance(at, int) else pl.multiple_of(at, LANES), size)


def added(terms):
    total = None
    for term in terms:
        total = term if total is None else total + term
    return total


def begin(copies):
    for copy in copies:
        copy.start()


def wait(copies):
    for copy in copies:
        copy.wait()


def nn(left, right):
    return lax.dot_general(left, right, (((1,), (0,)), ((), ())), preferred_element_type=FULL)


def nt(left, right):
    return lax.dot_general(left, right, (((1,), (1,)), ((), ())), preferred_element_type=FULL)


def tn(left, right):
    return lax.dot_general(left, right, (((0,), (0,)), ((), ())), preferred_element_type=FULL)


def tiles(extent, size, step):
    whole = extent // size

    def one(n, _):
        step(pl.multiple_of(n * size, size), size)
        return 0

    lax.fori_loop(0, whole, one, 0)
    if extent % size:
        step(whole * size, extent % size)


def turn(value, cos_t, down, up):
    return (
        value * cos_t
        + pltpu.roll(value, LANES - ROT // 2, 1) * down
        + pltpu.roll(value, ROT // 2, 1) * up
    )


def stats(values):
    mean = jnp.mean(values, 1, keepdims=True)
    second = jnp.mean(values * values, 1, keepdims=True)
    return mean, lax.rsqrt(second - mean * mean + EPS)


def causal(length):
    at = lax.broadcasted_iota(jnp.int32, (length, length), 0)
    return at >= lax.broadcasted_iota(jnp.int32, (length, length), 1)


def own_half(value, head):
    lane = lax.broadcasted_iota(jnp.int32, value.shape, 1)
    return jnp.where((lane < HD) == (head == 0), value, jnp.zeros_like(value))


def either(first, second):
    lane = lax.broadcasted_iota(jnp.int32, first.shape, 1)
    return jnp.where(lane < HD, first, second)


def backwards(product, part, part_h, odd, sems):
    size = part.shape[1] // 8

    def piece(n):
        at = lanes(jnp.where(n < 4, n, n ^ odd) * size, size)
        return at, pltpu.make_async_copy(part.at[:, at], part_h.at[:, at], sems.at[n])

    def one(n, _):
        at, copy = piece(n)
        part[:, at] = product(pl.ds(pl.multiple_of(n * size, size), size)).astype(HALF)
        copy.start()
        return 0

    lax.fori_loop(0, 8, one, 0, unroll=2)
    for n in range(8):
        piece(n)[1].wait()


def out_piece(source, target, start, size, sem):
    copy = pltpu.make_async_copy(
        source.at[:, lanes(start, size)], target.at[:, lanes(start, size)], sem
    )
    copy.start()
    return copy


def halves_kernel(place, inner, down, gate_h, up_h, down_h, wide, tall, sems):
    size, width = gate_h.shape
    at = pl.ds(pl.multiple_of(place[0] * size, size), size)
    loads = [
        pltpu.make_async_copy(down.at[:, at], tall, sems.at[0]),
        pltpu.make_async_copy(inner.at[at, 0:width], wide.at[0], sems.at[1]),
        pltpu.make_async_copy(inner.at[at, width : 2 * width], wide.at[1], sems.at[2]),
    ]
    stores = [
        pltpu.make_async_copy(tall, down_h, sems.at[3]),
        pltpu.make_async_copy(wide.at[0], gate_h, sems.at[4]),
        pltpu.make_async_copy(wide.at[1], up_h, sems.at[5]),
    ]
    begin(loads)
    for load, store in zip(loads, stores):
        load.wait()
        store.start()
    wait(stores)


def attention_kernel(place, *refs):
    x = refs[0:4]
    qkv_w, proj_w = refs[4:10], refs[10:14]
    bias, tables = refs[14:16]
    normed_h, qkv_h, attn_h, lse_h, part_h, keep_h = refs[16:22]
    normed, raw, xs, w1, w2, qkv, attn, lse, part, keep, sems = refs[22:]
    tokens, wide = normed.shape
    feats = wide // 4
    head_cols = attn.shape[1]
    store = pltpu.make_async_copy(normed, normed_h, sems.at[0])
    loads = [pltpu.make_async_copy(x[k], xs.at[k], sems.at[1 + k]) for k in range(4)]
    copies, views = staged(qkv_w, 0, place[0], w1, sems.at[pl.ds(5, 6)])
    copies2, views2 = staged(proj_w, 1, place[0], w2, sems.at[pl.ds(11, 4)])
    stores = [
        pltpu.make_async_copy(a, b, sems.at[15 + i])
        for i, (a, b) in enumerate(((qkv, qkv_h), (attn, attn_h), (lse, lse_h)))
    ]
    keeping = pltpu.make_async_copy(keep, keep_h, sems.at[18])
    chunk = keep.shape[0] - 8
    scales = keep.at[pl.ds(chunk, 8)]
    begin(loads + copies[:1])
    wait(loads)
    begin(copies[1:])
    for k in range(4):
        packed = xs[k, tokens : tokens + 16, :].astype(FULL)
        scales[:, k * feats : (k + 1) * feats] = packed[:8] + packed[8:]
    step = 32

    def norm(i, _):
        at = pl.ds(pl.multiple_of(i * step, step), step)
        values = jnp.concatenate([xs[k, at, :].astype(FULL) for k in range(4)], 1)
        mean, inverse = stats(values)
        normed[at, :] = ((values - mean) * inverse * scales[0:1] + scales[1:2]).astype(HALF)
        return 0

    lax.fori_loop(0, tokens // step, norm, 0)
    store.start()
    at = pl.ds(pl.multiple_of(place[2] * chunk, chunk), chunk)
    for k in range(4):
        keep[0:chunk, k * feats : (k + 1) * feats] = xs[k, at, :].astype(FULL)
    keeping.start()
    for i, (view, start, rows) in enumerate(views):
        wait(copies[i : i + 1])

        def product(at, size, i=i, view=view, start=start, rows=rows):
            at = pl.ds(at, size)
            value = nn(normed[:, lanes(start, rows)], view[:, at])
            raw[:, at] = value + (bias[:, at] if i == 0 else raw[:, at])

        tiles(3 * head_cols, 768, product)
    begin(copies2)
    mask = causal(tokens)
    lane = lax.broadcasted_iota(jnp.int32, (tokens, LANES), 1)

    def pair(p, _):
        at = [pl.ds(pl.multiple_of(j * head_cols + p * LANES, LANES), LANES) for j in range(3)]
        query = turn(raw[:, at[0]], tables[0], tables[1], tables[2]).astype(HALF)
        keys = turn(raw[:, at[1]], tables[0], tables[1], tables[2]).astype(HALF)
        values = raw[:, at[2]].astype(HALF)
        qkv[:, at[0]] = query
        qkv[:, at[1]] = keys
        qkv[:, at[2]] = values
        outs = []
        for h in range(PAIR):
            scores = jnp.where(mask, nt(own_half(query, h), keys) * SCALE, -1e30)
            top = jnp.max(scores, 1, keepdims=True)
            raised = jnp.exp(scores - top)
            total = jnp.sum(raised, 1, keepdims=True)
            lse[...] = jnp.where(lane == p * PAIR + h, top + jnp.log(total), lse[...])
            outs.append(nn((raised * (1.0 / total)).astype(HALF), values))
        attn[:, at[0]] = either(*outs).astype(HALF)
        return 0

    lax.fori_loop(0, head_cols // LANES, pair, 0)
    begin(stores)
    wait(copies2)
    outs = []
    for i, (view, start, size) in enumerate(views2):
        part[:, lanes(start, size)] = nn(attn[...], view[...]).astype(HALF)
        outs.append(out_piece(part, part_h, start, size, sems.at[19 + i]))
    wait([store, keeping] + stores + outs)


def received(got, chunk):
    total = got[0:chunk, :].astype(FULL)
    for c in range(1, got.shape[0] // chunk):
        total = total + got[c * chunk : (c + 1) * chunk, :].astype(FULL)
    return total


def second_norm_kernel(got, keep_h, copies_h, resid_h, keep, resid, normed, sems):
    chunk = resid.shape[0]
    load = pltpu.make_async_copy(keep_h, keep, sems.at[0])
    load.start()
    values = received(got, chunk)
    load.wait()
    values = values + keep[0:chunk]
    resid[...] = values
    store = pltpu.make_async_copy(resid, resid_h, sems.at[1])
    store.start()
    mean, inverse = stats(values)
    scales = keep[chunk : chunk + 8]
    normed[...] = ((values - mean) * inverse * scales[2:3] + scales[3:4]).astype(HALF)
    wait([store] + out_copies(normed, copies_h, sems, 2))


def out_copies(source, target, sems, first):
    rows = source.shape[0]
    copies = [
        pltpu.make_async_copy(source, target.at[pl.ds(n * rows, rows)], sems.at[first + n])
        for n in range(target.shape[0] // rows)
    ]
    begin(copies)
    return copies


def down_kernel(place, *refs):
    g, down_w = refs[0:4], refs[4:-7]
    dh_h, own_h, dh, gs, w1, own, sems = refs[-7:]
    feats = g[0].shape[1]
    loads = [
        pltpu.make_async_copy(g[k], gs.at[:, k * feats : (k + 1) * feats], sems.at[k])
        for k in range(4)
    ]
    copies, views = staged(down_w, 1, place[0], w1, sems.at[pl.ds(4, 6)])
    stores = [
        pltpu.make_async_copy(dh, dh_h, sems.at[10]),
        pltpu.make_async_copy(own, own_h, sems.at[11]),
    ]
    begin(loads + copies[:2])
    wait(loads)
    chunk = own.shape[0]
    own[...] = gs[pl.ds(pl.multiple_of(place[2] * chunk, chunk), chunk), :]
    stores[1].start()
    for i, (view, start, cols) in enumerate(views):
        wait(copies[i : i + 1])
        begin(copies[i + 2 : i + 3])
        value = nt(gs[:, lanes(start, cols)], view[...])
        dh[...] = value if i == 0 else dh[...] + value
    stores[0].start()
    wait(stores)


def mlp_kernel(place, *refs):
    normed, dh_h = refs[0:2]
    hidden_h, gate_h, up_h, part_h = refs[12:16]
    gate, up, w1, w2, hidden, d_gate, d_up, dh, part, sems = refs[16:]
    width = hidden.shape[1]
    gate_w = [ref.at[:, 0:width] for ref in refs[2:4]] + list(refs[4:8])
    up_w = [ref.at[:, width : 2 * width] for ref in refs[2:4]] + list(refs[8:12])
    stores = [
        pltpu.make_async_copy(a, b, sems.at[i])
        for i, (a, b) in enumerate(((hidden, hidden_h), (d_gate, gate_h), (d_up, up_h)))
    ]
    load = pltpu.make_async_copy(dh_h, dh, sems.at[3])
    copies, views = staged(gate_w, 0, place[0], w1, sems.at[pl.ds(4, 6)])
    copies2, views2 = staged(up_w, 0, place[0], w2, sems.at[pl.ds(10, 6)])
    copies = copies + copies2
    begin(copies[:3])
    for i, (view, start, rows) in enumerate(views + views2):
        wait(copies[i : i + 1])
        begin(copies[i + 3 : i + 4])
        if i == 6:
            load.start()
        acc = gate if i < 6 else up
        value = nn(normed[:, lanes(start, rows)], view[...])
        acc[...] = value if i % 6 == 0 else acc[...] + value
    load.wait()

    def act(n, _):
        at = pl.ds(pl.multiple_of(n * LANES, LANES), LANES)
        one, two, grad = gate[:, at], up[:, at], dh[:, at]
        sig = 1.0 / (1.0 + jnp.exp(-one))
        silu = one * sig
        hidden[:, at] = (silu * two).astype(HALF)
        d_gate[:, at] = (grad * two * sig * (1.0 + one * (1.0 - sig))).astype(HALF)
        d_up[:, at] = (grad * silu).astype(HALF)
        return 0

    lax.fori_loop(0, width // LANES, act, 0)
    begin(stores)

    def back(at):
        return nt(d_gate[...], w1[at, :]) + nt(d_up[...], w2[at, :])

    backwards(back, part, part_h, place[0], sems.at[pl.ds(16, 8)])
    wait(stores)


def norm_back(grad_normed, values, gain):
    mean, inverse = stats(values)
    centred = (values - mean) * inverse
    scaled = grad_normed * gain
    total = jnp.mean(scaled, 1, keepdims=True)
    cross = jnp.mean(scaled * centred, 1, keepdims=True)
    back = inverse * (scaled - total - centred * cross)
    return (
        back,
        jnp.sum(grad_normed * centred, 0, keepdims=True),
        jnp.sum(grad_normed, 0, keepdims=True),
    )


def second_back_kernel(got, resid_h, own_h, keep_h, copies_h, d_resid_h, resid, own, keep, d_resid, rounded, sems):
    chunk = resid.shape[0]
    loads = [
        pltpu.make_async_copy(a, b, sems.at[i])
        for i, (a, b) in enumerate(((resid_h, resid), (own_h, own), (keep_h, keep)))
    ]
    begin(loads)
    grad = received(got, chunk)
    wait(loads)
    back, gain, shift = norm_back(grad, resid[...], keep[chunk + 2 : chunk + 3])
    total = own[...].astype(FULL) + back
    rounded[...] = total.astype(HALF)
    copies = out_copies(rounded, copies_h, sems, 4)
    d_resid[0:chunk] = total
    row = lax.broadcasted_iota(jnp.int32, (8, gain.shape[1]), 0)
    d_resid[chunk : chunk + 8] = jnp.where(row == 2, gain, jnp.where(row == 3, shift, 0.0))
    store = pltpu.make_async_copy(d_resid, d_resid_h, sems.at[3])
    store.start()
    wait(copies + [store])


def attention_back_kernel(place, *refs):
    rounded, qkv_h, attn_h, lse_h, tables_h = refs[0:5]
    qkv_w, proj_w = refs[5:11], refs[11:15]
    d_qkv_h, part_h, d_attn, d_qkv, w1, w2, qkv, attn, lse, tables, part, sems = refs[15:]
    tokens = rounded.shape[0]
    head_cols = attn.shape[1]
    store = pltpu.make_async_copy(d_qkv, d_qkv_h, sems.at[0])
    copies2, views2 = staged(proj_w, 1, place[0], w2, sems.at[pl.ds(1, 4)])
    copies, _ = staged(qkv_w, 0, place[0], w1, sems.at[pl.ds(5, 6)])
    loads = [
        pltpu.make_async_copy(a, b, sems.at[11 + i])
        for i, (a, b) in enumerate(
            ((qkv_h, qkv), (attn_h, attn), (lse_h, lse), (tables_h, tables))
        )
    ]
    begin(copies2 + loads)
    wait(copies2)
    begin(copies)
    d_attn[...] = added(
        nt(rounded[:, lanes(start, size)], view[...]) for view, start, size in views2
    ).astype(HALF)
    wait(loads)
    mask = causal(tokens)
    lane = lax.broadcasted_iota(jnp.int32, (tokens, LANES), 1)

    def pair(p, _):
        at = [pl.ds(pl.multiple_of(j * head_cols + p * LANES, LANES), LANES) for j in range(3)]
        query, keys, values = [qkv[:, a] for a in at]
        grad = d_attn[:, at[0]]
        product = grad.astype(FULL) * attn[:, at[0]].astype(FULL)
        dq, dk, dv = [], [], []
        for h in range(PAIR):
            delta = jnp.sum(own_half(product, h), 1, keepdims=True)
            total = jnp.sum(jnp.where(lane == p * PAIR + h, lse[...], 0.0), 1, keepdims=True)
            scores = jnp.where(mask, nt(own_half(query, h), keys) * SCALE, -1e30)
            weights = jnp.exp(scores - total)
            d_probs = nt(own_half(grad, h), values)
            d_scores = (weights * (d_probs - delta)).astype(HALF)
            dq.append(nn(d_scores, keys))
            dk.append(tn(d_scores, query))
            dv.append(tn(weights.astype(HALF), grad))
        dq = either(*dq) * SCALE
        dk = either(*dk) * SCALE
        d_qkv[:, at[0]] = turn(dq, tables[0], -tables[1], -tables[2]).astype(HALF)
        d_qkv[:, at[1]] = turn(dk, tables[0], -tables[1], -tables[2]).astype(HALF)
        d_qkv[:, at[2]] = either(*dv).astype(HALF)
        return 0

    lax.fori_loop(0, head_cols // LANES, pair, 0)
    store.start()
    wait(copies)
    backwards(lambda at: nt(d_qkv[...], w1[at, :]), part, part_h, place[0], sems.at[pl.ds(15, 8)])
    store.wait()


def split_low(value, out, at):
    high = value.astype(HALF)
    out[at : at + 8, :] = high
    out[at + 8 : at + 16, :] = (value - high.astype(FULL)).astype(HALF)


def first_back_kernel(got, d_resid_h, keep_h, out, d_resid, keep, sems):
    chunk = out.shape[0] - 16
    loads = [
        pltpu.make_async_copy(d_resid_h, d_resid, sems.at[0]),
        pltpu.make_async_copy(keep_h, keep, sems.at[1]),
    ]
    begin(loads)
    grad = received(got, chunk)
    wait(loads)
    back, gain, shift = norm_back(grad, keep[0:chunk], keep[chunk : chunk + 1])
    out[0:chunk, :] = (d_resid[0:chunk] + back).astype(HALF)
    sums = d_resid[chunk : chunk + 8]
    row = lax.broadcasted_iota(jnp.int32, sums.shape, 0)
    split_low(jnp.where(row == 0, gain, jnp.where(row == 1, shift, sums)), out, chunk)


def pack_kernel(place, g0, g1, g2, g3, out):
    blocks = (g0, g1, g2, g3)
    chunk = g0.shape[0] - 16
    total = added(
        g[chunk : chunk + 8, :].astype(FULL) + g[chunk + 8 : chunk + 16, :].astype(FULL)
        for g in blocks
    )
    for k, g in enumerate(blocks):
        at = place[1] ^ k
        out[at, 0:chunk, :] = g[0:chunk, :]
        split_low(total, out.at[at], chunk)


def down_grad_kernel(place, *refs):
    hidden, own_g, other_g, out_h = refs[0:8], refs[8], refs[9], refs[10]
    left, turned, right, out, sems = refs[11:]
    rows, width = hidden[0].shape
    loads = []
    for n, group in enumerate((own_g, other_g)):
        base = (place[0] if n == 0 else 1 - place[0]) * 4
        for k in range(4):
            at = pl.ds(pl.multiple_of((base + k) * rows, rows), rows)
            loads.append(
                [
                    pltpu.make_async_copy(hidden[4 * n + k], left.at[base + k], sems.at[8 * n + k]),
                    pltpu.make_async_copy(
                        group.at[place[1] ^ k], right.at[at], sems.at[8 * n + 4 + k]
                    ),
                ]
            )
    for copies in loads:
        begin(copies)
    for copies in loads:
        wait(copies)

    def transpose(n, _):
        turned[:, pl.ds(pl.multiple_of(n * rows, rows), rows)] = left[n].T
        return 0

    lax.fori_loop(0, 8, transpose, 0)
    size = width // 4

    def store(n):
        at = pl.ds(pl.multiple_of(n * size, 16), size)
        return pltpu.make_async_copy(out.at[at], out_h.at[at], sems.at[16 + n])

    def product(n, _):
        at = pl.ds(pl.multiple_of(n * size, 16), size)
        out[at, :] = nn(turned[at, :], right[...])
        store(n).start()
        return 0

    lax.fori_loop(0, 4, product, 0)
    wait([store(n) for n in range(4)])


def weight_grad_kernel(ones, tile, *refs):
    lefts, rights, out_h = refs[0:4], refs[4:8], refs[8]
    left, turned, right, out, sems = refs[9:]
    rows, width = lefts[0].shape
    cols = right.shape[1]
    loads = [pltpu.make_async_copy(lefts[k], left.at[k], sems.at[k]) for k in range(4)]
    loads2 = [
        pltpu.make_async_copy(rights[k], right.at[pl.ds(k * rows, rows)], sems.at[4 + k])
        for k in range(4)
    ]
    begin(loads + loads2)
    for k in range(4):
        wait(loads[k : k + 1])
        turned[:, k * rows : (k + 1) * rows] = left[k].T
    wait(loads2)

    def store(at, size, n):
        return pltpu.make_async_copy(
            out.at[:, pl.ds(at, size)], out_h.at[:, pl.ds(at, size)], sems.at[8 + n]
        )

    def product(at, size):
        n = at // tile
        at = pl.ds(at, size)
        out[0:width, at] = nn(turned[...], right[:, at]).astype(HALF)
        if ones:
            total = jnp.sum(right[:, at].astype(FULL), 0, keepdims=True)
            high = total.astype(HALF).astype(FULL)
            row = lax.broadcasted_iota(jnp.int32, (16, size), 0)
            out[width : width + 16, at] = jnp.where(row < 8, high, total - high).astype(HALF)
        store(at.start, size, n).start()

    tiles(cols, tile, product)
    for at in range(0, cols, tile):
        store(at, min(tile, cols - at), at // tile).wait()


def total_kernel(axis, *refs):
    out = refs[-1]
    width = out.shape[2]
    j = 0
    for mine, other in zip(refs[0:-1:2], refs[1:-1:2]):
        for n in range(mine.shape[1] // width):
            at = slice(n * width, (n + 1) * width)
            value = mine[:, at].astype(FULL) + other[:, at].astype(FULL)
            if axis == 1:
                out[:, j, :] = value
            else:
                out[j] = value
            j += 1


def leaf_kernel(place, *refs):
    attn, hidden = refs[0:4], refs[4:8]
    proj_h, down_h, out_h = refs[8:11]
    w1, w2, left, left2, out, sems = refs[11:]
    tokens = attn[0].shape[0]
    loads = [
        pltpu.make_async_copy(proj_h, w1, sems.at[0]),
        pltpu.make_async_copy(down_h, w2, sems.at[1]),
    ]
    loads2 = [
        [
            pltpu.make_async_copy(attn[k], left.at[k], sems.at[2 + 2 * k]),
            pltpu.make_async_copy(hidden[k], left2.at[k], sems.at[3 + 2 * k]),
        ]
        for k in range(4)
    ]
    begin(loads)
    for copies in loads2:
        begin(copies)
    wait(loads)
    stores = []
    for k in range(4):
        wait(loads2[k])
        at = pl.ds(pl.multiple_of((place[1] ^ k) * tokens, tokens), tokens)
        out[k] = (nn(left[k], w1[...]) + nn(left2[k], w2[...])).astype(HALF)
        stores.append(pltpu.make_async_copy(out.at[k], out_h.at[at], sems.at[10 + k]))
        stores[k].start()
    wait(stores)


VM = pl.BlockSpec(memory_space=pltpu.VMEM)
SM = pl.BlockSpec(memory_space=pltpu.SMEM)
HB = pl.BlockSpec(memory_space=pltpu.HBM)


def call(kernel, specs, outs, args, scratch=(), flops=0, limit=None):
    moved = sum(a.size * a.dtype.itemsize for a in args)
    moved += sum(math.prod(s) * jnp.dtype(t).itemsize for s, t, _ in outs)
    return pl.pallas_call(
        kernel,
        out_shape=[pltpu.HBM(s, t) if m is HB else jax.ShapeDtypeStruct(s, t) for s, t, m in outs],
        in_specs=specs,
        out_specs=[m for _, _, m in outs],
        scratch_shapes=list(scratch),
        compiler_params=pltpu.CompilerParams(vmem_limit_bytes=limit),
        cost_estimate=pl.CostEstimate(flops=flops, bytes_accessed=moved, transcendentals=0),
    )(*[
        pltpu.with_memory_space_constraint(a, pltpu.HBM) if m is HB else a
        for a, m in zip(args, specs, strict=True)
    ])


def weight_grad(lefts, rights, ones=False, tile=512):
    rows, width = lefts[0].shape
    cols = rights[0].shape[1]
    high = width + (16 if ones else 0)
    size = 2 * (8 * rows * width + 4 * rows * cols + high * cols)
    (out,) = call(
        functools.partial(weight_grad_kernel, ones, tile),
        [HB] * 8,
        [((high, cols), HALF, HB)],
        [*lefts, *rights],
        [
            pltpu.VMEM((4, rows, width), HALF),
            pltpu.VMEM((width, 4 * rows), HALF),
            pltpu.VMEM((4 * rows, cols), HALF),
            pltpu.VMEM((high, cols), HALF),
            pltpu.SemaphoreType.DMA((8 + -(-cols // tile),)),
        ],
        flops=8 * rows * width * cols,
        limit=size + 4 * MIB,
    )
    return out


def rotation_tables(length):
    half = ROT // 2
    lane = jnp.arange(LANES) % HD
    freqs = THETA ** (-2.0 * (lane % half).astype(FULL) / ROT)
    angles = jnp.arange(length, dtype=FULL)[:, None] * freqs[None, :]
    cos_t = jnp.where(lane < ROT, jnp.cos(angles), 1.0)
    sin_t = jnp.sin(angles)
    down = jnp.where(lane < half, -sin_t, 0.0)
    up = jnp.where((lane >= half) & (lane < ROT), sin_t, 0.0)
    return jnp.stack([cos_t, down, up])


def bias_mask(width):
    lanes = jnp.arange(width) % HD < ROT
    ones = jnp.ones((width,), FULL)
    return jnp.stack([ones, jnp.where(lanes, 1.0, 0.0).astype(FULL), ones])


def block(
    block_in,
    norm1_gain,
    norm1_bias,
    w_qkv,
    qkv_bias,
    w_proj,
    norm2_gain,
    norm2_bias,
    w_gateup,
    w_down,
    out_grad,
):
    rows = lax.axis_size(ROW)
    cols = lax.axis_size(COL)
    col = lax.axis_index(COL)
    row = lax.axis_index(ROW)
    odd = lax.axis_index(DP) % 2
    two = lax.axis_size(DP) == 2
    feats = w_qkv.shape[0]
    head_cols = w_qkv.shape[2]
    width = w_gateup.shape[2]
    tokens = block_in.shape[0]
    chunk = tokens // cols
    wide = rows * feats
    place = jnp.stack([odd, row, col, odd]).astype(jnp.int32)
    tables = rotation_tables(SEQ)

    def narrow(value):
        return [value[:, k * feats : (k + 1) * feats] for k in range(rows)]

    def sequence(group, k):
        return lax.dynamic_index_in_dim(group, row ^ k, 0, False)

    def copies_of(local):
        return jnp.broadcast_to(local[None], (cols,) + local.shape).reshape(cols * tokens, feats)

    own_qkv = w_qkv.reshape(feats, 3 * head_cols)
    own_inner = w_gateup.reshape(feats, 2 * width)
    in_group = col_exchange(copies_of(block_in)).reshape(rows, tokens, feats)
    qkv_w = [own_qkv, swap(own_qkv, ROW, 1), *across(half_of(own_qkv))]
    proj_w = row_gather(w_proj)
    beside = swap(own_inner, ROW, 1)
    inner_w = [own_inner, beside]
    gate_half, up_half, down_half = call(
        halves_kernel,
        [SM, HB, HB],
        [((feats // 2, width), HALF, HB)] * 2 + [((width, feats // 2), HALF, HB)],
        [place, own_inner, w_down],
        [
            pltpu.VMEM((2, feats // 2, width), HALF),
            pltpu.VMEM((width, feats // 2), HALF),
            pltpu.SemaphoreType.DMA((6,)),
        ],
        limit=4 * MIB,
    )
    down_w = [w_down, swap(w_down, ROW, 1), *across(down_half)]
    inner_w += across(gate_half) + across(up_half)
    scales = jnp.concatenate(
        [jnp.stack([norm1_gain, norm1_bias, norm2_gain, norm2_bias]), jnp.zeros((4, feats), FULL)], 0
    )
    high = lax.reduce_precision(scales, 8, 7)
    packed = jnp.concatenate([high.astype(HALF), (scales - high).astype(HALF)], 0)
    x = row_exchange([jnp.concatenate([sequence(in_group, k), packed], 0) for k in range(rows)])
    grad_group = col_exchange(copies_of(out_grad)).reshape(rows, tokens, feats)
    grad_seq = row_exchange([sequence(grad_group, k) for k in range(rows)])

    normed1, qkv, attn, lse, part, keep = call(
        attention_kernel,
        [SM] + [HB] * 14 + [VM] * 2,
        [
            ((tokens, wide), HALF, HB),
            ((tokens, 3 * head_cols), HALF, HB),
            ((tokens, head_cols), HALF, HB),
            ((tokens, LANES), FULL, HB),
            ((tokens, wide), HALF, HB),
            ((chunk + 8, wide), FULL, HB),
        ],
        [place, *x, *qkv_w, *proj_w, qkv_bias.reshape(1, 3 * head_cols), tables],
        [
            pltpu.VMEM((tokens, wide), HALF),
            pltpu.VMEM((tokens, 3 * head_cols), FULL),
            pltpu.VMEM((4, tokens + 16, feats), HALF),
            pltpu.VMEM((wide, 3 * head_cols), HALF),
            pltpu.VMEM((head_cols, wide), HALF),
            pltpu.VMEM((tokens, 3 * head_cols), HALF),
            pltpu.VMEM((tokens, head_cols), HALF),
            pltpu.VMEM((tokens, LANES), FULL),
            pltpu.VMEM((tokens, wide), HALF),
            pltpu.VMEM((chunk + 8, wide), FULL),
            pltpu.SemaphoreType.DMA((23,)),
        ],
        flops=2 * tokens * wide * 4 * head_cols,
        limit=20 * MIB,
    )
    got = col_exchange(part.reshape(cols, chunk, wide)).reshape(tokens, wide)
    copies, resid = call(
        second_norm_kernel,
        [VM, HB],
        [((tokens, wide), HALF, HB), ((chunk, wide), FULL, HB)],
        [got, keep],
        [
            pltpu.VMEM((chunk + 8, wide), FULL),
            pltpu.VMEM((chunk, wide), FULL),
            pltpu.VMEM((chunk, wide), HALF),
            pltpu.SemaphoreType.DMA((2 + cols,)),
        ],
        limit=8 * MIB,
    )
    normed2 = col_exchange(copies.reshape(cols, chunk, wide)).reshape(tokens, wide)
    d_hidden, own_grad = call(
        down_kernel,
        [SM] + [HB] * (4 + len(down_w)),
        [((tokens, width), FULL, HB), ((chunk, wide), HALF, HB)],
        [place, *grad_seq, *down_w],
        [
            pltpu.VMEM((tokens, width), FULL),
            pltpu.VMEM((tokens, wide), HALF),
            pltpu.VMEM((width, wide), HALF),
            pltpu.VMEM((chunk, wide), HALF),
            pltpu.SemaphoreType.DMA((12,)),
        ],
        flops=2 * tokens * wide * width,
        limit=12 * MIB,
    )
    hidden, d_gate, d_up, part = call(
        mlp_kernel,
        [SM, VM] + [HB] * 11,
        [
            ((tokens, width), HALF, HB),
            ((tokens, width), HALF, HB),
            ((tokens, width), HALF, HB),
            ((tokens, wide), HALF, HB),
        ],
        [place, normed2, d_hidden, *inner_w],
        [
            pltpu.VMEM((tokens, width), FULL),
            pltpu.VMEM((tokens, width), FULL),
            pltpu.VMEM((wide, width), HALF),
            pltpu.VMEM((wide, width), HALF),
            pltpu.VMEM((tokens, width), HALF),
            pltpu.VMEM((tokens, width), HALF),
            pltpu.VMEM((tokens, width), HALF),
            pltpu.VMEM((tokens, width), FULL),
            pltpu.VMEM((tokens, wide), HALF),
            pltpu.SemaphoreType.DMA((24,)),
        ],
        flops=2 * tokens * wide * 4 * width,
        limit=26 * MIB,
    )
    got = col_exchange(part.reshape(cols, chunk, wide)).reshape(tokens, wide)
    copies, d_resid = call(
        second_back_kernel,
        [VM] + [HB] * 3,
        [((tokens, wide), HALF, HB), ((chunk + 8, wide), FULL, HB)],
        [got, resid, own_grad, keep],
        [
            pltpu.VMEM((chunk, wide), FULL),
            pltpu.VMEM((chunk, wide), HALF),
            pltpu.VMEM((chunk + 8, wide), FULL),
            pltpu.VMEM((chunk + 8, wide), FULL),
            pltpu.VMEM((chunk, wide), HALF),
            pltpu.SemaphoreType.DMA((4 + cols,)),
        ],
        limit=8 * MIB,
    )
    rounded = col_exchange(copies.reshape(cols, chunk, wide)).reshape(tokens, wide)
    d_qkv, part = call(
        attention_back_kernel,
        [SM, VM] + [HB] * 14,
        [((tokens, 3 * head_cols), HALF, HB), ((tokens, wide), HALF, HB)],
        [place, rounded, qkv, attn, lse, tables, *qkv_w, *proj_w],
        [
            pltpu.VMEM((tokens, head_cols), HALF),
            pltpu.VMEM((tokens, 3 * head_cols), HALF),
            pltpu.VMEM((wide, 3 * head_cols), HALF),
            pltpu.VMEM((head_cols, wide), HALF),
            pltpu.VMEM((tokens, 3 * head_cols), HALF),
            pltpu.VMEM((tokens, head_cols), HALF),
            pltpu.VMEM((tokens, LANES), FULL),
            pltpu.VMEM((3, tokens, LANES), FULL),
            pltpu.VMEM((tokens, wide), HALF),
            pltpu.SemaphoreType.DMA((23,)),
        ],
        flops=2 * tokens * wide * 5 * head_cols,
        limit=18 * MIB,
    )
    got = col_exchange(part.reshape(cols, chunk, wide)).reshape(tokens, wide)
    (last,) = call(
        first_back_kernel,
        [VM, HB, HB],
        [((chunk + 16, wide), HALF, VM)],
        [got, d_resid, keep],
        [
            pltpu.VMEM((chunk + 8, wide), FULL),
            pltpu.VMEM((chunk + 8, wide), FULL),
            pltpu.SemaphoreType.DMA((2,)),
        ],
        limit=8 * MIB,
    )

    got = row_exchange(narrow(last))
    (packed,) = call(
        pack_kernel,
        [SM] + [VM] * 4,
        [((rows, chunk + 16, feats), HALF, VM)],
        [place, *got],
        limit=4 * MIB,
    )
    got = col_exchange(packed)
    grad_in = got[:, :chunk].reshape(tokens, feats).astype(FULL)
    vectors = got[:, chunk:].astype(FULL)
    vectors = jnp.sum(vectors[:, :4] + vectors[:, 8:12], 0)
    if two:
        vectors = vectors + swap(vectors, DP, 1)
    else:
        vectors = lax.psum(vectors, DP)

    attn_group = row_gather(attn)
    normed_group = row_exchange(narrow(normed1))
    normed2_group = row_exchange(narrow(normed2))
    hidden_group = row_gather(hidden)
    gate_group = row_gather(d_gate)
    up_group = row_gather(d_up)
    gate_mine = weight_grad(normed2_group, gate_group)
    up_mine = weight_grad(normed2_group, up_group)
    if two:
        other_group = row_gather(swap(hidden, DP, 1))
        (grad_down,) = call(
            down_grad_kernel,
            [SM] + [HB] * 10,
            [((width, feats), FULL, HB)],
            [place, *hidden_group, *other_group, grad_group, swap(grad_group, DP, 1)],
            [
                pltpu.VMEM((8, tokens, width), HALF),
                pltpu.VMEM((width, 8 * tokens), HALF),
                pltpu.VMEM((8 * tokens, feats), HALF),
                pltpu.VMEM((width, feats), FULL),
                pltpu.SemaphoreType.DMA((20,)),
            ],
            flops=16 * tokens * width * feats,
            limit=22 * MIB,
        )
        pairs = [(gate_mine, swap(gate_mine, DP, 1)), (up_mine, swap(up_mine, DP, 1))]
        grad_gateup = total(pairs, (feats, 2, width))
    else:
        grads = [sequence(grad_group, k) for k in range(rows)]
        grad_down = over_groups(weight_grad(hidden_group, grads))
        grad_gateup = jnp.stack([over_groups(gate_mine), over_groups(up_mine)], 1)
    (leaf,) = call(
        leaf_kernel,
        [SM] + [HB] * 10,
        [((rows * tokens, feats), HALF, HB)],
        [place, *attn_group, *hidden_group, w_proj, w_down],
        [
            pltpu.VMEM((head_cols, feats), HALF),
            pltpu.VMEM((width, feats), HALF),
            pltpu.VMEM((4, tokens, head_cols), HALF),
            pltpu.VMEM((4, tokens, width), HALF),
            pltpu.VMEM((4, tokens, feats), HALF),
            pltpu.SemaphoreType.DMA((14,)),
        ],
        flops=2 * rows * tokens * feats * (head_cols + width),
        limit=12 * MIB,
    )
    leaf = col_exchange(leaf.reshape(cols, tokens, feats))
    block_out = block_in.astype(FULL) + jnp.sum(leaf.astype(FULL), 0)
    rounded_group = row_exchange(narrow(rounded))
    proj_mine = weight_grad(attn_group, rounded_group)
    if two:
        proj_other = swap(proj_mine, DP, 1)
        grad_proj = proj_mine.astype(FULL) + proj_other.astype(FULL)
    else:
        grad_proj = over_groups(proj_mine)
    qkv_group = row_gather(d_qkv)
    mine = weight_grad(normed_group, qkv_group, True)
    if two:
        other = swap(mine, DP, 1)
        grad_qkv = total([(mine, other)], (3, feats, head_cols), 0).swapaxes(0, 1)
        both = mine[feats:].astype(FULL) + other[feats:].astype(FULL)
    else:
        both = lax.psum(mine.astype(FULL), DP)
        grad_qkv = both[:feats].reshape(feats, 3, head_cols)
        both = both[feats:]
    grad_bias = (both[0] + both[8]).reshape(3, head_cols) * bias_mask(head_cols)
    gain1_grad, bias1_grad, gain2_grad, bias2_grad = vectors
    return (
        block_out,
        grad_in,
        grad_qkv,
        grad_bias,
        grad_proj,
        gain1_grad,
        bias1_grad,
        gain2_grad,
        bias2_grad,
        grad_gateup,
        grad_down,
    )


def solution(mesh):
    return jax.shard_map(
        block,
        mesh=mesh,
        in_specs=(
            P((DP, COL), ROW),
            P(ROW),
            P(ROW),
            P(ROW, None, COL),
            P(None, COL),
            P(COL, ROW),
            P(ROW),
            P(ROW),
            P(ROW, None, COL),
            P(COL, ROW),
            P((DP, COL), ROW),
        ),
        out_specs=(
            P((DP, COL), ROW),
            P((DP, COL), ROW),
            P(ROW, None, COL),
            P(None, COL),
            P(COL, ROW),
            P(ROW),
            P(ROW),
            P(ROW),
            P(ROW),
            P(ROW, None, COL),
            P(COL, ROW),
        ),
        check_vma=False,
    )
```

```python
import functools
import math

import jax
import jax.numpy as jnp
from jax import lax
from jax.experimental import pallas as pl
from jax.experimental.pallas import tpu as pltpu
from jax.sharding import PartitionSpec as P


HD = 64
ROT = 16
SEQ = 256

EPS = 1e-05
THETA = 10000.0
SCALE = 1.0 / math.sqrt(HD)

HALF = jnp.bfloat16
FULL = jnp.float32
LANES = 128
PAIR = LANES // HD
MIB = 1 << 20


DP, ROW, COL = "dp", "row", "col"


def swap(value, axis, bit):
    size = lax.axis_size(axis)
    return lax.ppermute(value, axis, [(i, i ^ bit) for i in range(size)])


def row_exchange(blocks):
    return [blocks[0]] + [swap(blocks[k], ROW, k) for k in range(1, 4)]


def col_exchange(blocks):
    return lax.all_to_all(blocks, COL, 0, 0, tiled=True)


def col_swaps(blocks):
    there = {j: swap(blocks[j], COL, j) for j in (2, 3, 1)}
    return [blocks[0], there[1], there[2], there[3]]


def row_gather(local):
    across = swap(local, ROW, 2)
    beside = swap(local, ROW, 1)
    both = swap(across, ROW, 1)
    return [local, beside, across, both]


def across(mine):
    first = swap(mine, ROW, 2)
    second = swap(first, DP, 1)
    third = swap(first, ROW, 1)
    return [first, second, third, swap(second, ROW, 1)]


def half_of(weight):
    half = weight.shape[0] // 2
    odd = lax.axis_index(DP) % 2
    return lax.dynamic_slice_in_dim(weight, odd * half, half, 0)


def total(pairs, shape, axis=1, tile=128):
    rows = shape[1 - axis]
    block = (tile, *shape[1:]) if axis == 1 else (shape[0], tile, shape[2])
    parts = [part for pair in pairs for part in pair]
    return pl.pallas_call(
        functools.partial(total_kernel, axis),
        grid=(rows // tile,),
        out_shape=jax.ShapeDtypeStruct(shape, FULL),
        in_specs=[pl.BlockSpec((tile, p.shape[1]), lambda n: (n, 0)) for p in parts],
        out_specs=pl.BlockSpec(block, (lambda n: (n, 0, 0)) if axis == 1 else (lambda n: (0, n, 0))),
        compiler_params=pltpu.CompilerParams(vmem_limit_bytes=10 * MIB),
        cost_estimate=pl.CostEstimate(
            flops=math.prod(shape), bytes_accessed=8 * math.prod(shape), transcendentals=0
        ),
    )(*parts)


def over_groups(mine):
    return lax.psum(mine.astype(FULL), DP)


def places(refs, axis, odd):
    size = refs[0].shape[axis]
    if len(refs) == 4:
        return [(ref, k * size, size) for k, ref in enumerate(refs)]
    half = size // 2
    own, beside, first, second, first_b, second_b = refs
    near = pl.multiple_of(odd * half, LANES)
    far = pl.multiple_of((1 - odd) * half, LANES)
    return [
        (own, 0, size),
        (beside, size, size),
        (first, 2 * size + near, half),
        (second, 2 * size + far, half),
        (first_b, 3 * size + near, half),
        (second_b, 3 * size + far, half),
    ]


def staged(refs, axis, odd, buffer, sems):
    copies, views, at = [], [], 0
    for i, (ref, start, size) in enumerate(places(refs, axis, odd)):
        here = pl.ds(at, size)
        view = buffer.at[here] if axis == 0 else buffer.at[:, here]
        copies.append(pltpu.make_async_copy(ref, view, sems.at[i]))
        views.append((view, start, size))
        at += size
    return copies, views


def lanes(at, size):
    return pl.ds(at if isinstance(at, int) else pl.multiple_of(at, LANES), size)


def added(terms):
    total = None
    for term in terms:
        total = term if total is None else total + term
    return total


def begin(copies):
    for copy in copies:
        copy.start()


def wait(copies):
    for copy in copies:
        copy.wait()


def nn(left, right):
    return lax.dot_general(left, right, (((1,), (0,)), ((), ())), preferred_element_type=FULL)


def nt(left, right):
    return lax.dot_general(left, right, (((1,), (1,)), ((), ())), preferred_element_type=FULL)


def tn(left, right):
    return lax.dot_general(left, right, (((0,), (0,)), ((), ())), preferred_element_type=FULL)


def tiles(extent, size, step):
    whole = extent // size

    def one(n, _):
        step(pl.multiple_of(n * size, size), size)
        return 0

    lax.fori_loop(0, whole, one, 0)
    if extent % size:
        step(whole * size, extent % size)


def turn(value, cos_t, down, up):
    return (
        value * cos_t
        + pltpu.roll(value, LANES - ROT // 2, 1) * down
        + pltpu.roll(value, ROT // 2, 1) * up
    )


def stats(values):
    mean = jnp.mean(values, 1, keepdims=True)
    second = jnp.mean(values * values, 1, keepdims=True)
    return mean, lax.rsqrt(second - mean * mean + EPS)


def causal(length):
    at = lax.broadcasted_iota(jnp.int32, (length, length), 0)
    return at >= lax.broadcasted_iota(jnp.int32, (length, length), 1)


def own_half(value, head):
    lane = lax.broadcasted_iota(jnp.int32, value.shape, 1)
    return jnp.where((lane < HD) == (head == 0), value, jnp.zeros_like(value))


def either(first, second):
    lane = lax.broadcasted_iota(jnp.int32, first.shape, 1)
    return jnp.where(lane < HD, first, second)


def backwards(product, part, outs, rows, odd, sems):
    size = part.shape[1] // 8

    def pieces(n):
        at = lanes(jnp.where(n < 4, n, n ^ odd) * size, size)
        return at, out_pieces(part, outs, rows, at, sems, 4 * n)

    def one(n, _):
        at, copies = pieces(n)
        part[:, at] = product(pl.ds(pl.multiple_of(n * size, size), size)).astype(HALF)
        begin(copies)
        return 0

    lax.fori_loop(0, 8, one, 0, unroll=2)
    for n in range(8):
        wait(pieces(n)[1])


def out_pieces(source, outs, rows, at, sems, first):
    size = outs[0].shape[0]
    return [
        pltpu.make_async_copy(
            source.at[pl.ds(rows[j], size), at], outs[j].at[:, at], sems.at[first + j]
        )
        for j in range(4)
    ]


def chunks(place, rows, apart=True):
    size = rows // 4
    if not apart:
        return [j * size for j in range(4)]
    return [pl.multiple_of((place[2] ^ j) * size, size) for j in range(4)]


def halves_kernel(place, inner, down, gate_h, up_h, down_h, wide, tall, sems):
    size, width = gate_h.shape
    at = pl.ds(pl.multiple_of(place[0] * size, size), size)
    loads = [
        pltpu.make_async_copy(down.at[:, at], tall, sems.at[0]),
        pltpu.make_async_copy(inner.at[at, 0:width], wide.at[0], sems.at[1]),
        pltpu.make_async_copy(inner.at[at, width : 2 * width], wide.at[1], sems.at[2]),
    ]
    stores = [
        pltpu.make_async_copy(tall, down_h, sems.at[3]),
        pltpu.make_async_copy(wide.at[0], gate_h, sems.at[4]),
        pltpu.make_async_copy(wide.at[1], up_h, sems.at[5]),
    ]
    begin(loads)
    for load, store in zip(loads, stores):
        load.wait()
        store.start()
    wait(stores)


def sort_kernel(place, *refs):
    blocks, below = refs[0:4], refs[4:-6]
    outs, every, both, sems = refs[-6:-3], refs[-3], refs[-2], refs[-1]
    apart = place[1] ^ place[2]
    rows = blocks[0].shape[0]
    loads = [
        pltpu.make_async_copy(blocks[j], both.at[apart ^ j, pl.ds(0, rows)], sems.at[j])
        for j in range(4)
    ]
    for ref in below:
        for k in range(4):
            at = pl.ds(rows, ref.shape[0])
            loads.append(pltpu.make_async_copy(ref, both.at[k, at], sems.at[4 + k]))
    begin(loads)
    wait(loads)
    stores = [pltpu.make_async_copy(both.at[k + 1], outs[k], sems.at[8 + k]) for k in range(3)]
    stores.append(pltpu.make_async_copy(both, every, sems.at[11]))
    begin(stores)
    wait(stores)


def attention_kernel(place, *refs):
    x = refs[0:4]
    qkv_w, proj_w = refs[4:10], refs[10:14]
    bias, tables = refs[14:16]
    normed_h, qkv_h, attn_h, lse_h, keep_h = refs[16:21]
    parts_h = refs[21:25]
    normed, raw, xs, w1, w2, qkv, attn, lse, part, keep, sems = refs[25:]
    tokens, wide = normed.shape
    feats = wide // 4
    head_cols = attn.shape[1]
    store = pltpu.make_async_copy(normed, normed_h, sems.at[0])
    x = (x[0].at[0], *x[1:])
    loads = [pltpu.make_async_copy(x[k], xs.at[k], sems.at[1 + k]) for k in range(4)]
    copies, views = staged(qkv_w, 0, place[0], w1, sems.at[pl.ds(5, 6)])
    copies2, views2 = staged(proj_w, 1, place[0], w2, sems.at[pl.ds(11, 4)])
    stores = [
        pltpu.make_async_copy(a, b, sems.at[15 + i])
        for i, (a, b) in enumerate(((qkv, qkv_h), (attn, attn_h), (lse, lse_h)))
    ]
    keeping = pltpu.make_async_copy(keep, keep_h, sems.at[18])
    chunk = keep.shape[0] - 8
    scales = keep.at[pl.ds(chunk, 8)]
    begin(loads + copies[:1])
    wait(loads)
    begin(copies[1:])
    for k in range(4):
        packed = xs[k, tokens : tokens + 16, :].astype(FULL)
        scales[:, k * feats : (k + 1) * feats] = packed[:8] + packed[8:]
    step = 32

    def norm(i, _):
        at = pl.ds(pl.multiple_of(i * step, step), step)
        values = jnp.concatenate([xs[k, at, :].astype(FULL) for k in range(4)], 1)
        mean, inverse = stats(values)
        normed[at, :] = ((values - mean) * inverse * scales[0:1] + scales[1:2]).astype(HALF)
        return 0

    lax.fori_loop(0, tokens // step, norm, 0)
    store.start()
    at = pl.ds(pl.multiple_of(place[2] * chunk, chunk), chunk)
    for k in range(4):
        keep[0:chunk, k * feats : (k + 1) * feats] = xs[k, at, :].astype(FULL)
    keeping.start()
    for i, (view, start, rows) in enumerate(views):
        wait(copies[i : i + 1])

        def product(at, size, i=i, view=view, start=start, rows=rows):
            at = pl.ds(at, size)
            value = nn(normed[:, lanes(start, rows)], view[:, at])
            raw[:, at] = value + (bias[:, at] if i == 0 else raw[:, at])

        tiles(3 * head_cols, 768, product)
    begin(copies2)
    mask = causal(tokens)
    lane = lax.broadcasted_iota(jnp.int32, (tokens, LANES), 1)

    def pair(p, _):
        at = [pl.ds(pl.multiple_of(j * head_cols + p * LANES, LANES), LANES) for j in range(3)]
        query = turn(raw[:, at[0]], tables[0], tables[1], tables[2]).astype(HALF)
        keys = turn(raw[:, at[1]], tables[0], tables[1], tables[2]).astype(HALF)
        values = raw[:, at[2]].astype(HALF)
        qkv[:, at[0]] = query
        qkv[:, at[1]] = keys
        qkv[:, at[2]] = values
        outs = []
        for h in range(PAIR):
            scores = jnp.where(mask, nt(own_half(query, h), keys) * SCALE, -1e30)
            top = jnp.max(scores, 1, keepdims=True)
            raised = jnp.exp(scores - top)
            total = jnp.sum(raised, 1, keepdims=True)
            lse[...] = jnp.where(lane == p * PAIR + h, top + jnp.log(total), lse[...])
            outs.append(nn((raised * (1.0 / total)).astype(HALF), values))
        attn[:, at[0]] = either(*outs).astype(HALF)
        return 0

    lax.fori_loop(0, head_cols // LANES, pair, 0, unroll=2)
    begin(stores)
    wait(copies2)
    outs = []
    for i, (view, start, size) in enumerate(views2):
        part[:, lanes(start, size)] = nn(attn[...], view[...]).astype(HALF)
        pieces = out_pieces(
            part, parts_h, chunks(place, tokens), lanes(start, size), sems, 19 + 4 * i
        )
        begin(pieces)
        outs += pieces
    wait([store, keeping] + stores + outs)


def received(got):
    return added(g[...].astype(FULL) for g in got)


def second_norm_kernel(g0, g1, g2, g3, keep_h, normed_h, resid_h, keep, resid, normed, sems):
    chunk = resid.shape[0]
    load = pltpu.make_async_copy(keep_h, keep, sems.at[0])
    load.start()
    values = received((g0, g1, g2, g3))
    load.wait()
    values = values + keep[0:chunk]
    resid[...] = values
    stores = [
        pltpu.make_async_copy(resid, resid_h, sems.at[1]),
        pltpu.make_async_copy(normed, normed_h, sems.at[2]),
    ]
    stores[0].start()
    mean, inverse = stats(values)
    scales = keep[chunk : chunk + 8]
    normed[...] = ((values - mean) * inverse * scales[2:3] + scales[3:4]).astype(HALF)
    stores[1].start()
    wait(stores)


def down_kernel(place, *refs):
    g, down_w = refs[0:4], refs[4:-7]
    dh_h, own_h, dh, gs, w1, own, sems = refs[-7:]
    feats = g[1].shape[1]
    g = (g[0].at[0], *g[1:])
    loads = [
        pltpu.make_async_copy(g[k], gs.at[:, k * feats : (k + 1) * feats], sems.at[k])
        for k in range(4)
    ]
    copies, views = staged(down_w, 1, place[0], w1, sems.at[pl.ds(4, 6)])
    stores = [
        pltpu.make_async_copy(dh, dh_h, sems.at[10]),
        pltpu.make_async_copy(own, own_h, sems.at[11]),
    ]
    begin(loads + copies[:2])
    wait(loads)
    chunk = own.shape[0]
    own[...] = gs[pl.ds(pl.multiple_of(place[2] * chunk, chunk), chunk), :]
    stores[1].start()
    for i, (view, start, cols) in enumerate(views):
        wait(copies[i : i + 1])
        begin(copies[i + 2 : i + 3])
        value = nt(gs[:, lanes(start, cols)], view[...])
        dh[...] = value if i == 0 else dh[...] + value
    stores[0].start()
    wait(stores)


def mlp_kernel(place, *refs):
    pieces, dh_h = refs[0:4], refs[4]
    hidden_h, gate_h, up_h = refs[15:18]
    parts_h = refs[18:22]
    normed, gate, up, w1, w2, hidden, d_gate, d_up, dh, part, sems = refs[22:]
    tokens, width = hidden.shape
    gate_w = [ref.at[:, 0:width] for ref in refs[5:7]] + list(refs[7:11])
    up_w = [ref.at[:, width : 2 * width] for ref in refs[5:7]] + list(refs[11:15])
    here, there = chunks(place, tokens, False), chunks(place, tokens)
    size = tokens // 4
    stores = [
        pltpu.make_async_copy(d_gate, gate_h, sems.at[0]),
        pltpu.make_async_copy(d_up, up_h, sems.at[1]),
    ]
    loads, loads2 = [], []
    for j in range(4):
        a, b = pl.ds(here[j], size), pl.ds(there[j], size)
        loads.append(pltpu.make_async_copy(pieces[j], normed.at[a], sems.at[48 + j]))
        loads2.append(pltpu.make_async_copy(dh_h.at[b], dh.at[a], sems.at[52 + j]))
        stores.append(pltpu.make_async_copy(hidden.at[a], hidden_h.at[b], sems.at[56 + j]))
    copies, views = staged(gate_w, 0, place[0], w1, sems.at[pl.ds(4, 6)])
    copies2, views2 = staged(up_w, 0, place[0], w2, sems.at[pl.ds(10, 6)])
    copies = copies + copies2
    begin(loads + copies[:2])
    wait(loads)
    begin(copies[2:3])
    for i, (view, start, rows) in enumerate(views + views2):
        wait(copies[i : i + 1])
        begin(copies[i + 3 : i + 4])
        if i == 6:
            begin(loads2)
        acc = gate if i < 6 else up
        value = nn(normed[:, lanes(start, rows)], view[...])
        acc[...] = value if i % 6 == 0 else acc[...] + value
    wait(loads2)

    def act(n, _):
        at = pl.ds(pl.multiple_of(n * LANES, LANES), LANES)
        one, two, grad = gate[:, at], up[:, at], dh[:, at]
        sig = 1.0 / (1.0 + jnp.exp(-one))
        silu = one * sig
        hidden[:, at] = (silu * two).astype(HALF)
        d_gate[:, at] = (grad * two * sig * (1.0 + one * (1.0 - sig))).astype(HALF)
        d_up[:, at] = (grad * silu).astype(HALF)
        return 0

    lax.fori_loop(0, width // LANES, act, 0)
    begin(stores)

    def back(at):
        return nt(d_gate[...], w1[at, :]) + nt(d_up[...], w2[at, :])

    backwards(back, part, parts_h, here, place[0], sems.at[pl.ds(16, 32)])
    wait(stores)


def norm_back(grad_normed, values, gain):
    mean, inverse = stats(values)
    centred = (values - mean) * inverse
    scaled = grad_normed * gain
    total = jnp.mean(scaled, 1, keepdims=True)
    cross = jnp.mean(scaled * centred, 1, keepdims=True)
    back = inverse * (scaled - total - centred * cross)
    return (
        back,
        jnp.sum(grad_normed * centred, 0, keepdims=True),
        jnp.sum(grad_normed, 0, keepdims=True),
    )


def second_back_kernel(g0, g1, g2, g3, resid_h, own_h, keep_h, rounded_h, d_resid_h, resid, own, keep, d_resid, rounded, sems):
    chunk = resid.shape[0]
    loads = [
        pltpu.make_async_copy(a, b, sems.at[i])
        for i, (a, b) in enumerate(((resid_h, resid), (own_h, own), (keep_h, keep)))
    ]
    stores = [
        pltpu.make_async_copy(rounded, rounded_h, sems.at[3]),
        pltpu.make_async_copy(d_resid, d_resid_h, sems.at[4]),
    ]
    begin(loads)
    grad = received((g0, g1, g2, g3))
    wait(loads)
    back, gain, shift = norm_back(grad, resid[...], keep[chunk + 2 : chunk + 3])
    total = own[...].astype(FULL) + back
    rounded[...] = total.astype(HALF)
    stores[0].start()
    d_resid[0:chunk] = total
    row = lax.broadcasted_iota(jnp.int32, (8, gain.shape[1]), 0)
    d_resid[chunk : chunk + 8] = jnp.where(row == 2, gain, jnp.where(row == 3, shift, 0.0))
    stores[1].start()
    wait(stores)


def attention_back_kernel(place, *refs):
    pieces, (qkv_h, attn_h, lse_h, tables_h) = refs[0:4], refs[4:8]
    qkv_w, proj_w = refs[8:14], refs[14:18]
    d_qkv_h, parts_h = refs[18], refs[19:23]
    rounded, d_attn, d_qkv, w1, w2, qkv, attn, lse, tables, part, sems = refs[23:]
    tokens = rounded.shape[0]
    rows = chunks(place, tokens)
    loads0 = [
        pltpu.make_async_copy(pieces[j], rounded.at[pl.ds(rows[j], tokens // 4)], sems.at[47 + j])
        for j in range(4)
    ]
    head_cols = attn.shape[1]
    store = pltpu.make_async_copy(d_qkv, d_qkv_h, sems.at[0])
    copies2, views2 = staged(proj_w, 1, place[0], w2, sems.at[pl.ds(1, 4)])
    copies, _ = staged(qkv_w, 0, place[0], w1, sems.at[pl.ds(5, 6)])
    loads = [
        pltpu.make_async_copy(a, b, sems.at[11 + i])
        for i, (a, b) in enumerate(
            ((qkv_h, qkv), (attn_h, attn), (lse_h, lse), (tables_h, tables))
        )
    ]
    begin(loads0 + copies2 + loads)
    wait(loads0 + copies2)
    begin(copies)
    d_attn[...] = added(
        nt(rounded[:, lanes(start, size)], view[...]) for view, start, size in views2
    ).astype(HALF)
    wait(loads)
    mask = causal(tokens)
    lane = lax.broadcasted_iota(jnp.int32, (tokens, LANES), 1)

    def pair(p, _):
        at = [pl.ds(pl.multiple_of(j * head_cols + p * LANES, LANES), LANES) for j in range(3)]
        query, keys, values = [qkv[:, a] for a in at]
        grad = d_attn[:, at[0]]
        product = grad.astype(FULL) * attn[:, at[0]].astype(FULL)
        dq, dk, dv = [], [], []
        for h in range(PAIR):
            delta = jnp.sum(own_half(product, h), 1, keepdims=True)
            total = jnp.sum(jnp.where(lane == p * PAIR + h, lse[...], 0.0), 1, keepdims=True)
            scores = jnp.where(mask, nt(own_half(query, h), keys) * SCALE, -1e30)
            weights = jnp.exp(scores - total)
            d_probs = nt(own_half(grad, h), values)
            d_scores = (weights * (d_probs - delta)).astype(HALF)
            dq.append(nn(d_scores, keys))
            dk.append(tn(d_scores, query))
            dv.append(tn(weights.astype(HALF), grad))
        dq = either(*dq) * SCALE
        dk = either(*dk) * SCALE
        d_qkv[:, at[0]] = turn(dq, tables[0], -tables[1], -tables[2]).astype(HALF)
        d_qkv[:, at[1]] = turn(dk, tables[0], -tables[1], -tables[2]).astype(HALF)
        d_qkv[:, at[2]] = either(*dv).astype(HALF)
        return 0

    lax.fori_loop(0, head_cols // LANES, pair, 0, unroll=2)
    store.start()
    wait(copies)
    backwards(
        lambda at: nt(d_qkv[...], w1[at, :]), part, parts_h, rows, place[0], sems.at[pl.ds(15, 32)]
    )
    store.wait()


def split_low(value, out, at):
    high = value.astype(HALF)
    out[at : at + 8, :] = high
    out[at + 8 : at + 16, :] = (value - high.astype(FULL)).astype(HALF)


def first_back_kernel(g0, g1, g2, g3, d_resid_h, keep_h, out, d_resid, keep, sems):
    chunk = out.shape[0] - 16
    loads = [
        pltpu.make_async_copy(d_resid_h, d_resid, sems.at[0]),
        pltpu.make_async_copy(keep_h, keep, sems.at[1]),
    ]
    begin(loads)
    grad = received((g0, g1, g2, g3))
    wait(loads)
    back, gain, shift = norm_back(grad, keep[0:chunk], keep[chunk : chunk + 1])
    out[0:chunk, :] = (d_resid[0:chunk] + back).astype(HALF)
    sums = d_resid[chunk : chunk + 8]
    row = lax.broadcasted_iota(jnp.int32, sums.shape, 0)
    split_low(jnp.where(row == 0, gain, jnp.where(row == 1, shift, sums)), out, chunk)


def pack_kernel(place, g0, g1, g2, g3, out):
    blocks = (g0, g1, g2, g3)
    chunk = g0.shape[0] - 16
    total = added(
        g[chunk : chunk + 8, :].astype(FULL) + g[chunk + 8 : chunk + 16, :].astype(FULL)
        for g in blocks
    )
    for k, g in enumerate(blocks):
        at = place[1] ^ k
        out[at, 0:chunk, :] = g[0:chunk, :]
        split_low(total, out.at[at], chunk)


def down_grad_kernel(place, *refs):
    hidden, groups, out_h = refs[0:8], refs[8:10], refs[10]
    left, turned, right, out, sems = refs[11:]
    rows, width = hidden[0].shape
    bases = (place[0] * 4, 4 - place[0] * 4)
    loads = [pltpu.make_async_copy(hidden[n], left.at[n], sems.at[n]) for n in range(8)]
    loads2 = [
        pltpu.make_async_copy(
            groups[n // 4].at[n % 4],
            right.at[pl.ds(pl.multiple_of((bases[n // 4] + n % 4) * rows, rows), rows)],
            sems.at[8 + n],
        )
        for n in range(8)
    ]
    begin(loads[:4])
    for n in range(8):
        wait(loads[n : n + 1])
        begin(loads[n + 4 : n + 5])
        begin(loads2[n : n + 1])
        at = pl.ds(pl.multiple_of((bases[n // 4] + n % 4) * rows, rows), rows)
        turned[:, at] = left[n].T
    wait(loads2)
    size = width // 4
    stores = []
    for n in range(4):
        at = pl.ds(n * size, size)
        out[at, :] = nn(turned[at, :], right[...])
        stores.append(pltpu.make_async_copy(out.at[at], out_h.at[at], sems.at[16 + n]))
        stores[n].start()
    wait(stores)


def weight_grad_kernel(ones, tile, mixed, place, *refs):
    lefts, rights, out_h = refs[0:4], refs[4:8], refs[8]
    left, turned, right, out, sems = refs[9:]
    rows, width = lefts[0].shape
    cols = right.shape[1]
    size = rows // 4
    loads = []
    for k in range(4):
        if mixed:
            here, there = chunks(place, rows, False), chunks(place, rows)
            loads.append(
                [
                    pltpu.make_async_copy(
                        lefts[k].at[pl.ds(there[j], size)],
                        left.at[k, pl.ds(here[j], size)],
                        sems.at[k, j],
                    )
                    for j in range(4)
                ]
            )
        else:
            loads.append([pltpu.make_async_copy(lefts[k], left.at[k], sems.at[k, 0])])
    loads2 = [
        pltpu.make_async_copy(rights[k], right.at[pl.ds(k * rows, rows)], sems.at[4, k])
        for k in range(4)
    ]
    for copies in loads:
        begin(copies)
    begin(loads2)
    for k in range(4):
        wait(loads[k])
        turned[:, k * rows : (k + 1) * rows] = left[k].T
    wait(loads2)

    def store(at, size, n):
        return pltpu.make_async_copy(
            out.at[:, pl.ds(at, size)], out_h.at[:, pl.ds(at, size)], sems.at[5, n]
        )

    def product(at, size):
        n = at // tile
        at = pl.ds(at, size)
        out[0:width, at] = nn(turned[...], right[:, at]).astype(HALF)
        if ones:
            total = jnp.sum(right[:, at].astype(FULL), 0, keepdims=True)
            high = total.astype(HALF).astype(FULL)
            row = lax.broadcasted_iota(jnp.int32, (16, size), 0)
            out[width : width + 16, at] = jnp.where(row < 8, high, total - high).astype(HALF)
        store(at.start, size, n).start()

    tiles(cols, tile, product)
    for at in range(0, cols, tile):
        store(at, min(tile, cols - at), at // tile).wait()


def total_kernel(axis, *refs):
    out = refs[-1]
    width = out.shape[2]
    j = 0
    for mine, other in zip(refs[0:-1:2], refs[1:-1:2]):
        for n in range(mine.shape[1] // width):
            at = slice(n * width, (n + 1) * width)
            value = mine[:, at].astype(FULL) + other[:, at].astype(FULL)
            if axis == 1:
                out[:, j, :] = value
            else:
                out[j] = value
            j += 1


def leaf_kernel(place, *refs):
    attn, hidden = refs[0:4], refs[4:8]
    proj_h, down_h = refs[8:10]
    outs = refs[10:14]
    w1, w2, left, left2, out, sems = refs[14:]
    apart = place[1] ^ place[2]
    loads = [
        pltpu.make_async_copy(proj_h, w1, sems.at[0]),
        pltpu.make_async_copy(down_h, w2, sems.at[1]),
    ]
    for k in range(4):
        loads.append(pltpu.make_async_copy(attn[k], left.at[apart ^ k], sems.at[2 + 2 * k]))
        loads.append(pltpu.make_async_copy(hidden[k], left2.at[apart ^ k], sems.at[3 + 2 * k]))
    begin(loads)
    wait(loads)
    stores = [pltpu.make_async_copy(out.at[k], outs[k], sems.at[10 + k]) for k in range(4)]
    for k in range(4):
        out[k] = (nn(left[k], w1[...]) + nn(left2[k], w2[...])).astype(HALF)
        stores[k].start()
    wait(stores)


VM = pl.BlockSpec(memory_space=pltpu.VMEM)
SM = pl.BlockSpec(memory_space=pltpu.SMEM)
HB = pl.BlockSpec(memory_space=pltpu.HBM)
AN = pl.BlockSpec(memory_space=pl.ANY)


def call(kernel, specs, outs, args, scratch=(), flops=0, limit=None):
    moved = sum(a.size * a.dtype.itemsize for a in args)
    moved += sum(math.prod(s) * jnp.dtype(t).itemsize for s, t, _ in outs)
    return pl.pallas_call(
        kernel,
        out_shape=[pltpu.HBM(s, t) if m is HB else jax.ShapeDtypeStruct(s, t) for s, t, m in outs],
        in_specs=specs,
        out_specs=[m for _, _, m in outs],
        scratch_shapes=list(scratch),
        compiler_params=pltpu.CompilerParams(vmem_limit_bytes=limit),
        cost_estimate=pl.CostEstimate(flops=flops, bytes_accessed=moved, transcendentals=0),
    )(*[
        pltpu.with_memory_space_constraint(a, pltpu.HBM) if m is HB else a
        for a, m in zip(args, specs, strict=True)
    ])


def weight_grad(place, lefts, rights, ones=False, tile=512, mixed=False):
    rows, width = lefts[0].shape
    cols = rights[0].shape[1]
    high = width + (16 if ones else 0)
    size = 2 * (8 * rows * width + 4 * rows * cols + high * cols)
    (out,) = call(
        functools.partial(weight_grad_kernel, ones, tile, mixed),
        [SM] + [HB] * 8,
        [((high, cols), HALF, HB)],
        [place, *lefts, *rights],
        [
            pltpu.VMEM((4, rows, width), HALF),
            pltpu.VMEM((width, 4 * rows), HALF),
            pltpu.VMEM((4 * rows, cols), HALF),
            pltpu.VMEM((high, cols), HALF),
            pltpu.SemaphoreType.DMA((6, 4)),
        ],
        flops=8 * rows * width * cols,
        limit=size + 4 * MIB,
    )
    return out


def rotation_tables(length):
    half = ROT // 2
    lane = jnp.arange(LANES) % HD
    freqs = THETA ** (-2.0 * (lane % half).astype(FULL) / ROT)
    angles = jnp.arange(length, dtype=FULL)[:, None] * freqs[None, :]
    cos_t = jnp.where(lane < ROT, jnp.cos(angles), 1.0)
    sin_t = jnp.sin(angles)
    down = jnp.where(lane < half, -sin_t, 0.0)
    up = jnp.where((lane >= half) & (lane < ROT), sin_t, 0.0)
    return jnp.stack([cos_t, down, up])


def bias_mask(width):
    lanes = jnp.arange(width) % HD < ROT
    ones = jnp.ones((width,), FULL)
    return jnp.stack([ones, jnp.where(lanes, 1.0, 0.0).astype(FULL), ones])


def block(
    block_in,
    norm1_gain,
    norm1_bias,
    w_qkv,
    qkv_bias,
    w_proj,
    norm2_gain,
    norm2_bias,
    w_gateup,
    w_down,
    out_grad,
):
    rows = lax.axis_size(ROW)
    cols = lax.axis_size(COL)
    col = lax.axis_index(COL)
    row = lax.axis_index(ROW)
    odd = lax.axis_index(DP) % 2
    two = lax.axis_size(DP) == 2
    feats = w_qkv.shape[0]
    head_cols = w_qkv.shape[2]
    width = w_gateup.shape[2]
    tokens = block_in.shape[0]
    chunk = tokens // cols
    wide = rows * feats
    place = jnp.stack([odd, row, col, odd]).astype(jnp.int32)
    tables = rotation_tables(SEQ)

    def narrow(value):
        return [value[:, k * feats : (k + 1) * feats] for k in range(rows)]

    own_qkv = w_qkv.reshape(feats, 3 * head_cols)
    own_inner = w_gateup.reshape(feats, 2 * width)
    in_group = col_swaps([block_in] * 4)
    qkv_w = [own_qkv, swap(own_qkv, ROW, 1), *across(half_of(own_qkv))]
    proj_w = row_gather(w_proj)
    beside = swap(own_inner, ROW, 1)
    inner_w = [own_inner, beside]
    gate_half, up_half, down_half = call(
        halves_kernel,
        [SM, HB, HB],
        [((feats // 2, width), HALF, HB)] * 2 + [((width, feats // 2), HALF, HB)],
        [place, own_inner, w_down],
        [
            pltpu.VMEM((2, feats // 2, width), HALF),
            pltpu.VMEM((width, feats // 2), HALF),
            pltpu.SemaphoreType.DMA((6,)),
        ],
        limit=4 * MIB,
    )
    down_w = [w_down, swap(w_down, ROW, 1), *across(down_half)]
    inner_w += across(gate_half) + across(up_half)
    scales = jnp.concatenate(
        [jnp.stack([norm1_gain, norm1_bias, norm2_gain, norm2_bias]), jnp.zeros((4, feats), FULL)], 0
    )
    high = lax.reduce_precision(scales, 8, 7)
    packed = jnp.concatenate([high.astype(HALF), (scales - high).astype(HALF)], 0)

    def sort(blocks, below):
        high = tokens + sum(b.shape[0] for b in below)
        *outs, every = call(
            sort_kernel,
            [SM] + [HB] * (4 + len(below)),
            [((high, feats), HALF, HB)] * 3 + [((rows, high, feats), HALF, HB)],
            [place, *blocks, *below],
            [pltpu.VMEM((rows, high, feats), HALF), pltpu.SemaphoreType.DMA((12,))],
            limit=4 * MIB,
        )
        return outs, every

    outs, x_own = sort(in_group, [packed])
    x = [x_own] + row_exchange([x_own] + outs)[1:]
    outs, grad_group = sort(col_swaps([out_grad] * 4), [])
    grad_seq = [grad_group] + row_exchange([grad_group] + outs)[1:]

    normed1, qkv, attn, lse, keep, *parts = call(
        attention_kernel,
        [SM] + [HB] * 9 + [AN] + [HB] * 4 + [VM] * 2,
        [
            ((tokens, wide), HALF, HB),
            ((tokens, 3 * head_cols), HALF, HB),
            ((tokens, head_cols), HALF, HB),
            ((tokens, LANES), FULL, HB),
            ((chunk + 8, wide), FULL, HB),
            *[((chunk, wide), HALF, HB)] * 4,
        ],
        [place, *x, *qkv_w, *proj_w, qkv_bias.reshape(1, 3 * head_cols), tables],
        [
            pltpu.VMEM((tokens, wide), HALF),
            pltpu.VMEM((tokens, 3 * head_cols), FULL),
            pltpu.VMEM((4, tokens + 16, feats), HALF),
            pltpu.VMEM((wide, 3 * head_cols), HALF),
            pltpu.VMEM((head_cols, wide), HALF),
            pltpu.VMEM((tokens, 3 * head_cols), HALF),
            pltpu.VMEM((tokens, head_cols), HALF),
            pltpu.VMEM((tokens, LANES), FULL),
            pltpu.VMEM((tokens, wide), HALF),
            pltpu.VMEM((chunk + 8, wide), FULL),
            pltpu.SemaphoreType.DMA((35,)),
        ],
        flops=2 * tokens * wide * 4 * head_cols,
        limit=20 * MIB,
    )
    normed2, resid = call(
        second_norm_kernel,
        [VM] * 4 + [HB],
        [((chunk, wide), HALF, HB), ((chunk, wide), FULL, HB)],
        [*col_swaps(parts), keep],
        [
            pltpu.VMEM((chunk + 8, wide), FULL),
            pltpu.VMEM((chunk, wide), FULL),
            pltpu.VMEM((chunk, wide), HALF),
            pltpu.SemaphoreType.DMA((3,)),
        ],
        limit=8 * MIB,
    )
    normed2 = col_swaps([normed2] * 4)
    d_hidden, own_grad = call(
        down_kernel,
        [SM] + [HB] * (4 + len(down_w)),
        [((tokens, width), FULL, HB), ((chunk, wide), HALF, HB)],
        [place, *grad_seq, *down_w],
        [
            pltpu.VMEM((tokens, width), FULL),
            pltpu.VMEM((tokens, wide), HALF),
            pltpu.VMEM((width, wide), HALF),
            pltpu.VMEM((chunk, wide), HALF),
            pltpu.SemaphoreType.DMA((12,)),
        ],
        flops=2 * tokens * wide * width,
        limit=12 * MIB,
    )
    hidden, d_gate, d_up, *parts = call(
        mlp_kernel,
        [SM] + [HB] * 14 + [AN],
        [
            ((tokens, width), HALF, HB),
            ((tokens, width), HALF, HB),
            ((tokens, width), HALF, HB),
            *[((chunk, wide), HALF, HB)] * 4,
        ],
        [place, *normed2, d_hidden, *inner_w],
        [
            pltpu.VMEM((tokens, wide), HALF),
            pltpu.VMEM((tokens, width), FULL),
            pltpu.VMEM((tokens, width), FULL),
            pltpu.VMEM((wide, width), HALF),
            pltpu.VMEM((wide, width), HALF),
            pltpu.VMEM((tokens, width), HALF),
            pltpu.VMEM((tokens, width), HALF),
            pltpu.VMEM((tokens, width), HALF),
            pltpu.VMEM((tokens, width), FULL),
            pltpu.VMEM((tokens, wide), HALF),
            pltpu.SemaphoreType.DMA((60,)),
        ],
        flops=2 * tokens * wide * 4 * width,
        limit=28 * MIB,
    )
    rounded, d_resid = call(
        second_back_kernel,
        [VM] * 4 + [HB] * 3,
        [((chunk, wide), HALF, HB), ((chunk + 8, wide), FULL, HB)],
        [*col_swaps(parts), resid, own_grad, keep],
        [
            pltpu.VMEM((chunk, wide), FULL),
            pltpu.VMEM((chunk, wide), HALF),
            pltpu.VMEM((chunk + 8, wide), FULL),
            pltpu.VMEM((chunk + 8, wide), FULL),
            pltpu.VMEM((chunk, wide), HALF),
            pltpu.SemaphoreType.DMA((5,)),
        ],
        limit=8 * MIB,
    )
    rounded = col_swaps([rounded] * 4)
    d_qkv, *parts = call(
        attention_back_kernel,
        [SM] + [HB] * 18,
        [((tokens, 3 * head_cols), HALF, HB), *[((chunk, wide), HALF, HB)] * 4],
        [place, *rounded, qkv, attn, lse, tables, *qkv_w, *proj_w],
        [
            pltpu.VMEM((tokens, wide), HALF),
            pltpu.VMEM((tokens, head_cols), HALF),
            pltpu.VMEM((tokens, 3 * head_cols), HALF),
            pltpu.VMEM((wide, 3 * head_cols), HALF),
            pltpu.VMEM((head_cols, wide), HALF),
            pltpu.VMEM((tokens, 3 * head_cols), HALF),
            pltpu.VMEM((tokens, head_cols), HALF),
            pltpu.VMEM((tokens, LANES), FULL),
            pltpu.VMEM((3, tokens, LANES), FULL),
            pltpu.VMEM((tokens, wide), HALF),
            pltpu.SemaphoreType.DMA((51,)),
        ],
        flops=2 * tokens * wide * 5 * head_cols,
        limit=18 * MIB,
    )
    (last,) = call(
        first_back_kernel,
        [VM] * 4 + [HB] * 2,
        [((chunk + 16, wide), HALF, VM)],
        [*col_swaps(parts), d_resid, keep],
        [
            pltpu.VMEM((chunk + 8, wide), FULL),
            pltpu.VMEM((chunk + 8, wide), FULL),
            pltpu.SemaphoreType.DMA((2,)),
        ],
        limit=8 * MIB,
    )

    got = row_exchange(narrow(last))
    (packed,) = call(
        pack_kernel,
        [SM] + [VM] * 4,
        [((rows, chunk + 16, feats), HALF, VM)],
        [place, *got],
        limit=4 * MIB,
    )
    got = col_exchange(packed)
    grad_in = got[:, :chunk].reshape(tokens, feats).astype(FULL)
    vectors = got[:, chunk:].astype(FULL)
    vectors = jnp.sum(vectors[:, :4] + vectors[:, 8:12], 0)
    if two:
        vectors = vectors + swap(vectors, DP, 1)
    else:
        vectors = lax.psum(vectors, DP)

    attn_group = row_gather(attn)
    normed_group = row_exchange(narrow(normed1))

    def blocks_of(pieces):
        return [jnp.concatenate(b, 0) for b in zip(*[narrow(p) for p in pieces])]

    normed2_group = row_exchange(blocks_of(normed2))
    hidden_group = row_gather(hidden)
    gate_group = row_gather(d_gate)
    up_group = row_gather(d_up)
    gate_mine = weight_grad(place, normed2_group, gate_group)
    up_mine = weight_grad(place, normed2_group, up_group)
    if two:
        other_group = row_gather(swap(hidden, DP, 1))
        (grad_down,) = call(
            down_grad_kernel,
            [SM] + [HB] * 10,
            [((width, feats), FULL, HB)],
            [place, *hidden_group, *other_group, grad_group, swap(grad_group, DP, 1)],
            [
                pltpu.VMEM((8, tokens, width), HALF),
                pltpu.VMEM((width, 8 * tokens), HALF),
                pltpu.VMEM((8 * tokens, feats), HALF),
                pltpu.VMEM((width, feats), FULL),
                pltpu.SemaphoreType.DMA((20,)),
            ],
            flops=16 * tokens * width * feats,
            limit=22 * MIB,
        )
        pairs = [(gate_mine, swap(gate_mine, DP, 1)), (up_mine, swap(up_mine, DP, 1))]
        grad_gateup = total(pairs, (feats, 2, width))
    else:
        grads = [grad_group[k] for k in range(rows)]
        grad_down = over_groups(weight_grad(place, hidden_group, grads))
        grad_gateup = jnp.stack([over_groups(gate_mine), over_groups(up_mine)], 1)
    leaf = call(
        leaf_kernel,
        [SM] + [HB] * 10,
        [((tokens, feats), HALF, HB)] * 4,
        [place, *attn_group, *hidden_group, w_proj, w_down],
        [
            pltpu.VMEM((head_cols, feats), HALF),
            pltpu.VMEM((width, feats), HALF),
            pltpu.VMEM((4, tokens, head_cols), HALF),
            pltpu.VMEM((4, tokens, width), HALF),
            pltpu.VMEM((4, tokens, feats), HALF),
            pltpu.SemaphoreType.DMA((14,)),
        ],
        flops=2 * rows * tokens * feats * (head_cols + width),
        limit=12 * MIB,
    )
    leaf = [leaf[0], swap(leaf[1], COL, 1), swap(leaf[2], COL, 2), swap(leaf[3], COL, 3)]
    block_out = block_in.astype(FULL) + sum(part.astype(FULL) for part in leaf)
    rounded_group = row_exchange(blocks_of(rounded))
    proj_mine = weight_grad(place, attn_group, rounded_group, mixed=True)
    if two:
        proj_other = swap(proj_mine, DP, 1)
        grad_proj = proj_mine.astype(FULL) + proj_other.astype(FULL)
    else:
        grad_proj = over_groups(proj_mine)
    qkv_group = row_gather(d_qkv)
    mine = weight_grad(place, normed_group, qkv_group, True)
    if two:
        other = swap(mine, DP, 1)
        grad_qkv = total([(mine, other)], (3, feats, head_cols), 0).swapaxes(0, 1)
        both = mine[feats:].astype(FULL) + other[feats:].astype(FULL)
    else:
        both = lax.psum(mine.astype(FULL), DP)
        grad_qkv = both[:feats].reshape(feats, 3, head_cols)
        both = both[feats:]
    grad_bias = (both[0] + both[8]).reshape(3, head_cols) * bias_mask(head_cols)
    gain1_grad, bias1_grad, gain2_grad, bias2_grad = vectors
    return (
        block_out,
        grad_in,
        grad_qkv,
        grad_bias,
        grad_proj,
        gain1_grad,
        bias1_grad,
        gain2_grad,
        bias2_grad,
        grad_gateup,
        grad_down,
    )


def solution(mesh):
    return jax.shard_map(
        block,
        mesh=mesh,
        in_specs=(
            P((DP, COL), ROW),
            P(ROW),
            P(ROW),
            P(ROW, None, COL),
            P(None, COL),
            P(COL, ROW),
            P(ROW),
            P(ROW),
            P(ROW, None, COL),
            P(COL, ROW),
            P((DP, COL), ROW),
        ),
        out_specs=(
            P((DP, COL), ROW),
            P((DP, COL), ROW),
            P(ROW, None, COL),
            P(None, COL),
            P(COL, ROW),
            P(ROW),
            P(ROW),
            P(ROW),
            P(ROW),
            P(ROW, None, COL),
            P(COL, ROW),
        ),
        check_vma=False,
    )
```

```python
import functools
import math

import jax
import jax.numpy as jnp
from jax import lax
from jax.experimental import pallas as pl
from jax.experimental.pallas import tpu as pltpu
from jax.sharding import PartitionSpec as P


HD = 64
ROT = 16
SEQ = 256

EPS = 1e-05
THETA = 10000.0
SCALE = 1.0 / math.sqrt(HD)

HALF = jnp.bfloat16
FULL = jnp.float32
LANES = 128
PAIR = LANES // HD
MIB = 1 << 20


DP, ROW, COL = "dp", "row", "col"


def swap(value, axis, bit):
    size = lax.axis_size(axis)
    return lax.ppermute(value, axis, [(i, i ^ bit) for i in range(size)])


def row_exchange(blocks):
    return [blocks[0]] + [swap(blocks[k], ROW, k) for k in range(1, 4)]


def col_exchange(blocks):
    return lax.all_to_all(blocks, COL, 0, 0, tiled=True)


def col_swaps(blocks):
    there = {j: swap(blocks[j], COL, j) for j in (2, 3, 1)}
    return [blocks[0], there[1], there[2], there[3]]


def row_gather(local):
    across = swap(local, ROW, 2)
    beside = swap(local, ROW, 1)
    both = swap(across, ROW, 1)
    return [local, beside, across, both]


def across(mine):
    first = swap(mine, ROW, 2)
    second = swap(first, DP, 1)
    third = swap(first, ROW, 1)
    return [first, second, third, swap(second, ROW, 1)]


def half_of(weight):
    half = weight.shape[0] // 2
    odd = lax.axis_index(DP) % 2
    return lax.dynamic_slice_in_dim(weight, odd * half, half, 0)


def total(pairs, shape, axis=1, tile=128):
    rows = shape[1 - axis]
    block = (tile, *shape[1:]) if axis == 1 else (shape[0], tile, shape[2])
    parts = [part for pair in pairs for part in pair]
    return pl.pallas_call(
        functools.partial(total_kernel, axis),
        grid=(rows // tile,),
        out_shape=jax.ShapeDtypeStruct(shape, FULL),
        in_specs=[pl.BlockSpec((tile, p.shape[1]), lambda n: (n, 0)) for p in parts],
        out_specs=pl.BlockSpec(block, (lambda n: (n, 0, 0)) if axis == 1 else (lambda n: (0, n, 0))),
        compiler_params=pltpu.CompilerParams(vmem_limit_bytes=10 * MIB),
        cost_estimate=pl.CostEstimate(
            flops=math.prod(shape), bytes_accessed=8 * math.prod(shape), transcendentals=0
        ),
    )(*parts)


def over_groups(mine):
    return lax.psum(mine.astype(FULL), DP)


def places(refs, axis, odd):
    size = refs[0].shape[axis]
    if len(refs) == 4:
        return [(ref, k * size, size) for k, ref in enumerate(refs)]
    half = size // 2
    own, beside, first, second, first_b, second_b = refs
    near = pl.multiple_of(odd * half, LANES)
    far = pl.multiple_of((1 - odd) * half, LANES)
    return [
        (own, 0, size),
        (beside, size, size),
        (first, 2 * size + near, half),
        (second, 2 * size + far, half),
        (first_b, 3 * size + near, half),
        (second_b, 3 * size + far, half),
    ]


def staged(refs, axis, odd, buffer, sems):
    copies, views, at = [], [], 0
    for i, (ref, start, size) in enumerate(places(refs, axis, odd)):
        here = pl.ds(at, size)
        view = buffer.at[here] if axis == 0 else buffer.at[:, here]
        copies.append(pltpu.make_async_copy(ref, view, sems.at[i]))
        views.append((view, start, size))
        at += size
    return copies, views


def staged_halves(refs, odd, first, second, sems, at):
    middle = first.shape[1]
    copies, views = [], []
    for n, buffer in enumerate((first, second)):
        cols = slice(n * middle, (n + 1) * middle)
        parts = [ref.at[:, cols] for ref in refs[0:2]] + list(refs[2 + 4 * n : 6 + 4 * n])
        more, views2 = staged(parts, 0, odd, buffer, sems.at[pl.ds(at + 6 * n, 6)])
        copies += more
        views += views2
    return copies, views, middle


def lanes(at, size):
    return pl.ds(at if isinstance(at, int) else pl.multiple_of(at, LANES), size)


def added(terms):
    total = None
    for term in terms:
        total = term if total is None else total + term
    return total


def begin(copies):
    for copy in copies:
        copy.start()


def wait(copies):
    for copy in copies:
        copy.wait()


def nn(left, right):
    return lax.dot_general(left, right, (((1,), (0,)), ((), ())), preferred_element_type=FULL)


def nt(left, right):
    return lax.dot_general(left, right, (((1,), (1,)), ((), ())), preferred_element_type=FULL)


def tn(left, right):
    return lax.dot_general(left, right, (((0,), (0,)), ((), ())), preferred_element_type=FULL)


def tiles(extent, size, step):
    whole = extent // size

    def one(n, _):
        step(pl.multiple_of(n * size, size), size)
        return 0

    lax.fori_loop(0, whole, one, 0)
    if extent % size:
        step(whole * size, extent % size)


def turn(value, cos_t, down, up):
    return (
        value * cos_t
        + pltpu.roll(value, LANES - ROT // 2, 1) * down
        + pltpu.roll(value, ROT // 2, 1) * up
    )


def stats(values):
    mean = jnp.mean(values, 1, keepdims=True)
    second = jnp.mean(values * values, 1, keepdims=True)
    return mean, lax.rsqrt(second - mean * mean + EPS)


def causal(length):
    at = lax.broadcasted_iota(jnp.int32, (length, length), 0)
    return at >= lax.broadcasted_iota(jnp.int32, (length, length), 1)


def own_half(value, head):
    lane = lax.broadcasted_iota(jnp.int32, value.shape, 1)
    return jnp.where((lane < HD) == (head == 0), value, jnp.zeros_like(value))


def either(first, second):
    lane = lax.broadcasted_iota(jnp.int32, first.shape, 1)
    return jnp.where(lane < HD, first, second)


def backwards(product, part, outs, rows, odd, sems):
    size = part.shape[1] // 8

    def pieces(n):
        at = lanes(jnp.where(n < 4, n, n ^ odd) * size, size)
        return at, out_pieces(part, outs, rows, at, sems, 4 * n)

    def one(n, _):
        at, copies = pieces(n)
        part[:, at] = product(pl.ds(pl.multiple_of(n * size, size), size)).astype(HALF)
        begin(copies)
        return 0

    lax.fori_loop(0, 8, one, 0, unroll=2)
    for n in range(8):
        wait(pieces(n)[1])


def out_pieces(source, outs, rows, at, sems, first):
    size = outs[0].shape[0]
    return [
        pltpu.make_async_copy(
            source.at[pl.ds(rows[j], size), at], outs[j].at[:, at], sems.at[first + j]
        )
        for j in range(4)
    ]


def chunks(place, rows, apart=True):
    size = rows // 4
    if not apart:
        return [j * size for j in range(4)]
    return [pl.multiple_of((place[2] ^ j) * size, size) for j in range(4)]


def halves_kernel(place, inner, down, gate_h, up_h, down_h, wide, tall, sems):
    size, width = gate_h.shape
    at = pl.ds(pl.multiple_of(place[0] * size, size), size)
    loads = [
        pltpu.make_async_copy(down.at[:, at], tall, sems.at[0]),
        pltpu.make_async_copy(inner.at[at, 0:width], wide.at[0], sems.at[1]),
        pltpu.make_async_copy(inner.at[at, width : 2 * width], wide.at[1], sems.at[2]),
    ]
    stores = [
        pltpu.make_async_copy(tall, down_h, sems.at[3]),
        pltpu.make_async_copy(wide.at[0], gate_h, sems.at[4]),
        pltpu.make_async_copy(wide.at[1], up_h, sems.at[5]),
    ]
    begin(loads)
    for load, store in zip(loads, stores):
        load.wait()
        store.start()
    wait(stores)


def sort_kernel(place, *refs):
    blocks, below = refs[0:4], refs[4:-6]
    outs, every, both, sems = refs[-6:-3], refs[-3], refs[-2], refs[-1]
    apart = place[1] ^ place[2]
    rows = blocks[0].shape[0]
    loads = [
        pltpu.make_async_copy(blocks[j], both.at[apart ^ j, pl.ds(0, rows)], sems.at[j])
        for j in range(4)
    ]
    for ref in below:
        for k in range(4):
            at = pl.ds(rows, ref.shape[0])
            loads.append(pltpu.make_async_copy(ref, both.at[k, at], sems.at[4 + k]))
    begin(loads)
    wait(loads)
    stores = [pltpu.make_async_copy(both.at[k + 1], outs[k], sems.at[8 + k]) for k in range(3)]
    stores.append(pltpu.make_async_copy(both, every, sems.at[11]))
    begin(stores)
    wait(stores)


def attention_kernel(place, *refs):
    x = refs[0:4]
    qkv_w, proj_w = refs[4:14], refs[14:18]
    bias, tables = refs[18:20]
    normed_h, qkv_h, attn_h, lse_h, keep_h = refs[20:25]
    parts_h = refs[25:29]
    normed, raw, xs, wa, wb, w2, qkv, attn, lse, part, keep, sems = refs[29:]
    tokens, wide = normed.shape
    feats = wide // 4
    head_cols = attn.shape[1]
    store = pltpu.make_async_copy(normed, normed_h, sems.at[0])
    x = (x[0].at[0], *x[1:])
    loads = [pltpu.make_async_copy(x[k], xs.at[k], sems.at[1 + k]) for k in range(4)]
    copies, views, middle = staged_halves(qkv_w, place[0], wa, wb, sems, 35)
    copies2, views2 = staged(proj_w, 1, place[0], w2, sems.at[pl.ds(11, 4)])
    stores = [
        pltpu.make_async_copy(a, b, sems.at[15 + i])
        for i, (a, b) in enumerate(((qkv, qkv_h), (attn, attn_h), (lse, lse_h)))
    ]
    keeping = pltpu.make_async_copy(keep, keep_h, sems.at[18])
    chunk = keep.shape[0] - 8
    scales = keep.at[pl.ds(chunk, 8)]
    begin(loads + copies[:1])
    wait(loads)
    begin(copies[1:])
    for k in range(4):
        packed = xs[k, tokens : tokens + 16, :].astype(FULL)
        scales[:, k * feats : (k + 1) * feats] = packed[:8] + packed[8:]
    step = 32

    def norm(i, _):
        at = pl.ds(pl.multiple_of(i * step, step), step)
        values = jnp.concatenate([xs[k, at, :].astype(FULL) for k in range(4)], 1)
        mean, inverse = stats(values)
        normed[at, :] = ((values - mean) * inverse * scales[0:1] + scales[1:2]).astype(HALF)
        return 0

    lax.fori_loop(0, tokens // step, norm, 0)
    store.start()
    at = pl.ds(pl.multiple_of(place[2] * chunk, chunk), chunk)
    for k in range(4):
        keep[0:chunk, k * feats : (k + 1) * feats] = xs[k, at, :].astype(FULL)
    keeping.start()
    for i, (view, start, rows) in enumerate(views):
        wait(copies[i : i + 1])
        at = slice(0, middle) if i < 6 else slice(middle, 2 * middle)
        value = nn(normed[:, lanes(start, rows)], view[...])
        raw[:, at] = value + (bias[:, at] if i % 6 == 0 else raw[:, at])
    begin(copies2)
    mask = causal(tokens)
    lane = lax.broadcasted_iota(jnp.int32, (tokens, LANES), 1)

    def pair(p, _):
        at = [pl.ds(pl.multiple_of(j * head_cols + p * LANES, LANES), LANES) for j in range(3)]
        query = turn(raw[:, at[0]], tables[0], tables[1], tables[2]).astype(HALF)
        keys = turn(raw[:, at[1]], tables[0], tables[1], tables[2]).astype(HALF)
        values = raw[:, at[2]].astype(HALF)
        qkv[:, at[0]] = query
        qkv[:, at[1]] = keys
        qkv[:, at[2]] = values
        outs = []
        for h in range(PAIR):
            scores = jnp.where(mask, nt(own_half(query, h), keys) * SCALE, -1e30)
            top = jnp.max(scores, 1, keepdims=True)
            raised = jnp.exp(scores - top)
            total = jnp.sum(raised, 1, keepdims=True)
            lse[...] = jnp.where(lane == p * PAIR + h, top + jnp.log(total), lse[...])
            outs.append(nn((raised * (1.0 / total)).astype(HALF), values))
        attn[:, at[0]] = either(*outs).astype(HALF)
        return 0

    lax.fori_loop(0, head_cols // LANES, pair, 0, unroll=2)
    begin(stores)
    wait(copies2)
    outs = []
    for i, (view, start, size) in enumerate(views2):
        part[:, lanes(start, size)] = nn(attn[...], view[...]).astype(HALF)
        pieces = out_pieces(
            part, parts_h, chunks(place, tokens), lanes(start, size), sems, 19 + 4 * i
        )
        begin(pieces)
        outs += pieces
    wait([store, keeping] + stores + outs)


def received(got):
    return added(g[...].astype(FULL) for g in got)


def second_norm_kernel(g0, g1, g2, g3, keep_h, normed_h, resid_h, own, keep, resid, normed, sems):
    chunk = resid.shape[0]
    loads = [
        pltpu.make_async_copy(keep_h, keep, sems.at[0]),
        pltpu.make_async_copy(g0, own, sems.at[3]),
    ]
    begin(loads)
    values = received((g1, g2, g3))
    wait(loads)
    values = values + keep[0:chunk] + own[...].astype(FULL)
    resid[...] = values
    stores = [
        pltpu.make_async_copy(resid, resid_h, sems.at[1]),
        pltpu.make_async_copy(normed, normed_h, sems.at[2]),
    ]
    stores[0].start()
    mean, inverse = stats(values)
    scales = keep[chunk : chunk + 8]
    normed[...] = ((values - mean) * inverse * scales[2:3] + scales[3:4]).astype(HALF)
    stores[1].start()
    wait(stores)


def down_kernel(place, *refs):
    g, down_w = refs[0:4], refs[4:-7]
    dh_h, own_h, dh, gs, w1, own, sems = refs[-7:]
    feats = g[1].shape[1]
    g = (g[0].at[0], *g[1:])
    loads = [
        pltpu.make_async_copy(g[k], gs.at[:, k * feats : (k + 1) * feats], sems.at[k])
        for k in range(4)
    ]
    copies, views = staged(down_w, 1, place[0], w1, sems.at[pl.ds(4, 6)])
    stores = [
        pltpu.make_async_copy(dh, dh_h, sems.at[10]),
        pltpu.make_async_copy(own, own_h, sems.at[11]),
    ]
    begin(loads + copies[:2])
    wait(loads)
    chunk = own.shape[0]
    own[...] = gs[pl.ds(pl.multiple_of(place[2] * chunk, chunk), chunk), :]
    stores[1].start()
    for i, (view, start, cols) in enumerate(views):
        wait(copies[i : i + 1])
        begin(copies[i + 2 : i + 3])
        value = nt(gs[:, lanes(start, cols)], view[...])
        dh[...] = value if i == 0 else dh[...] + value
    stores[0].start()
    wait(stores)


def mlp_kernel(place, *refs):
    pieces, dh_h = refs[0:4], refs[4]
    hidden_h, first_h, rest_h, up_h, own_h = refs[15:20]
    parts_h = refs[20:24]
    normed, gate, up, w1, w2, hidden, d_gate, d_up, dh, part, sems = refs[24:]
    cut = first_h.shape[1]
    tokens, width = hidden.shape
    gate_w = [ref.at[:, 0:width] for ref in refs[5:7]] + list(refs[7:11])
    up_w = [ref.at[:, width : 2 * width] for ref in refs[5:7]] + list(refs[11:15])
    here, there = chunks(place, tokens, False), chunks(place, tokens)
    size = tokens // 4
    stores = [
        pltpu.make_async_copy(d_gate.at[:, 0:cut], first_h, sems.at[0]),
        pltpu.make_async_copy(d_gate.at[:, cut:width], rest_h, sems.at[3]),
        pltpu.make_async_copy(d_up, up_h, sems.at[1]),
    ]
    loads, loads2 = [], []
    for j in range(4):
        a, b = pl.ds(here[j], size), pl.ds(there[j], size)
        loads.append(pltpu.make_async_copy(pieces[j], normed.at[a], sems.at[48 + j]))
        loads2.append(pltpu.make_async_copy(dh_h.at[b], dh.at[a], sems.at[52 + j]))
        stores.append(pltpu.make_async_copy(hidden.at[a], hidden_h.at[b], sems.at[56 + j]))
    copies, views = staged(gate_w, 0, place[0], w1, sems.at[pl.ds(4, 6)])
    copies2, views2 = staged(up_w, 0, place[0], w2, sems.at[pl.ds(10, 6)])
    copies = copies + copies2
    begin(loads + copies[:2])
    wait(loads)
    begin(copies[2:4])
    store = pltpu.make_async_copy(normed.at[:, 0 : own_h.shape[1]], own_h, sems.at[2])
    store.start()
    for i, (view, start, rows) in enumerate(views + views2):
        wait(copies[i : i + 1])
        begin(copies[i + 4 : i + 5])
        if i == 6:
            begin(loads2)
        acc = gate if i < 6 else up
        value = nn(normed[:, lanes(start, rows)], view[...])
        acc[...] = value if i % 6 == 0 else acc[...] + value
    wait(loads2)

    def act(n, _):
        at = pl.ds(pl.multiple_of(n * LANES, LANES), LANES)
        one, two, grad = gate[:, at], up[:, at], dh[:, at]
        sig = 1.0 / (1.0 + jnp.exp(-one))
        silu = one * sig
        hidden[:, at] = (silu * two).astype(HALF)
        d_gate[:, at] = (grad * two * sig * (1.0 + one * (1.0 - sig))).astype(HALF)
        d_up[:, at] = (grad * silu).astype(HALF)
        return 0

    lax.fori_loop(0, width // LANES, act, 0)
    begin(stores)

    def back(at):
        return nt(d_gate[...], w1[at, :]) + nt(d_up[...], w2[at, :])

    backwards(back, part, parts_h, here, place[0], sems.at[pl.ds(16, 32)])
    wait(stores + [store])


def norm_back(grad_normed, values, gain):
    mean, inverse = stats(values)
    centred = (values - mean) * inverse
    scaled = grad_normed * gain
    total = jnp.mean(scaled, 1, keepdims=True)
    cross = jnp.mean(scaled * centred, 1, keepdims=True)
    back = inverse * (scaled - total - centred * cross)
    return (
        back,
        jnp.sum(grad_normed * centred, 0, keepdims=True),
        jnp.sum(grad_normed, 0, keepdims=True),
    )


def second_back_kernel(g0, g1, g2, g3, resid_h, own_h, keep_h, rounded_h, d_resid_h, part, resid, own, keep, d_resid, rounded, sems):
    chunk = resid.shape[0]
    loads = [
        pltpu.make_async_copy(a, b, sems.at[i])
        for i, (a, b) in enumerate(((resid_h, resid), (own_h, own), (keep_h, keep)))
    ]
    loads.append(pltpu.make_async_copy(g0, part, sems.at[5]))
    stores = [
        pltpu.make_async_copy(rounded, rounded_h, sems.at[3]),
        pltpu.make_async_copy(d_resid, d_resid_h, sems.at[4]),
    ]
    begin(loads)
    grad = received((g1, g2, g3))
    wait(loads)
    grad = grad + part[...].astype(FULL)
    back, gain, shift = norm_back(grad, resid[...], keep[chunk + 2 : chunk + 3])
    total = own[...].astype(FULL) + back
    rounded[...] = total.astype(HALF)
    stores[0].start()
    d_resid[0:chunk] = total
    row = lax.broadcasted_iota(jnp.int32, (8, gain.shape[1]), 0)
    d_resid[chunk : chunk + 8] = jnp.where(row == 2, gain, jnp.where(row == 3, shift, 0.0))
    stores[1].start()
    wait(stores)


def attention_back_kernel(place, *refs):
    pieces, (qkv_h, attn_h, lse_h, tables_h) = refs[0:4], refs[4:8]
    qkv_w, proj_w = refs[8:18], refs[18:22]
    d_qkv_h, parts_h = refs[22], refs[23:27]
    rounded, d_attn, d_qkv, wa, wb, w2, qkv, attn, lse, tables, part, sems = refs[27:]
    tokens = rounded.shape[0]
    rows = chunks(place, tokens)
    loads0 = [
        pltpu.make_async_copy(pieces[j], rounded.at[pl.ds(rows[j], tokens // 4)], sems.at[47 + j])
        for j in range(4)
    ]
    head_cols = attn.shape[1]
    store = pltpu.make_async_copy(d_qkv, d_qkv_h, sems.at[0])
    copies2, views2 = staged(proj_w, 1, place[0], w2, sems.at[pl.ds(1, 4)])
    copies, _, middle = staged_halves(qkv_w, place[0], wa, wb, sems, 51)
    loads = [
        pltpu.make_async_copy(a, b, sems.at[11 + i])
        for i, (a, b) in enumerate(
            ((qkv_h, qkv), (attn_h, attn), (lse_h, lse), (tables_h, tables))
        )
    ]
    begin(loads0 + copies2 + loads)
    wait(loads0 + copies2)
    begin(copies)
    d_attn[...] = added(
        nt(rounded[:, lanes(start, size)], view[...]) for view, start, size in views2
    ).astype(HALF)
    wait(loads)
    mask = causal(tokens)
    lane = lax.broadcasted_iota(jnp.int32, (tokens, LANES), 1)

    def pair(p, _):
        at = [pl.ds(pl.multiple_of(j * head_cols + p * LANES, LANES), LANES) for j in range(3)]
        query, keys, values = [qkv[:, a] for a in at]
        grad = d_attn[:, at[0]]
        product = grad.astype(FULL) * attn[:, at[0]].astype(FULL)
        dq, dk, dv = [], [], []
        for h in range(PAIR):
            delta = jnp.sum(own_half(product, h), 1, keepdims=True)
            total = jnp.sum(jnp.where(lane == p * PAIR + h, lse[...], 0.0), 1, keepdims=True)
            scores = jnp.where(mask, nt(own_half(query, h), keys) * SCALE, -1e30)
            weights = jnp.exp(scores - total)
            d_probs = nt(own_half(grad, h), values)
            d_scores = (weights * (d_probs - delta)).astype(HALF)
            dq.append(nn(d_scores, keys))
            dk.append(tn(d_scores, query))
            dv.append(tn(weights.astype(HALF), grad))
        dq = either(*dq) * SCALE
        dk = either(*dk) * SCALE
        d_qkv[:, at[0]] = turn(dq, tables[0], -tables[1], -tables[2]).astype(HALF)
        d_qkv[:, at[1]] = turn(dk, tables[0], -tables[1], -tables[2]).astype(HALF)
        d_qkv[:, at[2]] = either(*dv).astype(HALF)
        return 0

    lax.fori_loop(0, head_cols // LANES, pair, 0, unroll=2)
    store.start()
    wait(copies)

    def back(at):
        return nt(d_qkv[:, 0:middle], wa[at, :]) + nt(d_qkv[:, middle:], wb[at, :])

    backwards(back, part, parts_h, rows, place[0], sems.at[pl.ds(15, 32)])
    store.wait()


def split_low(value, out, at):
    high = value.astype(HALF)
    out[at : at + 8, :] = high
    out[at + 8 : at + 16, :] = (value - high.astype(FULL)).astype(HALF)


def first_back_kernel(g0, g1, g2, g3, d_resid_h, keep_h, out, part, d_resid, keep, sems):
    chunk = out.shape[0] - 16
    loads = [
        pltpu.make_async_copy(d_resid_h, d_resid, sems.at[0]),
        pltpu.make_async_copy(keep_h, keep, sems.at[1]),
        pltpu.make_async_copy(g0, part, sems.at[2]),
    ]
    begin(loads)
    grad = received((g1, g2, g3))
    wait(loads)
    grad = grad + part[...].astype(FULL)
    back, gain, shift = norm_back(grad, keep[0:chunk], keep[chunk : chunk + 1])
    out[0:chunk, :] = (d_resid[0:chunk] + back).astype(HALF)
    sums = d_resid[chunk : chunk + 8]
    row = lax.broadcasted_iota(jnp.int32, sums.shape, 0)
    split_low(jnp.where(row == 0, gain, jnp.where(row == 1, shift, sums)), out, chunk)


def pack_kernel(place, g0, g1, g2, g3, out):
    blocks = (g0, g1, g2, g3)
    chunk = g0.shape[0] - 16
    total = added(
        g[chunk : chunk + 8, :].astype(FULL) + g[chunk + 8 : chunk + 16, :].astype(FULL)
        for g in blocks
    )
    for k, g in enumerate(blocks):
        at = place[1] ^ k
        out[at, 0:chunk, :] = g[0:chunk, :]
        split_low(total, out.at[at], chunk)


def down_grad_kernel(place, *refs):
    hidden, groups, out_h = refs[0:8], refs[8:10], refs[10]
    left, turned, right, out, sems = refs[11:]
    rows, width = hidden[0].shape
    bases = (place[0] * 4, 4 - place[0] * 4)
    loads = [pltpu.make_async_copy(hidden[n], left.at[n], sems.at[n]) for n in range(8)]
    loads2 = [
        pltpu.make_async_copy(
            groups[n // 4].at[n % 4],
            right.at[pl.ds(pl.multiple_of((bases[n // 4] + n % 4) * rows, rows), rows)],
            sems.at[8 + n],
        )
        for n in range(8)
    ]
    begin(loads[:4])
    for n in range(8):
        wait(loads[n : n + 1])
        begin(loads[n + 4 : n + 5])
        begin(loads2[n : n + 1])
        at = pl.ds(pl.multiple_of((bases[n // 4] + n % 4) * rows, rows), rows)
        turned[:, at] = left[n].T
    wait(loads2)
    size = width // 4

    def store(n):
        at = pl.ds(pl.multiple_of(n * size, 16), size)
        return pltpu.make_async_copy(out.at[at], out_h.at[at], sems.at[16 + n])

    def product(n, _):
        at = pl.ds(pl.multiple_of(n * size, 16), size)
        out[at, :] = nn(turned[at, :], right[...])
        store(n).start()
        return 0

    lax.fori_loop(0, 4, product, 0)
    wait([store(n) for n in range(4)])


def weight_grad_kernel(ones, tile, mixed, place, *refs):
    lefts, rights, out_h = refs[0:4], refs[4:8], refs[8]
    left, turned, right, out, sems = refs[9:]
    rows, width = lefts[0].shape
    cols = right.shape[1]
    size = rows // 4
    loads = []
    for k in range(4):
        if mixed:
            here, there = chunks(place, rows, False), chunks(place, rows)
            loads.append(
                [
                    pltpu.make_async_copy(
                        lefts[k].at[pl.ds(there[j], size)],
                        left.at[k, pl.ds(here[j], size)],
                        sems.at[k, j],
                    )
                    for j in range(4)
                ]
            )
        else:
            loads.append([pltpu.make_async_copy(lefts[k], left.at[k], sems.at[k, 0])])
    loads2 = [
        pltpu.make_async_copy(rights[k], right.at[pl.ds(k * rows, rows)], sems.at[4, k])
        for k in range(4)
    ]
    for copies in loads:
        begin(copies)
    begin(loads2)
    for k in range(4):
        wait(loads[k])
        turned[:, k * rows : (k + 1) * rows] = left[k].T
    wait(loads2)

    def store(at, size, n):
        return pltpu.make_async_copy(
            out.at[:, pl.ds(at, size)], out_h.at[:, pl.ds(at, size)], sems.at[5, n]
        )

    def product(at, size):
        n = at // tile
        at = pl.ds(at, size)
        out[0:width, at] = nn(turned[...], right[:, at]).astype(HALF)
        if ones:
            total = jnp.sum(right[:, at].astype(FULL), 0, keepdims=True)
            high = total.astype(HALF).astype(FULL)
            row = lax.broadcasted_iota(jnp.int32, (16, size), 0)
            out[width : width + 16, at] = jnp.where(row < 8, high, total - high).astype(HALF)
        store(at.start, size, n).start()

    tiles(cols, tile, product)
    for at in range(0, cols, tile):
        store(at, min(tile, cols - at), at // tile).wait()


def total_kernel(axis, *refs):
    out = refs[-1]
    width = out.shape[2]
    at = 0
    for mine, other in zip(refs[0:-1:2], refs[1:-1:2]):
        done = 0
        while done < mine.shape[1]:
            part, lane = divmod(at + done, width)
            size = min(width - lane, mine.shape[1] - done)
            here, there = slice(done, done + size), slice(lane, lane + size)
            value = mine[:, here].astype(FULL) + other[:, here].astype(FULL)
            if axis == 1:
                out[:, part, there] = value
            else:
                out[part, :, there] = value
            done += size
        at += done


def leaf_kernel(place, *refs):
    attn, hidden = refs[0:4], refs[4:8]
    proj_h, down_h = refs[8:10]
    outs = refs[10:14]
    w1, w2, left, left2, out, sems = refs[14:]
    apart = place[1] ^ place[2]
    loads = [
        pltpu.make_async_copy(proj_h, w1, sems.at[0]),
        pltpu.make_async_copy(down_h, w2, sems.at[1]),
    ]
    for k in range(4):
        loads.append(pltpu.make_async_copy(attn[k], left.at[apart ^ k], sems.at[2 + 2 * k]))
        loads.append(pltpu.make_async_copy(hidden[k], left2.at[apart ^ k], sems.at[3 + 2 * k]))
    begin(loads)
    wait(loads)
    stores = [pltpu.make_async_copy(out.at[k], outs[k], sems.at[10 + k]) for k in range(4)]
    for k in range(4):
        out[k] = (nn(left[k], w1[...]) + nn(left2[k], w2[...])).astype(HALF)
        stores[k].start()
    wait(stores)


VM = pl.BlockSpec(memory_space=pltpu.VMEM)
SM = pl.BlockSpec(memory_space=pltpu.SMEM)
HB = pl.BlockSpec(memory_space=pltpu.HBM)
AN = pl.BlockSpec(memory_space=pl.ANY)
FOUR = [HB, AN, HB, AN]
SIX = [HB, AN, HB, HB, AN, AN]


def call(kernel, specs, outs, args, scratch=(), flops=0, limit=None):
    moved = sum(a.size * a.dtype.itemsize for a in args)
    moved += sum(math.prod(s) * jnp.dtype(t).itemsize for s, t, _ in outs)
    return pl.pallas_call(
        kernel,
        out_shape=[pltpu.HBM(s, t) if m is HB else jax.ShapeDtypeStruct(s, t) for s, t, m in outs],
        in_specs=specs,
        out_specs=[m for _, _, m in outs],
        scratch_shapes=list(scratch),
        compiler_params=pltpu.CompilerParams(vmem_limit_bytes=limit),
        cost_estimate=pl.CostEstimate(flops=flops, bytes_accessed=moved, transcendentals=0),
    )(*[
        pltpu.with_memory_space_constraint(a, pltpu.HBM) if m is HB else a
        for a, m in zip(args, specs, strict=True)
    ])


def weight_grad(place, lefts, rights, ones=False, tile=256, mixed=False):
    rows, width = lefts[0].shape
    cols = rights[0].shape[1]
    high = width + (16 if ones else 0)
    size = 2 * (8 * rows * width + 4 * rows * cols + high * cols)
    (out,) = call(
        functools.partial(weight_grad_kernel, ones, tile, mixed),
        [SM] + FOUR + FOUR,
        [((high, cols), HALF, HB)],
        [place, *lefts, *rights],
        [
            pltpu.VMEM((4, rows, width), HALF),
            pltpu.VMEM((width, 4 * rows), HALF),
            pltpu.VMEM((4 * rows, cols), HALF),
            pltpu.VMEM((high, cols), HALF),
            pltpu.SemaphoreType.DMA((6, max(4, -(-cols // tile)))),
        ],
        flops=8 * rows * width * cols,
        limit=size + 4 * MIB,
    )
    return out


def rotation_tables(length):
    half = ROT // 2
    lane = jnp.arange(LANES) % HD
    freqs = THETA ** (-2.0 * (lane % half).astype(FULL) / ROT)
    angles = jnp.arange(length, dtype=FULL)[:, None] * freqs[None, :]
    cos_t = jnp.where(lane < ROT, jnp.cos(angles), 1.0)
    sin_t = jnp.sin(angles)
    down = jnp.where(lane < half, -sin_t, 0.0)
    up = jnp.where((lane >= half) & (lane < ROT), sin_t, 0.0)
    return jnp.stack([cos_t, down, up])


def bias_mask(width):
    lanes = jnp.arange(width) % HD < ROT
    ones = jnp.ones((width,), FULL)
    return jnp.stack([ones, jnp.where(lanes, 1.0, 0.0).astype(FULL), ones])


def block(
    block_in,
    norm1_gain,
    norm1_bias,
    w_qkv,
    qkv_bias,
    w_proj,
    norm2_gain,
    norm2_bias,
    w_gateup,
    w_down,
    out_grad,
):
    rows = lax.axis_size(ROW)
    cols = lax.axis_size(COL)
    col = lax.axis_index(COL)
    row = lax.axis_index(ROW)
    odd = lax.axis_index(DP) % 2
    two = lax.axis_size(DP) == 2
    feats = w_qkv.shape[0]
    head_cols = w_qkv.shape[2]
    width = w_gateup.shape[2]
    tokens = block_in.shape[0]
    chunk = tokens // cols
    wide = rows * feats
    place = jnp.stack([odd, row, col, odd]).astype(jnp.int32)
    tables = rotation_tables(SEQ)

    def narrow(value):
        return [value[:, k * feats : (k + 1) * feats] for k in range(rows)]

    own_qkv = w_qkv.reshape(feats, 3 * head_cols)
    own_inner = w_gateup.reshape(feats, 2 * width)
    in_group = col_swaps([block_in] * 4)
    qkv_half = half_of(own_qkv)
    middle = 3 * head_cols // 2
    qkv_w = [own_qkv, swap(own_qkv, ROW, 1)]
    qkv_w += across(qkv_half[:, :middle]) + across(qkv_half[:, middle:])
    proj_w = row_gather(w_proj)
    beside = swap(own_inner, ROW, 1)
    inner_w = [own_inner, beside]
    gate_half, up_half, down_half = call(
        halves_kernel,
        [SM, HB, HB],
        [((feats // 2, width), HALF, HB)] * 2 + [((width, feats // 2), HALF, HB)],
        [place, own_inner, w_down],
        [
            pltpu.VMEM((2, feats // 2, width), HALF),
            pltpu.VMEM((width, feats // 2), HALF),
            pltpu.SemaphoreType.DMA((6,)),
        ],
        limit=4 * MIB,
    )
    down_w = [w_down, swap(w_down, ROW, 1), *across(down_half)]
    inner_w += across(gate_half) + across(up_half)
    scales = jnp.concatenate(
        [jnp.stack([norm1_gain, norm1_bias, norm2_gain, norm2_bias]), jnp.zeros((4, feats), FULL)], 0
    )
    high = lax.reduce_precision(scales, 8, 7)
    packed = jnp.concatenate([high.astype(HALF), (scales - high).astype(HALF)], 0)

    def sort(blocks, below):
        high = tokens + sum(b.shape[0] for b in below)
        *outs, every = call(
            sort_kernel,
            [SM] + [AN] * (4 + len(below)),
            [((high, feats), HALF, HB)] * 3 + [((rows, high, feats), HALF, HB)],
            [place, *blocks, *below],
            [pltpu.VMEM((rows, high, feats), HALF), pltpu.SemaphoreType.DMA((12,))],
            limit=4 * MIB,
        )
        return outs, every

    outs, x_own = sort(in_group, [packed])
    x = [x_own] + row_exchange([x_own] + outs)[1:]
    outs, grad_group = sort(col_swaps([out_grad] * 4), [])
    grad_seq = [grad_group] + row_exchange([grad_group] + outs)[1:]

    normed1, qkv, attn, lse, keep, *parts = call(
        attention_kernel,
        [SM] + [HB] * 13 + [AN] + [HB] * 4 + [VM] * 2,
        [
            ((tokens, wide), HALF, HB),
            ((tokens, 3 * head_cols), HALF, HB),
            ((tokens, head_cols), HALF, HB),
            ((tokens, LANES), FULL, HB),
            ((chunk + 8, wide), FULL, HB),
            *[((chunk, wide), HALF, HB)] * 4,
        ],
        [place, *x, *qkv_w, *proj_w, qkv_bias.reshape(1, 3 * head_cols), tables],
        [
            pltpu.VMEM((tokens, wide), HALF),
            pltpu.VMEM((tokens, 3 * head_cols), FULL),
            pltpu.VMEM((4, tokens + 16, feats), HALF),
            pltpu.VMEM((wide, middle), HALF),
            pltpu.VMEM((wide, middle), HALF),
            pltpu.VMEM((head_cols, wide), HALF),
            pltpu.VMEM((tokens, 3 * head_cols), HALF),
            pltpu.VMEM((tokens, head_cols), HALF),
            pltpu.VMEM((tokens, LANES), FULL),
            pltpu.VMEM((tokens, wide), HALF),
            pltpu.VMEM((chunk + 8, wide), FULL),
            pltpu.SemaphoreType.DMA((47,)),
        ],
        flops=2 * tokens * wide * 4 * head_cols,
        limit=20 * MIB,
    )
    normed2, resid = call(
        second_norm_kernel,
        [HB] + [VM] * 3 + [HB],
        [((chunk, wide), HALF, HB), ((chunk, wide), FULL, HB)],
        [*col_swaps(parts), keep],
        [
            pltpu.VMEM((chunk, wide), HALF),
            pltpu.VMEM((chunk + 8, wide), FULL),
            pltpu.VMEM((chunk, wide), FULL),
            pltpu.VMEM((chunk, wide), HALF),
            pltpu.SemaphoreType.DMA((4,)),
        ],
        limit=8 * MIB,
    )
    normed2 = col_swaps([normed2] * 4)
    d_hidden, own_grad = call(
        down_kernel,
        [SM] + FOUR + SIX,
        [((tokens, width), FULL, HB), ((chunk, wide), HALF, HB)],
        [place, *grad_seq, *down_w],
        [
            pltpu.VMEM((tokens, width), FULL),
            pltpu.VMEM((tokens, wide), HALF),
            pltpu.VMEM((width, wide), HALF),
            pltpu.VMEM((chunk, wide), HALF),
            pltpu.SemaphoreType.DMA((12,)),
        ],
        flops=2 * tokens * wide * width,
        limit=12 * MIB,
    )
    cut = 4 * LANES
    hidden, d_first, d_rest, d_up, own_normed2, *parts = call(
        mlp_kernel,
        [SM, HB] + [AN] * 3 + [HB] + SIX + SIX[2:],
        [
            ((tokens, width), HALF, HB),
            ((tokens, cut), HALF, HB),
            ((tokens, width - cut), HALF, HB),
            ((tokens, width), HALF, HB),
            ((tokens, feats), HALF, HB),
            *[((chunk, wide), HALF, HB)] * 4,
        ],
        [place, *normed2, d_hidden, *inner_w],
        [
            pltpu.VMEM((tokens, wide), HALF),
            pltpu.VMEM((tokens, width), FULL),
            pltpu.VMEM((tokens, width), FULL),
            pltpu.VMEM((wide, width), HALF),
            pltpu.VMEM((wide, width), HALF),
            pltpu.VMEM((tokens, width), HALF),
            pltpu.VMEM((tokens, width), HALF),
            pltpu.VMEM((tokens, width), HALF),
            pltpu.VMEM((tokens, width), FULL),
            pltpu.VMEM((tokens, wide), HALF),
            pltpu.SemaphoreType.DMA((60,)),
        ],
        flops=2 * tokens * wide * 4 * width,
        limit=28 * MIB,
    )
    rounded, d_resid = call(
        second_back_kernel,
        [HB] + [VM] * 3 + [HB] * 3,
        [((chunk, wide), HALF, HB), ((chunk + 8, wide), FULL, HB)],
        [*col_swaps(parts), resid, own_grad, keep],
        [
            pltpu.VMEM((chunk, wide), HALF),
            pltpu.VMEM((chunk, wide), FULL),
            pltpu.VMEM((chunk, wide), HALF),
            pltpu.VMEM((chunk + 8, wide), FULL),
            pltpu.VMEM((chunk + 8, wide), FULL),
            pltpu.VMEM((chunk, wide), HALF),
            pltpu.SemaphoreType.DMA((6,)),
        ],
        limit=8 * MIB,
    )
    rounded = col_swaps([rounded] * 4)
    d_qkv, *parts = call(
        attention_back_kernel,
        [SM, HB] + [AN] * 3 + [HB] * 18,
        [((tokens, 3 * head_cols), HALF, HB), *[((chunk, wide), HALF, HB)] * 4],
        [place, *rounded, qkv, attn, lse, tables, *qkv_w, *proj_w],
        [
            pltpu.VMEM((tokens, wide), HALF),
            pltpu.VMEM((tokens, head_cols), HALF),
            pltpu.VMEM((tokens, 3 * head_cols), HALF),
            pltpu.VMEM((wide, middle), HALF),
            pltpu.VMEM((wide, middle), HALF),
            pltpu.VMEM((head_cols, wide), HALF),
            pltpu.VMEM((tokens, 3 * head_cols), HALF),
            pltpu.VMEM((tokens, head_cols), HALF),
            pltpu.VMEM((tokens, LANES), FULL),
            pltpu.VMEM((3, tokens, LANES), FULL),
            pltpu.VMEM((tokens, wide), HALF),
            pltpu.SemaphoreType.DMA((63,)),
        ],
        flops=2 * tokens * wide * 5 * head_cols,
        limit=18 * MIB,
    )
    (last,) = call(
        first_back_kernel,
        [HB] + [VM] * 3 + [HB] * 2,
        [((chunk + 16, wide), HALF, VM)],
        [*col_swaps(parts), d_resid, keep],
        [
            pltpu.VMEM((chunk, wide), HALF),
            pltpu.VMEM((chunk + 8, wide), FULL),
            pltpu.VMEM((chunk + 8, wide), FULL),
            pltpu.SemaphoreType.DMA((3,)),
        ],
        limit=8 * MIB,
    )

    got = row_exchange(narrow(last))
    (packed,) = call(
        pack_kernel,
        [SM] + [VM] * 4,
        [((rows, chunk + 16, feats), HALF, VM)],
        [place, *got],
        limit=4 * MIB,
    )
    got = col_exchange(packed)
    grad_in = got[:, :chunk].reshape(tokens, feats).astype(FULL)
    vectors = got[:, chunk:].astype(FULL)
    vectors = jnp.sum(vectors[:, :4] + vectors[:, 8:12], 0)
    if two:
        vectors = vectors + swap(vectors, DP, 1)
    else:
        vectors = lax.psum(vectors, DP)

    attn_group = row_gather(attn)
    normed_group = row_exchange(narrow(normed1))

    def blocks_of(pieces):
        return [jnp.concatenate(b, 0) for b in zip(*[narrow(p) for p in pieces])]

    normed2_group = [own_normed2] + row_exchange(blocks_of(normed2))[1:]
    hidden_group = row_gather(hidden)
    first_group = row_gather(d_first)
    rest_group = row_gather(d_rest)
    up_group = row_gather(d_up)
    first_mine = weight_grad(place, normed2_group, first_group)
    rest_mine = weight_grad(place, normed2_group, rest_group)
    up_mine = weight_grad(place, normed2_group, up_group)
    if two:
        other_group = row_gather(swap(hidden, DP, 1))
        (grad_down,) = call(
            down_grad_kernel,
            [SM] + FOUR + FOUR + [HB] * 2,
            [((width, feats), FULL, HB)],
            [place, *hidden_group, *other_group, grad_group, swap(grad_group, DP, 1)],
            [
                pltpu.VMEM((8, tokens, width), HALF),
                pltpu.VMEM((width, 8 * tokens), HALF),
                pltpu.VMEM((8 * tokens, feats), HALF),
                pltpu.VMEM((width, feats), FULL),
                pltpu.SemaphoreType.DMA((20,)),
            ],
            flops=16 * tokens * width * feats,
            limit=22 * MIB,
        )
        pairs = [
            (first_mine, swap(first_mine, DP, 1)),
            (rest_mine, swap(rest_mine, DP, 1)),
            (up_mine, swap(up_mine, DP, 1)),
        ]
        grad_gateup = total(pairs, (feats, 2, width))
    else:
        grads = [grad_group[k] for k in range(rows)]
        grad_down = over_groups(weight_grad(place, hidden_group, grads))
        mine = jnp.concatenate([first_mine, rest_mine, up_mine], 1)
        grad_gateup = over_groups(mine).reshape(feats, 2, width)
    leaf = call(
        leaf_kernel,
        [SM] + FOUR + FOUR + [HB] * 2,
        [((tokens, feats), HALF, HB)] * 4,
        [place, *attn_group, *hidden_group, w_proj, w_down],
        [
            pltpu.VMEM((head_cols, feats), HALF),
            pltpu.VMEM((width, feats), HALF),
            pltpu.VMEM((4, tokens, head_cols), HALF),
            pltpu.VMEM((4, tokens, width), HALF),
            pltpu.VMEM((4, tokens, feats), HALF),
            pltpu.SemaphoreType.DMA((14,)),
        ],
        flops=2 * rows * tokens * feats * (head_cols + width),
        limit=12 * MIB,
    )
    leaf = [leaf[0], swap(leaf[1], COL, 1), swap(leaf[2], COL, 2), swap(leaf[3], COL, 3)]
    block_out = block_in.astype(FULL) + sum(part.astype(FULL) for part in leaf)
    rounded_group = row_exchange(blocks_of(rounded))
    proj_mine = weight_grad(place, attn_group, rounded_group, mixed=True)
    if two:
        proj_other = swap(proj_mine, DP, 1)
        grad_proj = proj_mine.astype(FULL) + proj_other.astype(FULL)
    else:
        grad_proj = over_groups(proj_mine)
    qkv_group = row_gather(d_qkv)
    mine = weight_grad(place, normed_group, qkv_group, True)
    if two:
        other = swap(mine, DP, 1)
        grad_qkv = total([(mine, other)], (3, feats, head_cols), 0).swapaxes(0, 1)
        both = mine[feats:].astype(FULL) + other[feats:].astype(FULL)
    else:
        both = lax.psum(mine.astype(FULL), DP)
        grad_qkv = both[:feats].reshape(feats, 3, head_cols)
        both = both[feats:]
    grad_bias = (both[0] + both[8]).reshape(3, head_cols) * bias_mask(head_cols)
    gain1_grad, bias1_grad, gain2_grad, bias2_grad = vectors
    return (
        block_out,
        grad_in,
        grad_qkv,
        grad_bias,
        grad_proj,
        gain1_grad,
        bias1_grad,
        gain2_grad,
        bias2_grad,
        grad_gateup,
        grad_down,
    )


def solution(mesh):
    return jax.shard_map(
        block,
        mesh=mesh,
        in_specs=(
            P((DP, COL), ROW),
            P(ROW),
            P(ROW),
            P(ROW, None, COL),
            P(None, COL),
            P(COL, ROW),
            P(ROW),
            P(ROW),
            P(ROW, None, COL),
            P(COL, ROW),
            P((DP, COL), ROW),
        ),
        out_specs=(
            P((DP, COL), ROW),
            P((DP, COL), ROW),
            P(ROW, None, COL),
            P(None, COL),
            P(COL, ROW),
            P(ROW),
            P(ROW),
            P(ROW),
            P(ROW),
            P(ROW, None, COL),
            P(COL, ROW),
        ),
        check_vma=False,
    )
```

```python
import functools
import math

import jax
import jax.numpy as jnp
from jax import lax
from jax.experimental import pallas as pl
from jax.experimental.pallas import tpu as pltpu
from jax.sharding import PartitionSpec as P


HD = 64
ROT = 16
SEQ = 256

EPS = 1e-05
THETA = 10000.0
SCALE = 1.0 / math.sqrt(HD)

HALF = jnp.bfloat16
FULL = jnp.float32
LANES = 128
PAIR = LANES // HD
MIB = 1 << 20


DP, ROW, COL = "dp", "row", "col"


def swap(value, axis, bit):
    size = lax.axis_size(axis)
    return lax.ppermute(value, axis, [(i, i ^ bit) for i in range(size)])


def row_exchange(blocks):
    return [blocks[0]] + [swap(blocks[k], ROW, k) for k in range(1, 4)]


def col_exchange(blocks):
    return lax.all_to_all(blocks, COL, 0, 0, tiled=True)


def col_swaps(blocks):
    there = {j: swap(blocks[j], COL, j) for j in (2, 3, 1)}
    return [blocks[0], there[1], there[2], there[3]]


def row_gather(local):
    across = swap(local, ROW, 2)
    beside = swap(local, ROW, 1)
    both = swap(across, ROW, 1)
    return [local, beside, across, both]


def across(mine):
    first = swap(mine, ROW, 2)
    second = swap(first, DP, 1)
    third = swap(first, ROW, 1)
    return [first, second, third, swap(second, ROW, 1)]


def half_of(weight):
    half = weight.shape[0] // 2
    odd = lax.axis_index(DP) % 2
    return lax.dynamic_slice_in_dim(weight, odd * half, half, 0)


def total(pairs, shape, axis=1, tile=128):
    rows = shape[1 - axis]
    block = (tile, *shape[1:]) if axis == 1 else (shape[0], tile, shape[2])
    parts = [part for pair in pairs for part in pair]
    return pl.pallas_call(
        functools.partial(total_kernel, axis),
        grid=(rows // tile,),
        out_shape=jax.ShapeDtypeStruct(shape, FULL),
        in_specs=[pl.BlockSpec((tile, p.shape[1]), lambda n: (n, 0)) for p in parts],
        out_specs=pl.BlockSpec(block, (lambda n: (n, 0, 0)) if axis == 1 else (lambda n: (0, n, 0))),
        compiler_params=pltpu.CompilerParams(vmem_limit_bytes=10 * MIB),
        cost_estimate=pl.CostEstimate(
            flops=math.prod(shape), bytes_accessed=8 * math.prod(shape), transcendentals=0
        ),
    )(*parts)


def over_groups(mine):
    return lax.psum(mine.astype(FULL), DP)


def places(refs, axis, odd):
    size = refs[0].shape[axis]
    if len(refs) == 4:
        return [(ref, k * size, size) for k, ref in enumerate(refs)]
    half = size // 2
    own, beside, first, second, first_b, second_b = refs
    near = pl.multiple_of(odd * half, LANES)
    far = pl.multiple_of((1 - odd) * half, LANES)
    return [
        (own, 0, size),
        (beside, size, size),
        (first, 2 * size + near, half),
        (second, 2 * size + far, half),
        (first_b, 3 * size + near, half),
        (second_b, 3 * size + far, half),
    ]


def staged(refs, axis, odd, buffer, sems):
    copies, views, at = [], [], 0
    for i, (ref, start, size) in enumerate(places(refs, axis, odd)):
        here = pl.ds(at, size)
        view = buffer.at[here] if axis == 0 else buffer.at[:, here]
        copies.append(pltpu.make_async_copy(ref, view, sems.at[i]))
        views.append((view, start, size))
        at += size
    return copies, views


def staged_halves(refs, odd, first, second, sems, at):
    middle = first.shape[1]
    copies, views = [], []
    for n, buffer in enumerate((first, second)):
        cols = slice(n * middle, (n + 1) * middle)
        parts = [ref.at[:, cols] for ref in refs[0:2]] + list(refs[2 + 4 * n : 6 + 4 * n])
        more, views2 = staged(parts, 0, odd, buffer, sems.at[pl.ds(at + 6 * n, 6)])
        copies += more
        views += views2
    return copies, views, middle


def lanes(at, size):
    return pl.ds(at if isinstance(at, int) else pl.multiple_of(at, LANES), size)


def added(terms):
    total = None
    for term in terms:
        total = term if total is None else total + term
    return total


def begin(copies):
    for copy in copies:
        copy.start()


def wait(copies):
    for copy in copies:
        copy.wait()


def nn(left, right):
    return lax.dot_general(left, right, (((1,), (0,)), ((), ())), preferred_element_type=FULL)


def nt(left, right):
    return lax.dot_general(left, right, (((1,), (1,)), ((), ())), preferred_element_type=FULL)


def tn(left, right):
    return lax.dot_general(left, right, (((0,), (0,)), ((), ())), preferred_element_type=FULL)


def tiles(extent, size, step):
    whole = extent // size

    def one(n, _):
        step(pl.multiple_of(n * size, size), size)
        return 0

    lax.fori_loop(0, whole, one, 0)
    if extent % size:
        step(whole * size, extent % size)


def turn(value, cos_t, down, up):
    return (
        value * cos_t
        + pltpu.roll(value, LANES - ROT // 2, 1) * down
        + pltpu.roll(value, ROT // 2, 1) * up
    )


def stats(values):
    mean = jnp.mean(values, 1, keepdims=True)
    second = jnp.mean(values * values, 1, keepdims=True)
    return mean, lax.rsqrt(second - mean * mean + EPS)


def causal(length):
    at = lax.broadcasted_iota(jnp.int32, (length, length), 0)
    return at >= lax.broadcasted_iota(jnp.int32, (length, length), 1)


def own_half(value, head):
    lane = lax.broadcasted_iota(jnp.int32, value.shape, 1)
    return jnp.where((lane < HD) == (head == 0), value, jnp.zeros_like(value))


def either(first, second):
    lane = lax.broadcasted_iota(jnp.int32, first.shape, 1)
    return jnp.where(lane < HD, first, second)


def backwards(product, part, outs, rows, odd, sems):
    size = part.shape[1] // 8

    def pieces(n):
        at = lanes(jnp.where(n < 4, n, n ^ odd) * size, size)
        return at, out_pieces(part, outs, rows, at, sems, 4 * n)

    def one(n, _):
        at, copies = pieces(n)
        part[:, at] = product(pl.ds(pl.multiple_of(n * size, size), size)).astype(HALF)
        begin(copies)
        return 0

    lax.fori_loop(0, 8, one, 0, unroll=2)
    for n in range(8):
        wait(pieces(n)[1])


def out_pieces(source, outs, rows, at, sems, first):
    size = outs[0].shape[0]
    return [
        pltpu.make_async_copy(
            source.at[pl.ds(rows[j], size), at], outs[j].at[:, at], sems.at[first + j]
        )
        for j in range(4)
    ]


def chunks(place, rows, apart=True):
    size = rows // 4
    if not apart:
        return [j * size for j in range(4)]
    return [pl.multiple_of((place[2] ^ j) * size, size) for j in range(4)]


def halves_kernel(place, inner, down, gate_h, up_h, down_h, wide, tall, sems):
    size, width = gate_h.shape
    at = pl.ds(pl.multiple_of(place[0] * size, size), size)
    loads = [
        pltpu.make_async_copy(down.at[:, at], tall, sems.at[0]),
        pltpu.make_async_copy(inner.at[at, 0:width], wide.at[0], sems.at[1]),
        pltpu.make_async_copy(inner.at[at, width : 2 * width], wide.at[1], sems.at[2]),
    ]
    stores = [
        pltpu.make_async_copy(tall, down_h, sems.at[3]),
        pltpu.make_async_copy(wide.at[0], gate_h, sems.at[4]),
        pltpu.make_async_copy(wide.at[1], up_h, sems.at[5]),
    ]
    begin(loads)
    for load, store in zip(loads, stores):
        load.wait()
        store.start()
    wait(stores)


def sort_kernel(place, *refs):
    blocks, below = refs[0:4], refs[4:-6]
    outs, every, both, sems = refs[-6:-3], refs[-3], refs[-2], refs[-1]
    apart = place[1] ^ place[2]
    rows = blocks[0].shape[0]
    loads = [
        pltpu.make_async_copy(blocks[j], both.at[apart ^ j, pl.ds(0, rows)], sems.at[j])
        for j in range(4)
    ]
    for ref in below:
        for k in range(4):
            at = pl.ds(rows, ref.shape[0])
            loads.append(pltpu.make_async_copy(ref, both.at[k, at], sems.at[4 + k]))
    begin(loads)
    wait(loads)
    stores = [pltpu.make_async_copy(both.at[k + 1], outs[k], sems.at[8 + k]) for k in range(3)]
    stores.append(pltpu.make_async_copy(both, every, sems.at[11]))
    begin(stores)
    wait(stores)


def attention_kernel(place, *refs):
    x = refs[0:4]
    qkv_w, proj_w = refs[4:14], refs[14:18]
    bias, tables = refs[18:20]
    normed_h, qkv_h, attn_h, lse_h, keep_h = refs[20:25]
    parts_h = refs[25:29]
    normed, raw, xs, wa, wb, w2, qkv, attn, lse, part, keep, sems = refs[29:]
    tokens, wide = normed.shape
    feats = wide // 4
    head_cols = attn.shape[1]
    store = pltpu.make_async_copy(normed, normed_h, sems.at[0])
    x = (x[0].at[0], *x[1:])
    loads = [pltpu.make_async_copy(x[k], xs.at[k], sems.at[1 + k]) for k in range(4)]
    copies, views, middle = staged_halves(qkv_w, place[0], wa, wb, sems, 35)
    copies2, views2 = staged(proj_w, 1, place[0], w2, sems.at[pl.ds(11, 4)])
    stores = [
        pltpu.make_async_copy(a, b, sems.at[15 + i])
        for i, (a, b) in enumerate(((qkv, qkv_h), (attn, attn_h), (lse, lse_h)))
    ]
    keeping = pltpu.make_async_copy(keep, keep_h, sems.at[18])
    chunk = keep.shape[0] - 8
    scales = keep.at[pl.ds(chunk, 8)]
    begin(loads + copies[:1])
    wait(loads)
    begin(copies[1:])
    for k in range(4):
        packed = xs[k, tokens : tokens + 16, :].astype(FULL)
        scales[:, k * feats : (k + 1) * feats] = packed[:8] + packed[8:]
    step = 32

    def norm(i, _):
        at = pl.ds(pl.multiple_of(i * step, step), step)
        values = jnp.concatenate([xs[k, at, :].astype(FULL) for k in range(4)], 1)
        mean, inverse = stats(values)
        normed[at, :] = ((values - mean) * inverse * scales[0:1] + scales[1:2]).astype(HALF)
        return 0

    lax.fori_loop(0, tokens // step, norm, 0)
    store.start()
    at = pl.ds(pl.multiple_of(place[2] * chunk, chunk), chunk)
    for k in range(4):
        keep[0:chunk, k * feats : (k + 1) * feats] = xs[k, at, :].astype(FULL)
    keeping.start()
    for i, (view, start, rows) in enumerate(views):
        wait(copies[i : i + 1])
        at = slice(0, middle) if i < 6 else slice(middle, 2 * middle)
        value = nn(normed[:, lanes(start, rows)], view[...])
        raw[:, at] = value + (bias[:, at] if i % 6 == 0 else raw[:, at])
    begin(copies2)
    mask = causal(tokens)
    lane = lax.broadcasted_iota(jnp.int32, (tokens, LANES), 1)

    def pair(p, _):
        at = [pl.ds(pl.multiple_of(j * head_cols + p * LANES, LANES), LANES) for j in range(3)]
        query = turn(raw[:, at[0]], tables[0], tables[1], tables[2]).astype(HALF)
        keys = turn(raw[:, at[1]], tables[0], tables[1], tables[2]).astype(HALF)
        values = raw[:, at[2]].astype(HALF)
        qkv[:, at[0]] = query
        qkv[:, at[1]] = keys
        qkv[:, at[2]] = values
        outs = []
        for h in range(PAIR):
            scores = jnp.where(mask, nt(own_half(query, h), keys) * SCALE, -1e30)
            top = jnp.max(scores, 1, keepdims=True)
            raised = jnp.exp(scores - top)
            total = jnp.sum(raised, 1, keepdims=True)
            lse[...] = jnp.where(lane == p * PAIR + h, top + jnp.log(total), lse[...])
            outs.append(nn((raised * (1.0 / total)).astype(HALF), values))
        attn[:, at[0]] = either(*outs).astype(HALF)
        return 0

    lax.fori_loop(0, head_cols // LANES, pair, 0, unroll=2)
    begin(stores)
    wait(copies2)
    outs = []
    for i, (view, start, size) in enumerate(views2):
        part[:, lanes(start, size)] = nn(attn[...], view[...]).astype(HALF)
        pieces = out_pieces(
            part, parts_h, chunks(place, tokens), lanes(start, size), sems, 19 + 4 * i
        )
        begin(pieces)
        outs += pieces
    wait([store, keeping] + stores + outs)


def received(got):
    return added(g[...].astype(FULL) for g in got)


def second_norm_kernel(g0, g1, g2, g3, keep_h, normed_h, resid_h, own, keep, resid, normed, sems):
    chunk = resid.shape[0]
    loads = [
        pltpu.make_async_copy(keep_h, keep, sems.at[0]),
        pltpu.make_async_copy(g0, own, sems.at[3]),
    ]
    begin(loads)
    values = received((g1, g2, g3))
    wait(loads)
    values = values + keep[0:chunk] + own[...].astype(FULL)
    resid[...] = values
    stores = [
        pltpu.make_async_copy(resid, resid_h, sems.at[1]),
        pltpu.make_async_copy(normed, normed_h, sems.at[2]),
    ]
    stores[0].start()
    mean, inverse = stats(values)
    scales = keep[chunk : chunk + 8]
    normed[...] = ((values - mean) * inverse * scales[2:3] + scales[3:4]).astype(HALF)
    stores[1].start()
    wait(stores)


def down_kernel(place, *refs):
    g, down_w = refs[0:4], refs[4:-7]
    dh_h, own_h, dh, gs, w1, own, sems = refs[-7:]
    feats = g[1].shape[1]
    g = (g[0].at[0], *g[1:])
    loads = [
        pltpu.make_async_copy(g[k], gs.at[:, k * feats : (k + 1) * feats], sems.at[k])
        for k in range(4)
    ]
    copies, views = staged(down_w, 1, place[0], w1, sems.at[pl.ds(4, 6)])
    stores = [
        pltpu.make_async_copy(dh, dh_h, sems.at[10]),
        pltpu.make_async_copy(own, own_h, sems.at[11]),
    ]
    begin(loads + copies[:2])
    wait(loads)
    chunk = own.shape[0]
    own[...] = gs[pl.ds(pl.multiple_of(place[2] * chunk, chunk), chunk), :]
    stores[1].start()
    for i, (view, start, cols) in enumerate(views):
        wait(copies[i : i + 1])
        begin(copies[i + 2 : i + 3])
        value = nt(gs[:, lanes(start, cols)], view[...])
        dh[...] = value if i == 0 else dh[...] + value
    stores[0].start()
    wait(stores)


def mlp_kernel(place, *refs):
    pieces, dh_h = refs[0:4], refs[4]
    hidden_h, first_h, rest_h, up_h, own_h = refs[15:20]
    parts_h = refs[20:24]
    normed, gate, up, w1, w2, hidden, d_gate, d_up, dh, part, sems = refs[24:]
    cut = first_h.shape[1]
    tokens, width = hidden.shape
    gate_w = [ref.at[:, 0:width] for ref in refs[5:7]] + list(refs[7:11])
    up_w = [ref.at[:, width : 2 * width] for ref in refs[5:7]] + list(refs[11:15])
    here, there = chunks(place, tokens, False), chunks(place, tokens)
    size = tokens // 4
    stores = [
        pltpu.make_async_copy(d_gate.at[:, 0:cut], first_h, sems.at[0]),
        pltpu.make_async_copy(d_gate.at[:, cut:width], rest_h, sems.at[3]),
        pltpu.make_async_copy(d_up, up_h, sems.at[1]),
    ]
    loads, loads2 = [], []
    for j in range(4):
        a, b = pl.ds(here[j], size), pl.ds(there[j], size)
        loads.append(pltpu.make_async_copy(pieces[j], normed.at[a], sems.at[48 + j]))
        loads2.append(pltpu.make_async_copy(dh_h.at[b], dh.at[a], sems.at[52 + j]))
        stores.append(pltpu.make_async_copy(hidden.at[a], hidden_h.at[b], sems.at[56 + j]))
    copies, views = staged(gate_w, 0, place[0], w1, sems.at[pl.ds(4, 6)])
    copies2, views2 = staged(up_w, 0, place[0], w2, sems.at[pl.ds(10, 6)])
    copies = copies + copies2
    begin(loads + copies[:2])
    wait(loads)
    begin(copies[2:4])
    store = pltpu.make_async_copy(normed.at[:, 0 : own_h.shape[1]], own_h, sems.at[2])
    store.start()
    for i, (view, start, rows) in enumerate(views + views2):
        wait(copies[i : i + 1])
        begin(copies[i + 4 : i + 5])
        if i == 6:
            begin(loads2)
        acc = gate if i < 6 else up
        value = nn(normed[:, lanes(start, rows)], view[...])
        acc[...] = value if i % 6 == 0 else acc[...] + value
    wait(loads2)

    def act(n, _):
        at = pl.ds(pl.multiple_of(n * LANES, LANES), LANES)
        one, two, grad = gate[:, at], up[:, at], dh[:, at]
        sig = 1.0 / (1.0 + jnp.exp(-one))
        silu = one * sig
        hidden[:, at] = (silu * two).astype(HALF)
        d_gate[:, at] = (grad * two * sig * (1.0 + one * (1.0 - sig))).astype(HALF)
        d_up[:, at] = (grad * silu).astype(HALF)
        return 0

    lax.fori_loop(0, width // LANES, act, 0)
    begin(stores)

    def back(at):
        return nt(d_gate[...], w1[at, :]) + nt(d_up[...], w2[at, :])

    backwards(back, part, parts_h, here, place[0], sems.at[pl.ds(16, 32)])
    wait(stores + [store])


def norm_back(grad_normed, values, gain):
    mean, inverse = stats(values)
    centred = (values - mean) * inverse
    scaled = grad_normed * gain
    total = jnp.mean(scaled, 1, keepdims=True)
    cross = jnp.mean(scaled * centred, 1, keepdims=True)
    back = inverse * (scaled - total - centred * cross)
    return (
        back,
        jnp.sum(grad_normed * centred, 0, keepdims=True),
        jnp.sum(grad_normed, 0, keepdims=True),
    )


def second_back_kernel(g0, g1, g2, g3, resid_h, own_h, keep_h, rounded_h, d_resid_h, part, resid, own, keep, d_resid, rounded, sems):
    chunk = resid.shape[0]
    loads = [
        pltpu.make_async_copy(a, b, sems.at[i])
        for i, (a, b) in enumerate(((resid_h, resid), (own_h, own), (keep_h, keep)))
    ]
    loads.append(pltpu.make_async_copy(g0, part, sems.at[5]))
    stores = [
        pltpu.make_async_copy(rounded, rounded_h, sems.at[3]),
        pltpu.make_async_copy(d_resid, d_resid_h, sems.at[4]),
    ]
    begin(loads)
    grad = received((g1, g2, g3))
    wait(loads)
    grad = grad + part[...].astype(FULL)
    back, gain, shift = norm_back(grad, resid[...], keep[chunk + 2 : chunk + 3])
    total = own[...].astype(FULL) + back
    rounded[...] = total.astype(HALF)
    stores[0].start()
    d_resid[0:chunk] = total
    row = lax.broadcasted_iota(jnp.int32, (8, gain.shape[1]), 0)
    d_resid[chunk : chunk + 8] = jnp.where(row == 2, gain, jnp.where(row == 3, shift, 0.0))
    stores[1].start()
    wait(stores)


def attention_back_kernel(place, *refs):
    pieces, (qkv_h, attn_h, lse_h, tables_h) = refs[0:4], refs[4:8]
    qkv_w, proj_w = refs[8:18], refs[18:22]
    d_qkv_h, parts_h = refs[22], refs[23:27]
    rounded, d_attn, d_qkv, wa, wb, w2, qkv, attn, lse, tables, part, sems = refs[27:]
    tokens = rounded.shape[0]
    rows = chunks(place, tokens)
    loads0 = [
        pltpu.make_async_copy(pieces[j], rounded.at[pl.ds(rows[j], tokens // 4)], sems.at[47 + j])
        for j in range(4)
    ]
    head_cols = attn.shape[1]
    store = pltpu.make_async_copy(d_qkv, d_qkv_h, sems.at[0])
    copies2, views2 = staged(proj_w, 1, place[0], w2, sems.at[pl.ds(1, 4)])
    copies, _, middle = staged_halves(qkv_w, place[0], wa, wb, sems, 51)
    loads = [
        pltpu.make_async_copy(a, b, sems.at[11 + i])
        for i, (a, b) in enumerate(
            ((qkv_h, qkv), (attn_h, attn), (lse_h, lse), (tables_h, tables))
        )
    ]
    begin(loads0 + copies2 + loads)
    wait(loads0 + copies2)
    begin(copies)
    d_attn[...] = added(
        nt(rounded[:, lanes(start, size)], view[...]) for view, start, size in views2
    ).astype(HALF)
    wait(loads)
    mask = causal(tokens)
    lane = lax.broadcasted_iota(jnp.int32, (tokens, LANES), 1)

    def pair(p, _):
        at = [pl.ds(pl.multiple_of(j * head_cols + p * LANES, LANES), LANES) for j in range(3)]
        query, keys, values = [qkv[:, a] for a in at]
        grad = d_attn[:, at[0]]
        product = grad.astype(FULL) * attn[:, at[0]].astype(FULL)
        dq, dk, dv = [], [], []
        for h in range(PAIR):
            delta = jnp.sum(own_half(product, h), 1, keepdims=True)
            total = jnp.sum(jnp.where(lane == p * PAIR + h, lse[...], 0.0), 1, keepdims=True)
            scores = jnp.where(mask, nt(own_half(query, h), keys) * SCALE, -1e30)
            weights = jnp.exp(scores - total)
            d_probs = nt(own_half(grad, h), values)
            d_scores = (weights * (d_probs - delta)).astype(HALF)
            dq.append(nn(d_scores, keys))
            dk.append(tn(d_scores, query))
            dv.append(tn(weights.astype(HALF), grad))
        dq = either(*dq) * SCALE
        dk = either(*dk) * SCALE
        d_qkv[:, at[0]] = turn(dq, tables[0], -tables[1], -tables[2]).astype(HALF)
        d_qkv[:, at[1]] = turn(dk, tables[0], -tables[1], -tables[2]).astype(HALF)
        d_qkv[:, at[2]] = either(*dv).astype(HALF)
        return 0

    lax.fori_loop(0, head_cols // LANES, pair, 0, unroll=2)
    store.start()
    wait(copies)

    def back(at):
        return nt(d_qkv[:, 0:middle], wa[at, :]) + nt(d_qkv[:, middle:], wb[at, :])

    backwards(back, part, parts_h, rows, place[0], sems.at[pl.ds(15, 32)])
    store.wait()


def split_low(value, out, at):
    high = value.astype(HALF)
    out[at : at + 8, :] = high
    out[at + 8 : at + 16, :] = (value - high.astype(FULL)).astype(HALF)


def first_back_kernel(g0, g1, g2, g3, d_resid_h, keep_h, out, part, d_resid, keep, sems):
    chunk = out.shape[0] - 16
    loads = [
        pltpu.make_async_copy(d_resid_h, d_resid, sems.at[0]),
        pltpu.make_async_copy(keep_h, keep, sems.at[1]),
        pltpu.make_async_copy(g0, part, sems.at[2]),
    ]
    begin(loads)
    grad = received((g1, g2, g3))
    wait(loads)
    grad = grad + part[...].astype(FULL)
    back, gain, shift = norm_back(grad, keep[0:chunk], keep[chunk : chunk + 1])
    out[0:chunk, :] = (d_resid[0:chunk] + back).astype(HALF)
    sums = d_resid[chunk : chunk + 8]
    row = lax.broadcasted_iota(jnp.int32, sums.shape, 0)
    split_low(jnp.where(row == 0, gain, jnp.where(row == 1, shift, sums)), out, chunk)


def pack_kernel(place, g0, g1, g2, g3, out):
    blocks = (g0, g1, g2, g3)
    chunk = g0.shape[0] - 16
    total = added(
        g[chunk : chunk + 8, :].astype(FULL) + g[chunk + 8 : chunk + 16, :].astype(FULL)
        for g in blocks
    )
    for k, g in enumerate(blocks):
        at = place[1] ^ k
        out[at, 0:chunk, :] = g[0:chunk, :]
        split_low(total, out.at[at], chunk)


def down_grad_kernel(place, *refs):
    hidden, groups, out_h = refs[0:8], refs[8:10], refs[10]
    left, turned, right, out, sems = refs[11:]
    rows, width = hidden[0].shape
    bases = (place[0] * 4, 4 - place[0] * 4)
    loads = [pltpu.make_async_copy(hidden[n], left.at[n], sems.at[n]) for n in range(8)]
    loads2 = [
        pltpu.make_async_copy(
            groups[n // 4].at[n % 4],
            right.at[pl.ds(pl.multiple_of((bases[n // 4] + n % 4) * rows, rows), rows)],
            sems.at[8 + n],
        )
        for n in range(8)
    ]
    begin(loads[:4])
    for n in range(8):
        wait(loads[n : n + 1])
        begin(loads[n + 4 : n + 5])
        begin(loads2[n : n + 1])
        at = pl.ds(pl.multiple_of((bases[n // 4] + n % 4) * rows, rows), rows)
        turned[:, at] = left[n].T
    wait(loads2)
    size = width // 4

    def store(n):
        at = pl.ds(pl.multiple_of(n * size, 16), size)
        return pltpu.make_async_copy(out.at[at], out_h.at[at], sems.at[16 + n])

    def product(n, _):
        at = pl.ds(pl.multiple_of(n * size, 16), size)
        out[at, :] = nn(turned[at, :], right[...])
        store(n).start()
        return 0

    lax.fori_loop(0, 4, product, 0)
    wait([store(n) for n in range(4)])


def weight_grad_kernel(ones, tile, mixed, place, *refs):
    lefts, rights, out_h = refs[0:4], refs[4:8], refs[8]
    left, turned, right, out, sems = refs[9:]
    rows, width = lefts[0].shape
    cols = right.shape[1]
    size = rows // 4
    loads = []
    for k in range(4):
        if mixed:
            here, there = chunks(place, rows, False), chunks(place, rows)
            loads.append(
                [
                    pltpu.make_async_copy(
                        lefts[k].at[pl.ds(there[j], size)],
                        left.at[k, pl.ds(here[j], size)],
                        sems.at[k, j],
                    )
                    for j in range(4)
                ]
            )
        else:
            loads.append([pltpu.make_async_copy(lefts[k], left.at[k], sems.at[k, 0])])
    loads2 = [
        pltpu.make_async_copy(rights[k], right.at[pl.ds(k * rows, rows)], sems.at[4, k])
        for k in range(4)
    ]
    for copies in loads:
        begin(copies)
    begin(loads2)
    for k in range(4):
        wait(loads[k])
        turned[:, k * rows : (k + 1) * rows] = left[k].T
    wait(loads2)

    def store(at, size, n):
        return pltpu.make_async_copy(
            out.at[:, pl.ds(at, size)], out_h.at[:, pl.ds(at, size)], sems.at[5, n]
        )

    def product(at, size):
        n = at // tile
        at = pl.ds(at, size)
        out[0:width, at] = nn(turned[...], right[:, at]).astype(HALF)
        if ones:
            total = jnp.sum(right[:, at].astype(FULL), 0, keepdims=True)
            high = total.astype(HALF).astype(FULL)
            row = lax.broadcasted_iota(jnp.int32, (16, size), 0)
            out[width : width + 16, at] = jnp.where(row < 8, high, total - high).astype(HALF)
        store(at.start, size, n).start()

    tiles(cols, tile, product)
    for at in range(0, cols, tile):
        store(at, min(tile, cols - at), at // tile).wait()


def unpack_kernel(*refs):
    ins, (grad_h, out_h, vec_h) = refs[0:6], refs[6:9]
    packed, own, leaf, grad, out, vec, sems = refs[9:]
    targets = [packed, own] + [leaf.at[j] for j in range(4)]
    loads = [pltpu.make_async_copy(a, b, sems.at[i]) for i, (a, b) in enumerate(zip(ins, targets))]
    stores = [
        pltpu.make_async_copy(a, b, sems.at[6 + i])
        for i, (a, b) in enumerate(((vec, vec_h), (grad, grad_h), (out, out_h)))
    ]
    begin(loads)
    wait(loads)
    chunk = packed.shape[1] - 16
    vec[...] = added(
        packed[s, chunk : chunk + 8, :].astype(FULL) + packed[s, chunk + 8 : chunk + 16, :].astype(FULL)
        for s in range(4)
    )
    stores[0].start()
    for s in range(4):
        grad[s * chunk : (s + 1) * chunk, :] = packed[s, 0:chunk, :].astype(FULL)
    stores[1].start()
    out[...] = own[...].astype(FULL) + added(leaf[j].astype(FULL) for j in range(4))
    stores[2].start()
    wait(stores)


def total_kernel(axis, *refs):
    out = refs[-1]
    width = out.shape[2]
    at = 0
    for mine, other in zip(refs[0:-1:2], refs[1:-1:2]):
        done = 0
        while done < mine.shape[1]:
            part, lane = divmod(at + done, width)
            size = min(width - lane, mine.shape[1] - done)
            here, there = slice(done, done + size), slice(lane, lane + size)
            value = mine[:, here].astype(FULL) + other[:, here].astype(FULL)
            if axis == 1:
                out[:, part, there] = value
            else:
                out[part, :, there] = value
            done += size
        at += done


def leaf_kernel(place, *refs):
    attn, hidden = refs[0:4], refs[4:8]
    proj_h, down_h = refs[8:10]
    outs = refs[10:14]
    w1, w2, left, left2, out, sems = refs[14:]
    apart = place[1] ^ place[2]
    loads = [
        pltpu.make_async_copy(proj_h, w1, sems.at[0]),
        pltpu.make_async_copy(down_h, w2, sems.at[1]),
    ]
    for k in range(4):
        loads.append(pltpu.make_async_copy(attn[k], left.at[apart ^ k], sems.at[2 + 2 * k]))
        loads.append(pltpu.make_async_copy(hidden[k], left2.at[apart ^ k], sems.at[3 + 2 * k]))
    begin(loads)
    wait(loads)
    stores = [pltpu.make_async_copy(out.at[k], outs[k], sems.at[10 + k]) for k in range(4)]
    for k in range(4):
        out[k] = (nn(left[k], w1[...]) + nn(left2[k], w2[...])).astype(HALF)
        stores[k].start()
    wait(stores)


VM = pl.BlockSpec(memory_space=pltpu.VMEM)
SM = pl.BlockSpec(memory_space=pltpu.SMEM)
HB = pl.BlockSpec(memory_space=pltpu.HBM)
AN = pl.BlockSpec(memory_space=pl.ANY)
FOUR = [HB, AN, HB, AN]
SIX = [HB, AN, HB, HB, AN, AN]


def call(kernel, specs, outs, args, scratch=(), flops=0, limit=None):
    moved = sum(a.size * a.dtype.itemsize for a in args)
    moved += sum(math.prod(s) * jnp.dtype(t).itemsize for s, t, _ in outs)
    return pl.pallas_call(
        kernel,
        out_shape=[pltpu.HBM(s, t) if m is HB else jax.ShapeDtypeStruct(s, t) for s, t, m in outs],
        in_specs=specs,
        out_specs=[m for _, _, m in outs],
        scratch_shapes=list(scratch),
        compiler_params=pltpu.CompilerParams(vmem_limit_bytes=limit),
        cost_estimate=pl.CostEstimate(flops=flops, bytes_accessed=moved, transcendentals=0),
    )(*[
        pltpu.with_memory_space_constraint(a, pltpu.HBM) if m is HB else a
        for a, m in zip(args, specs, strict=True)
    ])


def weight_grad(place, lefts, rights, ones=False, tile=256, mixed=False):
    rows, width = lefts[0].shape
    cols = rights[0].shape[1]
    high = width + (16 if ones else 0)
    size = 2 * (8 * rows * width + 4 * rows * cols + high * cols)
    (out,) = call(
        functools.partial(weight_grad_kernel, ones, tile, mixed),
        [SM] + FOUR + FOUR,
        [((high, cols), HALF, HB)],
        [place, *lefts, *rights],
        [
            pltpu.VMEM((4, rows, width), HALF),
            pltpu.VMEM((width, 4 * rows), HALF),
            pltpu.VMEM((4 * rows, cols), HALF),
            pltpu.VMEM((high, cols), HALF),
            pltpu.SemaphoreType.DMA((6, max(4, -(-cols // tile)))),
        ],
        flops=8 * rows * width * cols,
        limit=size + 4 * MIB,
    )
    return out


def rotation_tables(length):
    half = ROT // 2
    lane = jnp.arange(LANES) % HD
    freqs = THETA ** (-2.0 * (lane % half).astype(FULL) / ROT)
    angles = jnp.arange(length, dtype=FULL)[:, None] * freqs[None, :]
    cos_t = jnp.where(lane < ROT, jnp.cos(angles), 1.0)
    sin_t = jnp.sin(angles)
    down = jnp.where(lane < half, -sin_t, 0.0)
    up = jnp.where((lane >= half) & (lane < ROT), sin_t, 0.0)
    return jnp.stack([cos_t, down, up])


def bias_mask(width):
    lanes = jnp.arange(width) % HD < ROT
    ones = jnp.ones((width,), FULL)
    return jnp.stack([ones, jnp.where(lanes, 1.0, 0.0).astype(FULL), ones])


def block(
    block_in,
    norm1_gain,
    norm1_bias,
    w_qkv,
    qkv_bias,
    w_proj,
    norm2_gain,
    norm2_bias,
    w_gateup,
    w_down,
    out_grad,
):
    rows = lax.axis_size(ROW)
    cols = lax.axis_size(COL)
    col = lax.axis_index(COL)
    row = lax.axis_index(ROW)
    odd = lax.axis_index(DP) % 2
    two = lax.axis_size(DP) == 2
    feats = w_qkv.shape[0]
    head_cols = w_qkv.shape[2]
    width = w_gateup.shape[2]
    tokens = block_in.shape[0]
    chunk = tokens // cols
    wide = rows * feats
    place = jnp.stack([odd, row, col, odd]).astype(jnp.int32)
    tables = rotation_tables(SEQ)

    def narrow(value):
        return [value[:, k * feats : (k + 1) * feats] for k in range(rows)]

    own_qkv = w_qkv.reshape(feats, 3 * head_cols)
    own_inner = w_gateup.reshape(feats, 2 * width)
    in_group = col_swaps([block_in] * 4)
    qkv_half = half_of(own_qkv)
    middle = 3 * head_cols // 2
    qkv_w = [own_qkv, swap(own_qkv, ROW, 1)]
    qkv_w += across(qkv_half[:, :middle]) + across(qkv_half[:, middle:])
    proj_w = row_gather(w_proj)
    beside = swap(own_inner, ROW, 1)
    inner_w = [own_inner, beside]
    gate_half, up_half, down_half = call(
        halves_kernel,
        [SM, HB, HB],
        [((feats // 2, width), HALF, HB)] * 2 + [((width, feats // 2), HALF, HB)],
        [place, own_inner, w_down],
        [
            pltpu.VMEM((2, feats // 2, width), HALF),
            pltpu.VMEM((width, feats // 2), HALF),
            pltpu.SemaphoreType.DMA((6,)),
        ],
        limit=4 * MIB,
    )
    down_w = [w_down, swap(w_down, ROW, 1), *across(down_half)]
    inner_w += across(gate_half) + across(up_half)
    scales = jnp.concatenate(
        [jnp.stack([norm1_gain, norm1_bias, norm2_gain, norm2_bias]), jnp.zeros((4, feats), FULL)], 0
    )
    high = lax.reduce_precision(scales, 8, 7)
    packed = jnp.concatenate([high.astype(HALF), (scales - high).astype(HALF)], 0)

    def sort(blocks, below):
        high = tokens + sum(b.shape[0] for b in below)
        *outs, every = call(
            sort_kernel,
            [SM] + [AN] * (4 + len(below)),
            [((high, feats), HALF, HB)] * 3 + [((rows, high, feats), HALF, HB)],
            [place, *blocks, *below],
            [pltpu.VMEM((rows, high, feats), HALF), pltpu.SemaphoreType.DMA((12,))],
            limit=4 * MIB,
        )
        return outs, every

    outs, x_own = sort(in_group, [packed])
    x = [x_own] + row_exchange([x_own] + outs)[1:]
    outs, grad_group = sort(col_swaps([out_grad] * 4), [])
    grad_seq = [grad_group] + row_exchange([grad_group] + outs)[1:]

    normed1, qkv, attn, lse, keep, *parts = call(
        attention_kernel,
        [SM] + [HB] * 13 + [AN] + [HB] * 4 + [VM] * 2,
        [
            ((tokens, wide), HALF, HB),
            ((tokens, 3 * head_cols), HALF, HB),
            ((tokens, head_cols), HALF, HB),
            ((tokens, LANES), FULL, HB),
            ((chunk + 8, wide), FULL, HB),
            *[((chunk, wide), HALF, HB)] * 4,
        ],
        [place, *x, *qkv_w, *proj_w, qkv_bias.reshape(1, 3 * head_cols), tables],
        [
            pltpu.VMEM((tokens, wide), HALF),
            pltpu.VMEM((tokens, 3 * head_cols), FULL),
            pltpu.VMEM((4, tokens + 16, feats), HALF),
            pltpu.VMEM((wide, middle), HALF),
            pltpu.VMEM((wide, middle), HALF),
            pltpu.VMEM((head_cols, wide), HALF),
            pltpu.VMEM((tokens, 3 * head_cols), HALF),
            pltpu.VMEM((tokens, head_cols), HALF),
            pltpu.VMEM((tokens, LANES), FULL),
            pltpu.VMEM((tokens, wide), HALF),
            pltpu.VMEM((chunk + 8, wide), FULL),
            pltpu.SemaphoreType.DMA((47,)),
        ],
        flops=2 * tokens * wide * 4 * head_cols,
        limit=20 * MIB,
    )
    normed2, resid = call(
        second_norm_kernel,
        [HB] + [VM] * 3 + [HB],
        [((chunk, wide), HALF, HB), ((chunk, wide), FULL, HB)],
        [*col_swaps(parts), keep],
        [
            pltpu.VMEM((chunk, wide), HALF),
            pltpu.VMEM((chunk + 8, wide), FULL),
            pltpu.VMEM((chunk, wide), FULL),
            pltpu.VMEM((chunk, wide), HALF),
            pltpu.SemaphoreType.DMA((4,)),
        ],
        limit=8 * MIB,
    )
    normed2 = col_swaps([normed2] * 4)
    d_hidden, own_grad = call(
        down_kernel,
        [SM] + FOUR + SIX,
        [((tokens, width), FULL, HB), ((chunk, wide), HALF, HB)],
        [place, *grad_seq, *down_w],
        [
            pltpu.VMEM((tokens, width), FULL),
            pltpu.VMEM((tokens, wide), HALF),
            pltpu.VMEM((width, wide), HALF),
            pltpu.VMEM((chunk, wide), HALF),
            pltpu.SemaphoreType.DMA((12,)),
        ],
        flops=2 * tokens * wide * width,
        limit=12 * MIB,
    )
    cut = 6 * LANES
    hidden, d_first, d_rest, d_up, own_normed2, *parts = call(
        mlp_kernel,
        [SM, HB] + [AN] * 3 + [HB] + SIX + SIX[2:],
        [
            ((tokens, width), HALF, HB),
            ((tokens, cut), HALF, HB),
            ((tokens, width - cut), HALF, HB),
            ((tokens, width), HALF, HB),
            ((tokens, feats), HALF, HB),
            *[((chunk, wide), HALF, HB)] * 4,
        ],
        [place, *normed2, d_hidden, *inner_w],
        [
            pltpu.VMEM((tokens, wide), HALF),
            pltpu.VMEM((tokens, width), FULL),
            pltpu.VMEM((tokens, width), FULL),
            pltpu.VMEM((wide, width), HALF),
            pltpu.VMEM((wide, width), HALF),
            pltpu.VMEM((tokens, width), HALF),
            pltpu.VMEM((tokens, width), HALF),
            pltpu.VMEM((tokens, width), HALF),
            pltpu.VMEM((tokens, width), FULL),
            pltpu.VMEM((tokens, wide), HALF),
            pltpu.SemaphoreType.DMA((60,)),
        ],
        flops=2 * tokens * wide * 4 * width,
        limit=28 * MIB,
    )
    rounded, d_resid = call(
        second_back_kernel,
        [HB] + [VM] * 3 + [HB] * 3,
        [((chunk, wide), HALF, HB), ((chunk + 8, wide), FULL, HB)],
        [*col_swaps(parts), resid, own_grad, keep],
        [
            pltpu.VMEM((chunk, wide), HALF),
            pltpu.VMEM((chunk, wide), FULL),
            pltpu.VMEM((chunk, wide), HALF),
            pltpu.VMEM((chunk + 8, wide), FULL),
            pltpu.VMEM((chunk + 8, wide), FULL),
            pltpu.VMEM((chunk, wide), HALF),
            pltpu.SemaphoreType.DMA((6,)),
        ],
        limit=8 * MIB,
    )
    rounded = col_swaps([rounded] * 4)
    d_qkv, *parts = call(
        attention_back_kernel,
        [SM, HB] + [AN] * 3 + [HB] * 18,
        [((tokens, 3 * head_cols), HALF, HB), *[((chunk, wide), HALF, HB)] * 4],
        [place, *rounded, qkv, attn, lse, tables, *qkv_w, *proj_w],
        [
            pltpu.VMEM((tokens, wide), HALF),
            pltpu.VMEM((tokens, head_cols), HALF),
            pltpu.VMEM((tokens, 3 * head_cols), HALF),
            pltpu.VMEM((wide, middle), HALF),
            pltpu.VMEM((wide, middle), HALF),
            pltpu.VMEM((head_cols, wide), HALF),
            pltpu.VMEM((tokens, 3 * head_cols), HALF),
            pltpu.VMEM((tokens, head_cols), HALF),
            pltpu.VMEM((tokens, LANES), FULL),
            pltpu.VMEM((3, tokens, LANES), FULL),
            pltpu.VMEM((tokens, wide), HALF),
            pltpu.SemaphoreType.DMA((63,)),
        ],
        flops=2 * tokens * wide * 5 * head_cols,
        limit=18 * MIB,
    )
    (last,) = call(
        first_back_kernel,
        [HB] + [VM] * 3 + [HB] * 2,
        [((chunk + 16, wide), HALF, VM)],
        [*col_swaps(parts), d_resid, keep],
        [
            pltpu.VMEM((chunk, wide), HALF),
            pltpu.VMEM((chunk + 8, wide), FULL),
            pltpu.VMEM((chunk + 8, wide), FULL),
            pltpu.SemaphoreType.DMA((3,)),
        ],
        limit=8 * MIB,
    )

    got = row_exchange(narrow(last))
    (packed,) = call(
        pack_kernel,
        [SM] + [VM] * 4,
        [((rows, chunk + 16, feats), HALF, VM)],
        [place, *got],
        limit=4 * MIB,
    )
    got = col_exchange(packed)
    attn_group = row_gather(attn)
    normed_group = row_exchange(narrow(normed1))

    def blocks_of(pieces):
        return [jnp.concatenate(b, 0) for b in zip(*[narrow(p) for p in pieces])]

    normed2_group = [own_normed2] + row_exchange(blocks_of(normed2))[1:]
    hidden_group = row_gather(hidden)
    first_group = row_gather(d_first)
    rest_group = row_gather(d_rest)
    up_group = row_gather(d_up)
    first_mine = weight_grad(place, normed2_group, first_group)
    rest_mine = weight_grad(place, normed2_group, rest_group)
    up_mine = weight_grad(place, normed2_group, up_group)
    if two:
        other_group = row_gather(swap(hidden, DP, 1))
        (grad_down,) = call(
            down_grad_kernel,
            [SM] + FOUR + FOUR + [HB] * 2,
            [((width, feats), FULL, HB)],
            [place, *hidden_group, *other_group, grad_group, swap(grad_group, DP, 1)],
            [
                pltpu.VMEM((8, tokens, width), HALF),
                pltpu.VMEM((width, 8 * tokens), HALF),
                pltpu.VMEM((8 * tokens, feats), HALF),
                pltpu.VMEM((width, feats), FULL),
                pltpu.SemaphoreType.DMA((20,)),
            ],
            flops=16 * tokens * width * feats,
            limit=22 * MIB,
        )
        pairs = [
            (first_mine, swap(first_mine, DP, 1)),
            (rest_mine, swap(rest_mine, DP, 1)),
            (up_mine, swap(up_mine, DP, 1)),
        ]
        grad_gateup = total(pairs, (feats, 2, width))
    else:
        grads = [grad_group[k] for k in range(rows)]
        grad_down = over_groups(weight_grad(place, hidden_group, grads))
        mine = jnp.concatenate([first_mine, rest_mine, up_mine], 1)
        grad_gateup = over_groups(mine).reshape(feats, 2, width)
    leaf = call(
        leaf_kernel,
        [SM] + FOUR + FOUR + [HB] * 2,
        [((tokens, feats), HALF, HB)] * 4,
        [place, *attn_group, *hidden_group, w_proj, w_down],
        [
            pltpu.VMEM((head_cols, feats), HALF),
            pltpu.VMEM((width, feats), HALF),
            pltpu.VMEM((4, tokens, head_cols), HALF),
            pltpu.VMEM((4, tokens, width), HALF),
            pltpu.VMEM((4, tokens, feats), HALF),
            pltpu.SemaphoreType.DMA((14,)),
        ],
        flops=2 * rows * tokens * feats * (head_cols + width),
        limit=12 * MIB,
    )
    leaf = [leaf[0], swap(leaf[1], COL, 1), swap(leaf[2], COL, 2), swap(leaf[3], COL, 3)]
    grad_in, block_out, vectors = call(
        unpack_kernel,
        [AN, HB, HB, AN, AN, AN],
        [((tokens, feats), FULL, HB), ((tokens, feats), FULL, HB), ((8, feats), FULL, HB)],
        [got, block_in, *leaf],
        [
            pltpu.VMEM((rows, chunk + 16, feats), HALF),
            pltpu.VMEM((tokens, feats), HALF),
            pltpu.VMEM((4, tokens, feats), HALF),
            pltpu.VMEM((tokens, feats), FULL),
            pltpu.VMEM((tokens, feats), FULL),
            pltpu.VMEM((8, feats), FULL),
            pltpu.SemaphoreType.DMA((9,)),
        ],
        limit=8 * MIB,
    )
    if two:
        vectors = vectors + swap(vectors, DP, 1)
    else:
        vectors = lax.psum(vectors, DP)

    rounded_group = row_exchange(blocks_of(rounded))
    proj_mine = weight_grad(place, attn_group, rounded_group, mixed=True)
    if two:
        proj_other = swap(proj_mine, DP, 1)
        grad_proj = total([(proj_mine, proj_other)], (1, head_cols, feats), 0)[0]
    else:
        grad_proj = over_groups(proj_mine)
    qkv_group = row_gather(d_qkv)
    mine = weight_grad(place, normed_group, qkv_group, True)
    if two:
        other = swap(mine, DP, 1)
        grad_qkv = total([(mine, other)], (3, feats, head_cols), 0).swapaxes(0, 1)
        both = mine[feats:].astype(FULL) + other[feats:].astype(FULL)
    else:
        both = lax.psum(mine.astype(FULL), DP)
        grad_qkv = both[:feats].reshape(feats, 3, head_cols)
        both = both[feats:]
    grad_bias = (both[0] + both[8]).reshape(3, head_cols) * bias_mask(head_cols)
    gain1_grad, bias1_grad, gain2_grad, bias2_grad = vectors[:4]
    return (
        block_out,
        grad_in,
        grad_qkv,
        grad_bias,
        grad_proj,
        gain1_grad,
        bias1_grad,
        gain2_grad,
        bias2_grad,
        grad_gateup,
        grad_down,
    )


def solution(mesh):
    return jax.shard_map(
        block,
        mesh=mesh,
        in_specs=(
            P((DP, COL), ROW),
            P(ROW),
            P(ROW),
            P(ROW, None, COL),
            P(None, COL),
            P(COL, ROW),
            P(ROW),
            P(ROW),
            P(ROW, None, COL),
            P(COL, ROW),
            P((DP, COL), ROW),
        ),
        out_specs=(
            P((DP, COL), ROW),
            P((DP, COL), ROW),
            P(ROW, None, COL),
            P(None, COL),
            P(COL, ROW),
            P(ROW),
            P(ROW),
            P(ROW),
            P(ROW),
            P(ROW, None, COL),
            P(COL, ROW),
        ),
        check_vma=False,
    )
```

```python
import functools
import math

import jax
import jax.numpy as jnp
from jax import lax
from jax.experimental import pallas as pl
from jax.experimental.pallas import tpu as pltpu
from jax.sharding import PartitionSpec as P


HD = 64
ROT = 16
SEQ = 256

EPS = 1e-05
THETA = 10000.0
SCALE = 1.0 / math.sqrt(HD)

HALF = jnp.bfloat16
FULL = jnp.float32
LANES = 128
PAIR = LANES // HD
MIB = 1 << 20


DP, ROW, COL = "dp", "row", "col"


def swap(value, axis, bit):
    size = lax.axis_size(axis)
    return lax.ppermute(value, axis, [(i, i ^ bit) for i in range(size)])


def row_exchange(blocks):
    return [blocks[0]] + [swap(blocks[k], ROW, k) for k in range(1, 4)]


def col_exchange(blocks):
    return lax.all_to_all(blocks, COL, 0, 0, tiled=True)


def col_swaps(blocks):
    there = {j: swap(blocks[j], COL, j) for j in (2, 3, 1)}
    return [blocks[0], there[1], there[2], there[3]]


def row_gather(local):
    across = swap(local, ROW, 2)
    beside = swap(local, ROW, 1)
    both = swap(across, ROW, 1)
    return [local, beside, across, both]


def across(mine):
    first = swap(mine, ROW, 2)
    second = swap(first, DP, 1)
    third = swap(first, ROW, 1)
    return [first, second, third, swap(second, ROW, 1)]


def half_of(weight):
    half = weight.shape[0] // 2
    odd = lax.axis_index(DP) % 2
    return lax.dynamic_slice_in_dim(weight, odd * half, half, 0)


def total(pairs, shape, axis=1, tile=128):
    rows = shape[1 - axis]
    block = (tile, *shape[1:]) if axis == 1 else (shape[0], tile, shape[2])
    parts = [part for pair in pairs for part in pair]
    return pl.pallas_call(
        functools.partial(total_kernel, axis),
        grid=(rows // tile,),
        out_shape=jax.ShapeDtypeStruct(shape, FULL),
        in_specs=[pl.BlockSpec((tile, p.shape[1]), lambda n: (n, 0)) for p in parts],
        out_specs=pl.BlockSpec(block, (lambda n: (n, 0, 0)) if axis == 1 else (lambda n: (0, n, 0))),
        compiler_params=pltpu.CompilerParams(vmem_limit_bytes=10 * MIB),
        cost_estimate=pl.CostEstimate(
            flops=math.prod(shape), bytes_accessed=8 * math.prod(shape), transcendentals=0
        ),
    )(*parts)


def over_groups(mine):
    return lax.psum(mine.astype(FULL), DP)


def places(refs, axis, odd):
    size = refs[0].shape[axis]
    if len(refs) == 4:
        return [(ref, k * size, size) for k, ref in enumerate(refs)]
    half = size // 2
    own, beside, first, second, first_b, second_b = refs
    near = pl.multiple_of(odd * half, LANES)
    far = pl.multiple_of((1 - odd) * half, LANES)
    return [
        (own, 0, size),
        (beside, size, size),
        (first, 2 * size + near, half),
        (second, 2 * size + far, half),
        (first_b, 3 * size + near, half),
        (second_b, 3 * size + far, half),
    ]


def staged(refs, axis, odd, buffer, sems):
    copies, views, at = [], [], 0
    for i, (ref, start, size) in enumerate(places(refs, axis, odd)):
        here = pl.ds(at, size)
        view = buffer.at[here] if axis == 0 else buffer.at[:, here]
        copies.append(pltpu.make_async_copy(ref, view, sems.at[i]))
        views.append((view, start, size))
        at += size
    return copies, views


def staged_halves(refs, odd, first, second, sems, at):
    middle = first.shape[1]
    copies, views = [], []
    for n, buffer in enumerate((first, second)):
        cols = slice(n * middle, (n + 1) * middle)
        parts = [ref.at[:, cols] for ref in refs[0:2]] + list(refs[2 + 4 * n : 6 + 4 * n])
        more, views2 = staged(parts, 0, odd, buffer, sems.at[pl.ds(at + 6 * n, 6)])
        copies += more
        views += views2
    return copies, views, middle


def lanes(at, size):
    return pl.ds(at if isinstance(at, int) else pl.multiple_of(at, LANES), size)


def added(terms):
    total = None
    for term in terms:
        total = term if total is None else total + term
    return total


def begin(copies):
    for copy in copies:
        copy.start()


def wait(copies):
    for copy in copies:
        copy.wait()


def nn(left, right):
    return lax.dot_general(left, right, (((1,), (0,)), ((), ())), preferred_element_type=FULL)


def nt(left, right):
    return lax.dot_general(left, right, (((1,), (1,)), ((), ())), preferred_element_type=FULL)


def tn(left, right):
    return lax.dot_general(left, right, (((0,), (0,)), ((), ())), preferred_element_type=FULL)


def tiles(extent, size, step):
    whole = extent // size

    def one(n, _):
        step(pl.multiple_of(n * size, size), size)
        return 0

    lax.fori_loop(0, whole, one, 0)
    if extent % size:
        step(whole * size, extent % size)


def turn(value, cos_t, down, up):
    return (
        value * cos_t
        + pltpu.roll(value, LANES - ROT // 2, 1) * down
        + pltpu.roll(value, ROT // 2, 1) * up
    )


def stats(values):
    mean = jnp.mean(values, 1, keepdims=True)
    second = jnp.mean(values * values, 1, keepdims=True)
    return mean, lax.rsqrt(second - mean * mean + EPS)


def causal(length):
    at = lax.broadcasted_iota(jnp.int32, (length, length), 0)
    return at >= lax.broadcasted_iota(jnp.int32, (length, length), 1)


def own_half(value, head):
    lane = lax.broadcasted_iota(jnp.int32, value.shape, 1)
    return jnp.where((lane < HD) == (head == 0), value, jnp.zeros_like(value))


def either(first, second):
    lane = lax.broadcasted_iota(jnp.int32, first.shape, 1)
    return jnp.where(lane < HD, first, second)


def backwards(product, part, outs, rows, odd, sems):
    size = part.shape[1] // 8

    def pieces(n):
        at = lanes(jnp.where(n < 4, n, n ^ odd) * size, size)
        return at, out_pieces(part, outs, rows, at, sems, 4 * n)

    def one(n, _):
        at, copies = pieces(n)
        part[:, at] = product(pl.ds(pl.multiple_of(n * size, size), size)).astype(HALF)
        begin(copies)
        return 0

    lax.fori_loop(0, 8, one, 0, unroll=2)
    for n in range(8):
        wait(pieces(n)[1])


def out_pieces(source, outs, rows, at, sems, first):
    size = outs[0].shape[0]
    return [
        pltpu.make_async_copy(
            source.at[pl.ds(rows[j], size), at], outs[j].at[:, at], sems.at[first + j]
        )
        for j in range(4)
    ]


def chunks(place, rows, apart=True):
    size = rows // 4
    if not apart:
        return [j * size for j in range(4)]
    return [pl.multiple_of((place[2] ^ j) * size, size) for j in range(4)]


def halves_kernel(place, inner, down, gate_h, up_h, down_h, wide, tall, sems):
    size, width = gate_h.shape
    at = pl.ds(pl.multiple_of(place[0] * size, size), size)
    loads = [
        pltpu.make_async_copy(down.at[:, at], tall, sems.at[0]),
        pltpu.make_async_copy(inner.at[at, 0:width], wide.at[0], sems.at[1]),
        pltpu.make_async_copy(inner.at[at, width : 2 * width], wide.at[1], sems.at[2]),
    ]
    stores = [
        pltpu.make_async_copy(tall, down_h, sems.at[3]),
        pltpu.make_async_copy(wide.at[0], gate_h, sems.at[4]),
        pltpu.make_async_copy(wide.at[1], up_h, sems.at[5]),
    ]
    begin(loads)
    for load, store in zip(loads, stores):
        load.wait()
        store.start()
    wait(stores)


def sort_kernel(place, *refs):
    blocks, below = refs[0:4], refs[4:-6]
    outs, every, both, sems = refs[-6:-3], refs[-3], refs[-2], refs[-1]
    apart = place[1] ^ place[2]
    rows = blocks[0].shape[0]
    loads = [
        pltpu.make_async_copy(blocks[j], both.at[apart ^ j, pl.ds(0, rows)], sems.at[j])
        for j in range(4)
    ]
    for ref in below:
        for k in range(4):
            at = pl.ds(rows, ref.shape[0])
            loads.append(pltpu.make_async_copy(ref, both.at[k, at], sems.at[4 + k]))
    begin(loads)
    wait(loads)
    stores = [pltpu.make_async_copy(both.at[k + 1], outs[k], sems.at[8 + k]) for k in range(3)]
    stores.append(pltpu.make_async_copy(both, every, sems.at[11]))
    begin(stores)
    wait(stores)


def attention_kernel(place, *refs):
    x = refs[0:4]
    qkv_w, proj_w = refs[4:14], refs[14:18]
    bias, tables = refs[18:20]
    normed_h, qkv_h, attn_h, lse_h, keep_h = refs[20:25]
    parts_h = refs[25:29]
    normed, raw, xs, wa, wb, w2, qkv, attn, lse, part, keep, sems = refs[29:]
    tokens, wide = normed.shape
    feats = wide // 4
    head_cols = attn.shape[1]
    store = pltpu.make_async_copy(normed, normed_h, sems.at[0])
    x = (x[0].at[0], *x[1:])
    loads = [pltpu.make_async_copy(x[k], xs.at[k], sems.at[1 + k]) for k in range(4)]
    copies, views, middle = staged_halves(qkv_w, place[0], wa, wb, sems, 35)
    copies2, views2 = staged(proj_w, 1, place[0], w2, sems.at[pl.ds(11, 4)])
    stores = [
        pltpu.make_async_copy(a, b, sems.at[15 + i])
        for i, (a, b) in enumerate(((qkv, qkv_h), (attn, attn_h), (lse, lse_h)))
    ]
    keeping = pltpu.make_async_copy(keep, keep_h, sems.at[18])
    chunk = keep.shape[0] - 8
    scales = keep.at[pl.ds(chunk, 8)]
    begin(loads + copies[:3])
    wait(loads)
    begin(copies[3:])
    for k in range(4):
        packed = xs[k, tokens : tokens + 16, :].astype(FULL)
        scales[:, k * feats : (k + 1) * feats] = packed[:8] + packed[8:]
    step = 32

    def norm(i, _):
        at = pl.ds(pl.multiple_of(i * step, step), step)
        values = jnp.concatenate([xs[k, at, :].astype(FULL) for k in range(4)], 1)
        mean, inverse = stats(values)
        normed[at, :] = ((values - mean) * inverse * scales[0:1] + scales[1:2]).astype(HALF)
        return 0

    lax.fori_loop(0, tokens // step, norm, 0)
    store.start()
    at = pl.ds(pl.multiple_of(place[2] * chunk, chunk), chunk)
    for k in range(4):
        keep[0:chunk, k * feats : (k + 1) * feats] = xs[k, at, :].astype(FULL)
    keeping.start()
    for i, (view, start, rows) in enumerate(views):
        wait(copies[i : i + 1])
        at = slice(0, middle) if i < 6 else slice(middle, 2 * middle)
        value = nn(normed[:, lanes(start, rows)], view[...])
        raw[:, at] = value + (bias[:, at] if i % 6 == 0 else raw[:, at])
    begin(copies2)
    mask = causal(tokens)
    lane = lax.broadcasted_iota(jnp.int32, (tokens, LANES), 1)

    def pair(p, _):
        at = [pl.ds(pl.multiple_of(j * head_cols + p * LANES, LANES), LANES) for j in range(3)]
        query = turn(raw[:, at[0]], tables[0], tables[1], tables[2]).astype(HALF)
        keys = turn(raw[:, at[1]], tables[0], tables[1], tables[2]).astype(HALF)
        values = raw[:, at[2]].astype(HALF)
        qkv[:, at[0]] = query
        qkv[:, at[1]] = keys
        qkv[:, at[2]] = values
        outs = []
        for h in range(PAIR):
            scores = jnp.where(mask, nt(own_half(query, h), keys) * SCALE, -1e30)
            top = jnp.max(scores, 1, keepdims=True)
            raised = jnp.exp(scores - top)
            total = jnp.sum(raised, 1, keepdims=True)
            lse[...] = jnp.where(lane == p * PAIR + h, top + jnp.log(total), lse[...])
            outs.append(nn((raised * (1.0 / total)).astype(HALF), values))
        attn[:, at[0]] = either(*outs).astype(HALF)
        return 0

    lax.fori_loop(0, head_cols // LANES, pair, 0, unroll=2)
    begin(stores)
    wait(copies2)
    outs = []
    for i, (view, start, size) in enumerate(views2):
        part[:, lanes(start, size)] = nn(attn[...], view[...]).astype(HALF)
        pieces = out_pieces(
            part, parts_h, chunks(place, tokens), lanes(start, size), sems, 19 + 4 * i
        )
        begin(pieces)
        outs += pieces
    wait([store, keeping] + stores + outs)


def received(got):
    return added(g[...].astype(FULL) for g in got)


def second_norm_kernel(g0, g1, g2, g3, keep_h, normed_h, resid_h, own, keep, resid, normed, sems):
    chunk = resid.shape[0]
    loads = [
        pltpu.make_async_copy(keep_h, keep, sems.at[0]),
        pltpu.make_async_copy(g0, own, sems.at[3]),
    ]
    begin(loads)
    values = received((g1, g2, g3))
    wait(loads)
    values = values + keep[0:chunk] + own[...].astype(FULL)
    resid[...] = values
    stores = [
        pltpu.make_async_copy(resid, resid_h, sems.at[1]),
        pltpu.make_async_copy(normed, normed_h, sems.at[2]),
    ]
    stores[0].start()
    mean, inverse = stats(values)
    scales = keep[chunk : chunk + 8]
    normed[...] = ((values - mean) * inverse * scales[2:3] + scales[3:4]).astype(HALF)
    stores[1].start()
    wait(stores)


def down_kernel(place, *refs):
    g, down_w = refs[0:4], refs[4:-7]
    dh_h, own_h, dh, gs, w1, own, sems = refs[-7:]
    feats = g[1].shape[1]
    g = (g[0].at[0], *g[1:])
    loads = [
        pltpu.make_async_copy(g[k], gs.at[:, k * feats : (k + 1) * feats], sems.at[k])
        for k in range(4)
    ]
    copies, views = staged(down_w, 1, place[0], w1, sems.at[pl.ds(4, 6)])
    stores = [
        pltpu.make_async_copy(dh, dh_h, sems.at[10]),
        pltpu.make_async_copy(own, own_h, sems.at[11]),
    ]
    begin(loads + copies[:2])
    wait(loads)
    chunk = own.shape[0]
    own[...] = gs[pl.ds(pl.multiple_of(place[2] * chunk, chunk), chunk), :]
    stores[1].start()
    for i, (view, start, cols) in enumerate(views):
        wait(copies[i : i + 1])
        begin(copies[i + 2 : i + 3])
        value = nt(gs[:, lanes(start, cols)], view[...])
        dh[...] = value if i == 0 else dh[...] + value
    stores[0].start()
    wait(stores)


def mlp_kernel(place, *refs):
    pieces, dh_h = refs[0:4], refs[4]
    hidden_h, first_h, rest_h, up_h, own_h = refs[15:20]
    parts_h = refs[20:24]
    normed, gate, up, w1, w2, hidden, d_gate, d_up, dh, part, sems = refs[24:]
    cut = first_h.shape[1]
    tokens, width = hidden.shape
    gate_w = [ref.at[:, 0:width] for ref in refs[5:7]] + list(refs[7:11])
    up_w = [ref.at[:, width : 2 * width] for ref in refs[5:7]] + list(refs[11:15])
    here, there = chunks(place, tokens, False), chunks(place, tokens)
    size = tokens // 4
    stores = [
        pltpu.make_async_copy(d_gate.at[:, 0:cut], first_h, sems.at[0]),
        pltpu.make_async_copy(d_gate.at[:, cut:width], rest_h, sems.at[3]),
        pltpu.make_async_copy(d_up, up_h, sems.at[1]),
    ]
    loads, loads2 = [], []
    for j in range(4):
        a, b = pl.ds(here[j], size), pl.ds(there[j], size)
        loads.append(pltpu.make_async_copy(pieces[j], normed.at[a], sems.at[48 + j]))
        loads2.append(pltpu.make_async_copy(dh_h.at[b], dh.at[a], sems.at[52 + j]))
        stores.append(pltpu.make_async_copy(hidden.at[a], hidden_h.at[b], sems.at[56 + j]))
    copies, views = staged(gate_w, 0, place[0], w1, sems.at[pl.ds(4, 6)])
    copies2, views2 = staged(up_w, 0, place[0], w2, sems.at[pl.ds(10, 6)])
    copies = copies + copies2
    begin(loads + copies[:2])
    wait(loads)
    begin(copies[2:6])
    store = pltpu.make_async_copy(normed.at[:, 0 : own_h.shape[1]], own_h, sems.at[2])
    store.start()
    for i, (view, start, rows) in enumerate(views + views2):
        wait(copies[i : i + 1])
        begin(copies[i + 6 : i + 7])
        if i == 6:
            begin(loads2)
        acc = gate if i < 6 else up
        value = nn(normed[:, lanes(start, rows)], view[...])
        acc[...] = value if i % 6 == 0 else acc[...] + value
    wait(loads2)

    def act(n, _):
        at = pl.ds(pl.multiple_of(n * LANES, LANES), LANES)
        one, two, grad = gate[:, at], up[:, at], dh[:, at]
        sig = 1.0 / (1.0 + jnp.exp(-one))
        silu = one * sig
        hidden[:, at] = (silu * two).astype(HALF)
        d_gate[:, at] = (grad * two * sig * (1.0 + one * (1.0 - sig))).astype(HALF)
        d_up[:, at] = (grad * silu).astype(HALF)
        return 0

    lax.fori_loop(0, width // LANES, act, 0)
    begin(stores)

    def back(at):
        return nt(d_gate[...], w1[at, :]) + nt(d_up[...], w2[at, :])

    backwards(back, part, parts_h, here, place[0], sems.at[pl.ds(16, 32)])
    wait(stores + [store])


def norm_back(grad_normed, values, gain):
    mean, inverse = stats(values)
    centred = (values - mean) * inverse
    scaled = grad_normed * gain
    total = jnp.mean(scaled, 1, keepdims=True)
    cross = jnp.mean(scaled * centred, 1, keepdims=True)
    back = inverse * (scaled - total - centred * cross)
    return (
        back,
        jnp.sum(grad_normed * centred, 0, keepdims=True),
        jnp.sum(grad_normed, 0, keepdims=True),
    )


def second_back_kernel(g0, g1, g2, g3, resid_h, own_h, keep_h, rounded_h, d_resid_h, part, resid, own, keep, d_resid, rounded, sems):
    chunk = resid.shape[0]
    loads = [
        pltpu.make_async_copy(a, b, sems.at[i])
        for i, (a, b) in enumerate(((resid_h, resid), (own_h, own), (keep_h, keep)))
    ]
    loads.append(pltpu.make_async_copy(g0, part, sems.at[5]))
    stores = [
        pltpu.make_async_copy(rounded, rounded_h, sems.at[3]),
        pltpu.make_async_copy(d_resid, d_resid_h, sems.at[4]),
    ]
    begin(loads)
    grad = received((g1, g2, g3))
    wait(loads)
    grad = grad + part[...].astype(FULL)
    back, gain, shift = norm_back(grad, resid[...], keep[chunk + 2 : chunk + 3])
    total = own[...].astype(FULL) + back
    rounded[...] = total.astype(HALF)
    stores[0].start()
    d_resid[0:chunk] = total
    row = lax.broadcasted_iota(jnp.int32, (8, gain.shape[1]), 0)
    d_resid[chunk : chunk + 8] = jnp.where(row == 2, gain, jnp.where(row == 3, shift, 0.0))
    stores[1].start()
    wait(stores)


def attention_back_kernel(place, *refs):
    pieces, (qkv_h, attn_h, lse_h, tables_h) = refs[0:4], refs[4:8]
    qkv_w, proj_w = refs[8:18], refs[18:22]
    d_qkv_h, parts_h = refs[22], refs[23:27]
    rounded, d_attn, d_qkv, wa, wb, w2, qkv, attn, lse, tables, part, sems = refs[27:]
    tokens = rounded.shape[0]
    rows = chunks(place, tokens)
    loads0 = [
        pltpu.make_async_copy(pieces[j], rounded.at[pl.ds(rows[j], tokens // 4)], sems.at[47 + j])
        for j in range(4)
    ]
    head_cols = attn.shape[1]
    store = pltpu.make_async_copy(d_qkv, d_qkv_h, sems.at[0])
    copies2, views2 = staged(proj_w, 1, place[0], w2, sems.at[pl.ds(1, 4)])
    copies, _, middle = staged_halves(qkv_w, place[0], wa, wb, sems, 51)
    loads = [
        pltpu.make_async_copy(a, b, sems.at[11 + i])
        for i, (a, b) in enumerate(
            ((qkv_h, qkv), (attn_h, attn), (lse_h, lse), (tables_h, tables))
        )
    ]
    begin(loads0 + copies2 + loads)
    wait(loads0 + copies2)
    begin(copies)
    d_attn[...] = added(
        nt(rounded[:, lanes(start, size)], view[...]) for view, start, size in views2
    ).astype(HALF)
    wait(loads)
    mask = causal(tokens)
    lane = lax.broadcasted_iota(jnp.int32, (tokens, LANES), 1)

    def pair(p, _):
        at = [pl.ds(pl.multiple_of(j * head_cols + p * LANES, LANES), LANES) for j in range(3)]
        query, keys, values = [qkv[:, a] for a in at]
        grad = d_attn[:, at[0]]
        product = grad.astype(FULL) * attn[:, at[0]].astype(FULL)
        dq, dk, dv = [], [], []
        for h in range(PAIR):
            delta = jnp.sum(own_half(product, h), 1, keepdims=True)
            total = jnp.sum(jnp.where(lane == p * PAIR + h, lse[...], 0.0), 1, keepdims=True)
            scores = jnp.where(mask, nt(own_half(query, h), keys) * SCALE, -1e30)
            weights = jnp.exp(scores - total)
            d_probs = nt(own_half(grad, h), values)
            d_scores = (weights * (d_probs - delta)).astype(HALF)
            dq.append(nn(d_scores, keys))
            dk.append(tn(d_scores, query))
            dv.append(tn(weights.astype(HALF), grad))
        dq = either(*dq) * SCALE
        dk = either(*dk) * SCALE
        d_qkv[:, at[0]] = turn(dq, tables[0], -tables[1], -tables[2]).astype(HALF)
        d_qkv[:, at[1]] = turn(dk, tables[0], -tables[1], -tables[2]).astype(HALF)
        d_qkv[:, at[2]] = either(*dv).astype(HALF)
        return 0

    lax.fori_loop(0, head_cols // LANES, pair, 0, unroll=2)
    store.start()
    wait(copies)

    def back(at):
        return nt(d_qkv[:, 0:middle], wa[at, :]) + nt(d_qkv[:, middle:], wb[at, :])

    backwards(back, part, parts_h, rows, place[0], sems.at[pl.ds(15, 32)])
    store.wait()


def split_low(value, out, at):
    high = value.astype(HALF)
    out[at : at + 8, :] = high
    out[at + 8 : at + 16, :] = (value - high.astype(FULL)).astype(HALF)


def first_back_kernel(g0, g1, g2, g3, d_resid_h, keep_h, out, part, d_resid, keep, sems):
    chunk = out.shape[0] - 16
    loads = [
        pltpu.make_async_copy(d_resid_h, d_resid, sems.at[0]),
        pltpu.make_async_copy(keep_h, keep, sems.at[1]),
        pltpu.make_async_copy(g0, part, sems.at[2]),
    ]
    begin(loads)
    grad = received((g1, g2, g3))
    wait(loads)
    grad = grad + part[...].astype(FULL)
    back, gain, shift = norm_back(grad, keep[0:chunk], keep[chunk : chunk + 1])
    out[0:chunk, :] = (d_resid[0:chunk] + back).astype(HALF)
    sums = d_resid[chunk : chunk + 8]
    row = lax.broadcasted_iota(jnp.int32, sums.shape, 0)
    split_low(jnp.where(row == 0, gain, jnp.where(row == 1, shift, sums)), out, chunk)


def pack_kernel(place, g0, g1, g2, g3, out):
    blocks = (g0, g1, g2, g3)
    chunk = g0.shape[0] - 16
    total = added(
        g[chunk : chunk + 8, :].astype(FULL) + g[chunk + 8 : chunk + 16, :].astype(FULL)
        for g in blocks
    )
    for k, g in enumerate(blocks):
        at = place[1] ^ k
        out[at, 0:chunk, :] = g[0:chunk, :]
        split_low(total, out.at[at], chunk)


def down_grad_kernel(place, *refs):
    hidden, groups, out_h = refs[0:8], refs[8:10], refs[10]
    left, turned, right, out, sems = refs[11:]
    rows, width = hidden[0].shape
    bases = (place[0] * 4, 4 - place[0] * 4)
    loads = [pltpu.make_async_copy(hidden[n], left.at[n], sems.at[n]) for n in range(8)]
    loads2 = [
        pltpu.make_async_copy(
            groups[n // 4].at[n % 4],
            right.at[pl.ds(pl.multiple_of((bases[n // 4] + n % 4) * rows, rows), rows)],
            sems.at[8 + n],
        )
        for n in range(8)
    ]
    begin(loads[:4])
    for n in range(8):
        wait(loads[n : n + 1])
        begin(loads[n + 4 : n + 5])
        begin(loads2[n : n + 1])
        at = pl.ds(pl.multiple_of((bases[n // 4] + n % 4) * rows, rows), rows)
        turned[:, at] = left[n].T
    wait(loads2)
    size = width // 4

    def store(n):
        at = pl.ds(pl.multiple_of(n * size, 16), size)
        return pltpu.make_async_copy(out.at[at], out_h.at[at], sems.at[16 + n])

    def product(n, _):
        at = pl.ds(pl.multiple_of(n * size, 16), size)
        out[at, :] = nn(turned[at, :], right[...])
        store(n).start()
        return 0

    lax.fori_loop(0, 4, product, 0)
    wait([store(n) for n in range(4)])


def weight_grad_kernel(ones, tile, mixed, place, *refs):
    lefts, rights, out_h = refs[0:4], refs[4:8], refs[8]
    left, turned, right, out, sems = refs[9:]
    rows, width = lefts[0].shape
    cols = right.shape[1]
    size = rows // 4
    loads = []
    for k in range(4):
        if mixed:
            here, there = chunks(place, rows, False), chunks(place, rows)
            loads.append(
                [
                    pltpu.make_async_copy(
                        lefts[k].at[pl.ds(there[j], size)],
                        left.at[k, pl.ds(here[j], size)],
                        sems.at[k, j],
                    )
                    for j in range(4)
                ]
            )
        else:
            loads.append([pltpu.make_async_copy(lefts[k], left.at[k], sems.at[k, 0])])
    loads2 = [
        pltpu.make_async_copy(rights[k], right.at[pl.ds(k * rows, rows)], sems.at[4, k])
        for k in range(4)
    ]
    for copies in loads:
        begin(copies)
    begin(loads2)
    for k in range(4):
        wait(loads[k])
        turned[:, k * rows : (k + 1) * rows] = left[k].T
    wait(loads2)

    def store(at, size, n):
        return pltpu.make_async_copy(
            out.at[:, pl.ds(at, size)], out_h.at[:, pl.ds(at, size)], sems.at[5, n]
        )

    def product(at, size):
        n = at // tile
        at = pl.ds(at, size)
        out[0:width, at] = nn(turned[...], right[:, at]).astype(HALF)
        if ones:
            sums = [
                jnp.sum(right[k * rows : (k + 1) * rows, at].astype(FULL), 0, keepdims=True)
                for k in range(4)
            ]
            total = (sums[0] + sums[1]) + (sums[2] + sums[3])
            high = total.astype(HALF).astype(FULL)
            row = lax.broadcasted_iota(jnp.int32, (16, size), 0)
            out[width : width + 16, at] = jnp.where(row < 8, high, total - high).astype(HALF)
        store(at.start, size, n).start()

    tiles(cols, tile, product)
    for at in range(0, cols, tile):
        store(at, min(tile, cols - at), at // tile).wait()


def unpack_kernel(*refs):
    ins, (grad_h, out_h, vec_h) = refs[0:6], refs[6:9]
    packed, own, leaf, grad, out, vec, sems = refs[9:]
    targets = [packed, own] + [leaf.at[j] for j in range(4)]
    loads = [pltpu.make_async_copy(a, b, sems.at[i]) for i, (a, b) in enumerate(zip(ins, targets))]
    stores = [
        pltpu.make_async_copy(a, b, sems.at[6 + i])
        for i, (a, b) in enumerate(((vec, vec_h), (grad, grad_h), (out, out_h)))
    ]
    begin(loads)
    wait(loads)
    chunk = packed.shape[1] - 16
    vec[...] = added(
        packed[s, chunk : chunk + 8, :].astype(FULL) + packed[s, chunk + 8 : chunk + 16, :].astype(FULL)
        for s in range(4)
    )
    stores[0].start()
    for s in range(4):
        grad[s * chunk : (s + 1) * chunk, :] = packed[s, 0:chunk, :].astype(FULL)
    stores[1].start()
    out[...] = own[...].astype(FULL) + added(leaf[j].astype(FULL) for j in range(4))
    stores[2].start()
    wait(stores)


def total_kernel(axis, *refs):
    out = refs[-1]
    width = out.shape[2]
    at = 0
    for mine, other in zip(refs[0:-1:2], refs[1:-1:2]):
        done = 0
        while done < mine.shape[1]:
            part, lane = divmod(at + done, width)
            size = min(width - lane, mine.shape[1] - done)
            here, there = slice(done, done + size), slice(lane, lane + size)
            value = mine[:, here].astype(FULL) + other[:, here].astype(FULL)
            if axis == 1:
                out[:, part, there] = value
            else:
                out[part, :, there] = value
            done += size
        at += done


def leaf_kernel(place, *refs):
    attn, hidden = refs[0:4], refs[4:8]
    proj_h, down_h = refs[8:10]
    outs = refs[10:14]
    w1, w2, left, left2, out, sems = refs[14:]
    apart = place[1] ^ place[2]
    loads = [
        pltpu.make_async_copy(proj_h, w1, sems.at[0]),
        pltpu.make_async_copy(down_h, w2, sems.at[1]),
    ]
    for k in range(4):
        loads.append(pltpu.make_async_copy(attn[k], left.at[apart ^ k], sems.at[2 + 2 * k]))
        loads.append(pltpu.make_async_copy(hidden[k], left2.at[apart ^ k], sems.at[3 + 2 * k]))
    begin(loads)
    wait(loads)
    stores = [pltpu.make_async_copy(out.at[k], outs[k], sems.at[10 + k]) for k in range(4)]
    for k in range(4):
        out[k] = (nn(left[k], w1[...]) + nn(left2[k], w2[...])).astype(HALF)
        stores[k].start()
    wait(stores)


VM = pl.BlockSpec(memory_space=pltpu.VMEM)
SM = pl.BlockSpec(memory_space=pltpu.SMEM)
HB = pl.BlockSpec(memory_space=pltpu.HBM)
AN = pl.BlockSpec(memory_space=pl.ANY)
FOUR = [HB, AN, HB, AN]
SIX = [HB, AN, HB, HB, AN, AN]


def call(kernel, specs, outs, args, scratch=(), flops=0, limit=None):
    moved = sum(a.size * a.dtype.itemsize for a in args)
    moved += sum(math.prod(s) * jnp.dtype(t).itemsize for s, t, _ in outs)
    return pl.pallas_call(
        kernel,
        out_shape=[pltpu.HBM(s, t) if m is HB else jax.ShapeDtypeStruct(s, t) for s, t, m in outs],
        in_specs=specs,
        out_specs=[m for _, _, m in outs],
        scratch_shapes=list(scratch),
        compiler_params=pltpu.CompilerParams(vmem_limit_bytes=limit),
        cost_estimate=pl.CostEstimate(flops=flops, bytes_accessed=moved, transcendentals=0),
    )(*[
        pltpu.with_memory_space_constraint(a, pltpu.HBM) if m is HB else a
        for a, m in zip(args, specs, strict=True)
    ])


def weight_grad(place, lefts, rights, ones=False, tile=256, mixed=False):
    rows, width = lefts[0].shape
    cols = rights[0].shape[1]
    high = width + (16 if ones else 0)
    size = 2 * (8 * rows * width + 4 * rows * cols + high * cols)
    (out,) = call(
        functools.partial(weight_grad_kernel, ones, tile, mixed),
        [SM] + FOUR + FOUR,
        [((high, cols), HALF, HB)],
        [place, *lefts, *rights],
        [
            pltpu.VMEM((4, rows, width), HALF),
            pltpu.VMEM((width, 4 * rows), HALF),
            pltpu.VMEM((4 * rows, cols), HALF),
            pltpu.VMEM((high, cols), HALF),
            pltpu.SemaphoreType.DMA((6, max(4, -(-cols // tile)))),
        ],
        flops=8 * rows * width * cols,
        limit=size + 4 * MIB,
    )
    return out


def rotation_tables(length):
    half = ROT // 2
    lane = jnp.arange(LANES) % HD
    freqs = THETA ** (-2.0 * (lane % half).astype(FULL) / ROT)
    angles = jnp.arange(length, dtype=FULL)[:, None] * freqs[None, :]
    cos_t = jnp.where(lane < ROT, jnp.cos(angles), 1.0)
    sin_t = jnp.sin(angles)
    down = jnp.where(lane < half, -sin_t, 0.0)
    up = jnp.where((lane >= half) & (lane < ROT), sin_t, 0.0)
    return jnp.stack([cos_t, down, up])


def bias_mask(width):
    lanes = jnp.arange(width) % HD < ROT
    ones = jnp.ones((width,), FULL)
    return jnp.stack([ones, jnp.where(lanes, 1.0, 0.0).astype(FULL), ones])


def block(
    block_in,
    norm1_gain,
    norm1_bias,
    w_qkv,
    qkv_bias,
    w_proj,
    norm2_gain,
    norm2_bias,
    w_gateup,
    w_down,
    out_grad,
):
    rows = lax.axis_size(ROW)
    cols = lax.axis_size(COL)
    col = lax.axis_index(COL)
    row = lax.axis_index(ROW)
    odd = lax.axis_index(DP) % 2
    two = lax.axis_size(DP) == 2
    feats = w_qkv.shape[0]
    head_cols = w_qkv.shape[2]
    width = w_gateup.shape[2]
    tokens = block_in.shape[0]
    chunk = tokens // cols
    wide = rows * feats
    place = jnp.stack([odd, row, col, odd]).astype(jnp.int32)
    tables = rotation_tables(SEQ)

    def narrow(value):
        return [value[:, k * feats : (k + 1) * feats] for k in range(rows)]

    own_qkv = w_qkv.reshape(feats, 3 * head_cols)
    own_inner = w_gateup.reshape(feats, 2 * width)
    in_group = col_swaps([block_in] * 4)
    qkv_half = half_of(own_qkv)
    middle = 3 * head_cols // 2
    qkv_w = [own_qkv, swap(own_qkv, ROW, 1)]
    qkv_w += across(qkv_half[:, :middle]) + across(qkv_half[:, middle:])
    proj_w = row_gather(w_proj)
    beside = swap(own_inner, ROW, 1)
    inner_w = [own_inner, beside]
    gate_half, up_half, down_half = call(
        halves_kernel,
        [SM, HB, HB],
        [((feats // 2, width), HALF, HB)] * 2 + [((width, feats // 2), HALF, HB)],
        [place, own_inner, w_down],
        [
            pltpu.VMEM((2, feats // 2, width), HALF),
            pltpu.VMEM((width, feats // 2), HALF),
            pltpu.SemaphoreType.DMA((6,)),
        ],
        limit=4 * MIB,
    )
    down_w = [w_down, swap(w_down, ROW, 1), *across(down_half)]
    inner_w += across(gate_half) + across(up_half)
    scales = jnp.concatenate(
        [jnp.stack([norm1_gain, norm1_bias, norm2_gain, norm2_bias]), jnp.zeros((4, feats), FULL)], 0
    )
    high = lax.reduce_precision(scales, 8, 7)
    packed = jnp.concatenate([high.astype(HALF), (scales - high).astype(HALF)], 0)

    def sort(blocks, below):
        high = tokens + sum(b.shape[0] for b in below)
        *outs, every = call(
            sort_kernel,
            [SM] + [AN] * (4 + len(below)),
            [((high, feats), HALF, HB)] * 3 + [((rows, high, feats), HALF, HB)],
            [place, *blocks, *below],
            [pltpu.VMEM((rows, high, feats), HALF), pltpu.SemaphoreType.DMA((12,))],
            limit=4 * MIB,
        )
        return outs, every

    outs, x_own = sort(in_group, [packed])
    x = [x_own] + row_exchange([x_own] + outs)[1:]
    outs, grad_group = sort(col_swaps([out_grad] * 4), [])
    grad_seq = [grad_group] + row_exchange([grad_group] + outs)[1:]

    normed1, qkv, attn, lse, keep, *parts = call(
        attention_kernel,
        [SM] + [HB] * 13 + [AN] + [HB] * 4 + [VM] * 2,
        [
            ((tokens, wide), HALF, HB),
            ((tokens, 3 * head_cols), HALF, HB),
            ((tokens, head_cols), HALF, HB),
            ((tokens, LANES), FULL, HB),
            ((chunk + 8, wide), FULL, HB),
            *[((chunk, wide), HALF, HB)] * 4,
        ],
        [place, *x, *qkv_w, *proj_w, qkv_bias.reshape(1, 3 * head_cols), tables],
        [
            pltpu.VMEM((tokens, wide), HALF),
            pltpu.VMEM((tokens, 3 * head_cols), FULL),
            pltpu.VMEM((4, tokens + 16, feats), HALF),
            pltpu.VMEM((wide, middle), HALF),
            pltpu.VMEM((wide, middle), HALF),
            pltpu.VMEM((head_cols, wide), HALF),
            pltpu.VMEM((tokens, 3 * head_cols), HALF),
            pltpu.VMEM((tokens, head_cols), HALF),
            pltpu.VMEM((tokens, LANES), FULL),
            pltpu.VMEM((tokens, wide), HALF),
            pltpu.VMEM((chunk + 8, wide), FULL),
            pltpu.SemaphoreType.DMA((47,)),
        ],
        flops=2 * tokens * wide * 4 * head_cols,
        limit=20 * MIB,
    )
    normed2, resid = call(
        second_norm_kernel,
        [HB] + [VM] * 3 + [HB],
        [((chunk, wide), HALF, HB), ((chunk, wide), FULL, HB)],
        [*col_swaps(parts), keep],
        [
            pltpu.VMEM((chunk, wide), HALF),
            pltpu.VMEM((chunk + 8, wide), FULL),
            pltpu.VMEM((chunk, wide), FULL),
            pltpu.VMEM((chunk, wide), HALF),
            pltpu.SemaphoreType.DMA((4,)),
        ],
        limit=8 * MIB,
    )
    normed2 = col_swaps([normed2] * 4)
    d_hidden, own_grad = call(
        down_kernel,
        [SM] + FOUR + SIX,
        [((tokens, width), FULL, HB), ((chunk, wide), HALF, HB)],
        [place, *grad_seq, *down_w],
        [
            pltpu.VMEM((tokens, width), FULL),
            pltpu.VMEM((tokens, wide), HALF),
            pltpu.VMEM((width, wide), HALF),
            pltpu.VMEM((chunk, wide), HALF),
            pltpu.SemaphoreType.DMA((12,)),
        ],
        flops=2 * tokens * wide * width,
        limit=12 * MIB,
    )
    cut = 6 * LANES
    hidden, d_first, d_rest, d_up, own_normed2, *parts = call(
        mlp_kernel,
        [SM, HB] + [AN] * 3 + [HB] + SIX + SIX[2:],
        [
            ((tokens, width), HALF, HB),
            ((tokens, cut), HALF, HB),
            ((tokens, width - cut), HALF, HB),
            ((tokens, width), HALF, HB),
            ((tokens, feats), HALF, HB),
            *[((chunk, wide), HALF, HB)] * 4,
        ],
        [place, *normed2, d_hidden, *inner_w],
        [
            pltpu.VMEM((tokens, wide), HALF),
            pltpu.VMEM((tokens, width), FULL),
            pltpu.VMEM((tokens, width), FULL),
            pltpu.VMEM((wide, width), HALF),
            pltpu.VMEM((wide, width), HALF),
            pltpu.VMEM((tokens, width), HALF),
            pltpu.VMEM((tokens, width), HALF),
            pltpu.VMEM((tokens, width), HALF),
            pltpu.VMEM((tokens, width), FULL),
            pltpu.VMEM((tokens, wide), HALF),
            pltpu.SemaphoreType.DMA((60,)),
        ],
        flops=2 * tokens * wide * 4 * width,
        limit=28 * MIB,
    )
    rounded, d_resid = call(
        second_back_kernel,
        [HB] + [VM] * 3 + [HB] * 3,
        [((chunk, wide), HALF, HB), ((chunk + 8, wide), FULL, HB)],
        [*col_swaps(parts), resid, own_grad, keep],
        [
            pltpu.VMEM((chunk, wide), HALF),
            pltpu.VMEM((chunk, wide), FULL),
            pltpu.VMEM((chunk, wide), HALF),
            pltpu.VMEM((chunk + 8, wide), FULL),
            pltpu.VMEM((chunk + 8, wide), FULL),
            pltpu.VMEM((chunk, wide), HALF),
            pltpu.SemaphoreType.DMA((6,)),
        ],
        limit=8 * MIB,
    )
    rounded = col_swaps([rounded] * 4)
    d_qkv, *parts = call(
        attention_back_kernel,
        [SM, HB] + [AN] * 3 + [HB] * 18,
        [((tokens, 3 * head_cols), HALF, HB), *[((chunk, wide), HALF, HB)] * 4],
        [place, *rounded, qkv, attn, lse, tables, *qkv_w, *proj_w],
        [
            pltpu.VMEM((tokens, wide), HALF),
            pltpu.VMEM((tokens, head_cols), HALF),
            pltpu.VMEM((tokens, 3 * head_cols), HALF),
            pltpu.VMEM((wide, middle), HALF),
            pltpu.VMEM((wide, middle), HALF),
            pltpu.VMEM((head_cols, wide), HALF),
            pltpu.VMEM((tokens, 3 * head_cols), HALF),
            pltpu.VMEM((tokens, head_cols), HALF),
            pltpu.VMEM((tokens, LANES), FULL),
            pltpu.VMEM((3, tokens, LANES), FULL),
            pltpu.VMEM((tokens, wide), HALF),
            pltpu.SemaphoreType.DMA((63,)),
        ],
        flops=2 * tokens * wide * 5 * head_cols,
        limit=18 * MIB,
    )
    (last,) = call(
        first_back_kernel,
        [HB] + [VM] * 3 + [HB] * 2,
        [((chunk + 16, wide), HALF, VM)],
        [*col_swaps(parts), d_resid, keep],
        [
            pltpu.VMEM((chunk, wide), HALF),
            pltpu.VMEM((chunk + 8, wide), FULL),
            pltpu.VMEM((chunk + 8, wide), FULL),
            pltpu.SemaphoreType.DMA((3,)),
        ],
        limit=8 * MIB,
    )

    got = row_exchange(narrow(last))
    (packed,) = call(
        pack_kernel,
        [SM] + [VM] * 4,
        [((rows, chunk + 16, feats), HALF, VM)],
        [place, *got],
        limit=4 * MIB,
    )
    got = col_exchange(packed)
    attn_group = row_gather(attn)
    normed_group = row_exchange(narrow(normed1))

    def blocks_of(pieces):
        return [jnp.concatenate(b, 0) for b in zip(*[narrow(p) for p in pieces])]

    normed2_group = [own_normed2] + row_exchange(blocks_of(normed2))[1:]
    hidden_group = row_gather(hidden)
    first_group = row_gather(d_first)
    rest_group = row_gather(d_rest)
    up_group = row_gather(d_up)
    first_mine = weight_grad(place, normed2_group, first_group)
    rest_mine = weight_grad(place, normed2_group, rest_group)
    up_mine = weight_grad(place, normed2_group, up_group)
    if two:
        other_group = row_gather(swap(hidden, DP, 1))
        (grad_down,) = call(
            down_grad_kernel,
            [SM] + FOUR + FOUR + [HB] * 2,
            [((width, feats), FULL, HB)],
            [place, *hidden_group, *other_group, grad_group, swap(grad_group, DP, 1)],
            [
                pltpu.VMEM((8, tokens, width), HALF),
                pltpu.VMEM((width, 8 * tokens), HALF),
                pltpu.VMEM((8 * tokens, feats), HALF),
                pltpu.VMEM((width, feats), FULL),
                pltpu.SemaphoreType.DMA((20,)),
            ],
            flops=16 * tokens * width * feats,
            limit=22 * MIB,
        )
        pairs = [
            (first_mine, swap(first_mine, DP, 1)),
            (rest_mine, swap(rest_mine, DP, 1)),
            (up_mine, swap(up_mine, DP, 1)),
        ]
        grad_gateup = total(pairs, (feats, 2, width))
    else:
        grads = [grad_group[k] for k in range(rows)]
        grad_down = over_groups(weight_grad(place, hidden_group, grads))
        mine = jnp.concatenate([first_mine, rest_mine, up_mine], 1)
        grad_gateup = over_groups(mine).reshape(feats, 2, width)
    leaf = call(
        leaf_kernel,
        [SM] + FOUR + FOUR + [HB] * 2,
        [((tokens, feats), HALF, HB)] * 4,
        [place, *attn_group, *hidden_group, w_proj, w_down],
        [
            pltpu.VMEM((head_cols, feats), HALF),
            pltpu.VMEM((width, feats), HALF),
            pltpu.VMEM((4, tokens, head_cols), HALF),
            pltpu.VMEM((4, tokens, width), HALF),
            pltpu.VMEM((4, tokens, feats), HALF),
            pltpu.SemaphoreType.DMA((14,)),
        ],
        flops=2 * rows * tokens * feats * (head_cols + width),
        limit=12 * MIB,
    )
    leaf = [leaf[0], swap(leaf[1], COL, 1), swap(leaf[2], COL, 2), swap(leaf[3], COL, 3)]
    grad_in, block_out, vectors = call(
        unpack_kernel,
        [AN, HB, HB, AN, AN, AN],
        [((tokens, feats), FULL, HB), ((tokens, feats), FULL, HB), ((8, feats), FULL, HB)],
        [got, block_in, *leaf],
        [
            pltpu.VMEM((rows, chunk + 16, feats), HALF),
            pltpu.VMEM((tokens, feats), HALF),
            pltpu.VMEM((4, tokens, feats), HALF),
            pltpu.VMEM((tokens, feats), FULL),
            pltpu.VMEM((tokens, feats), FULL),
            pltpu.VMEM((8, feats), FULL),
            pltpu.SemaphoreType.DMA((9,)),
        ],
        limit=8 * MIB,
    )
    if two:
        vectors = vectors + swap(vectors, DP, 1)
    else:
        vectors = lax.psum(vectors, DP)

    rounded_group = row_exchange(blocks_of(rounded))
    proj_mine = weight_grad(place, attn_group, rounded_group, mixed=True)
    if two:
        proj_other = swap(proj_mine, DP, 1)
        grad_proj = total([(proj_mine, proj_other)], (1, head_cols, feats), 0)[0]
    else:
        grad_proj = over_groups(proj_mine)
    qkv_group = row_gather(d_qkv)
    mine = weight_grad(place, normed_group, qkv_group, True)
    if two:
        other = swap(mine, DP, 1)
        grad_qkv = total([(mine, other)], (3, feats, head_cols), 0).swapaxes(0, 1)
        both = mine[feats:].astype(FULL) + other[feats:].astype(FULL)
    else:
        both = lax.psum(mine.astype(FULL), DP)
        grad_qkv = both[:feats].reshape(feats, 3, head_cols)
        both = both[feats:]
    grad_bias = (both[0] + both[8]).reshape(3, head_cols) * bias_mask(head_cols)
    gain1_grad, bias1_grad, gain2_grad, bias2_grad = vectors[:4]
    return (
        block_out,
        grad_in,
        grad_qkv,
        grad_bias,
        grad_proj,
        gain1_grad,
        bias1_grad,
        gain2_grad,
        bias2_grad,
        grad_gateup,
        grad_down,
    )


def solution(mesh):
    return jax.shard_map(
        block,
        mesh=mesh,
        in_specs=(
            P((DP, COL), ROW),
            P(ROW),
            P(ROW),
            P(ROW, None, COL),
            P(None, COL),
            P(COL, ROW),
            P(ROW),
            P(ROW),
            P(ROW, None, COL),
            P(COL, ROW),
            P((DP, COL), ROW),
        ),
        out_specs=(
            P((DP, COL), ROW),
            P((DP, COL), ROW),
            P(ROW, None, COL),
            P(None, COL),
            P(COL, ROW),
            P(ROW),
            P(ROW),
            P(ROW),
            P(ROW),
            P(ROW, None, COL),
            P(COL, ROW),
        ),
        check_vma=False,
    )
```
